32 devices in a mesh: dp: 8 (over z, y), seq: 4 (over x, core).
Axes of the slice: x: 2, y: 2, z: 4, core: 2. Of those that a mesh axis runs over, the one named last changes fastest.
Arguments:
- hidden_in: float32 [8, 2048, 768], P('dp', 'seq'), may hold values from -6 to 6
- teacher: float32 [8, 2048, 768], P('dp', 'seq'), may hold values from -6 to 6
- lengths: int32 [8, 8], P('dp'), may hold values from 32 to 128, as said below
- qkv_weight: float32 [3, 768, 768], P(None, 'dp'), may hold values from -0.21875 to 0.21875
- qkv_bias: float32 [2, 768], P(None, 'dp'), may hold values from -0.75 to 0.75
- out_weight: float32 [768, 768], P('dp'), may hold values from -1.75 to 1.75
- out_bias: float32 [2, 768], P(None, 'dp'), may hold values from -6 to 6
- ln_gain: float32 [2, 768], P(None, 'dp'), may hold values from 0.25 to 1.75
- ln_shift: float32 [2, 768], P(None, 'dp'), may hold values from -6 to 6
- ffn_in: float32 [768, 3072], P('dp'), may hold values from -0.21875 to 0.21875
- ffn_in_bias: float32 [3072], P('dp'), may hold values from -6 to 6
- ffn_out: float32 [3072, 768], P('dp'), may hold values from -0.109375 to 0.109375
Outputs:
- hidden_out: float32 [8, 2048, 768], P('dp', 'seq')
- grad_in: float32 [8, 2048, 768], P('dp', 'seq')
- grad_qkv_weight: float32 [3, 768, 768], P(None, 'dp')
- grad_qkv_bias: float32 [2, 768], P(None, 'dp')
- grad_out_weight: float32 [768, 768], P('dp')
- grad_out_bias: float32 [2, 768], P(None, 'dp')
- grad_ln_gain: float32 [2, 768], P(None, 'dp')
- grad_ln_shift: float32 [2, 768], P(None, 'dp')
- grad_ffn_in: float32 [768, 3072], P('dp')
- grad_ffn_in_bias: float32 [3072], P('dp')
- grad_ffn_out: float32 [3072, 768], P('dp')
- loss: float32 [], replicated
The draws below stay inside these ranges and needn't reach their ends.
Inputs may be any that keep to these rules, and one draw needn't show every extreme that they name: `lengths`: in every group one continuation has all 128 tokens valid and another has 32.
All inputs are finite; a program needn't handle non-finite values.
Results may differ from the reference program's by a relative error of at most 0.0003.
Values sent between devices are 32-bit elements; how exact they have to be, the bound alone decides.
A program may use at most 256 MiB of HBM per device.

```python
import jax
import jax.numpy as jnp
from jax import lax

D = 768
H = 12
HD = 64
FF = 3072
PROMPT = 1024
CONT = 8
CLEN = 128
GTOK = 2048
GROUPS = 8
TOKENS = 16384


def draw_lengths(key, part):
    first_key = jax.random.fold_in(key, 11)
    second_key = jax.random.fold_in(key, 23)
    third_key = jax.random.fold_in(key, 37)
    values = jax.random.randint(first_key, (GROUPS, CONT), CLEN // 4, CLEN + 1, dtype=jnp.int32)
    full_pick = jax.random.randint(second_key, (GROUPS,), 0, CONT, dtype=jnp.int32)
    short_step = jax.random.randint(third_key, (GROUPS,), 1, CONT, dtype=jnp.int32)
    short_pick = (full_pick + short_step) % CONT
    columns = jnp.arange(CONT, dtype=jnp.int32)[None, :]
    values = jnp.where(columns == full_pick[:, None], CLEN, values)
    values = jnp.where(columns == short_pick[:, None], CLEN // 4, values)
    return values.astype(jnp.int32)


def levels(own_key, extent, cuts, low, largest):
    level, own = 1.0, jax.random.fold_in(own_key, 6)
    for position, blocks in cuts:
        draws = jnp.exp(jax.random.uniform(jax.random.fold_in(own, position), (blocks,), jnp.float32, low / len(cuts), largest / len(cuts)))
        level = level * jnp.repeat(draws, extent[position] // blocks).reshape([-1 if axis == position else 1 for axis in range(len(extent))])
    return level


def normal_values(key, dims, spread, reach, cuts=(), held_as=jnp.bfloat16):
    loudness = levels(key, dims, cuts, -0.22, 0.18) if cuts else 1.0
    result = jax.random.normal(key, dims, jnp.float32) * spread * loudness
    return jnp.minimum(jnp.maximum(result, -reach), reach).astype(held_as)


def setup_inputs(seed: int = 0) -> dict:
    key_of = jax.random.split(jax.random.key(seed), 13)
    return {
        "hidden_in": normal_values(key_of[0], (GROUPS, GTOK, D), 1.0, 6.0, ((0, 8), (1, 4)), jnp.float32),
        "teacher": normal_values(key_of[1], (GROUPS, GTOK, D), 1.0, 6.0, ((0, 8), (1, 4)), jnp.float32),
        "lengths": draw_lengths(jax.random.fold_in(key_of[12], 71), 0),
        "qkv_weight": normal_values(key_of[3], (3, D, D), D ** -0.5, 0.21875, ((1, 8),), jnp.float32),
        "qkv_bias": normal_values(key_of[4], (2, D), 0.05, 0.75, ((1, 8),), jnp.float32),
        "out_weight": normal_values(key_of[5], (D, D), (D // 64) ** -0.5, 1.75, ((0, 8),), jnp.float32),
        "out_bias": normal_values(key_of[6], (2, D), 0.5, 6.0, ((1, 8),), jnp.float32),
        "ln_gain": jnp.clip(1.0 + 0.15 * jax.random.normal(key_of[7], (2, D), jnp.float32), 0.25, 1.75),
        "ln_shift": normal_values(key_of[8], (2, D), 0.5, 6.0, ((1, 8),), jnp.float32),
        "ffn_in": normal_values(key_of[9], (D, FF), D ** -0.5, 0.21875, ((0, 8),), jnp.float32),
        "ffn_in_bias": normal_values(key_of[10], (FF,), 0.5, 6.0, ((0, 8),), jnp.float32),
        "ffn_out": normal_values(key_of[11], (FF, D), FF ** -0.5, 0.109375, ((0, 8),), jnp.float32),
    }


@jax.custom_vjp
def low(v):
    return lax.optimization_barrier(v.astype(jnp.bfloat16)).astype(jnp.float32)

@jax.custom_vjp
def low_back(v):
    return v

def low_keep(v):
    return (low(v), None)

def low_pass(kept, grad):
    return (grad,)

def back_keep(v):
    return (v, None)

def back_low(kept, grad):
    return (low(grad),)
low.defvjp(low_keep, low_pass)
low_back.defvjp(back_keep, back_low)
HIGHEST = lax.Precision.HIGHEST
EPSILON = 1e-05
MASKED = -1e+30

def product(left, right):
    return jnp.dot(left, right, precision=HIGHEST, preferred_element_type=jnp.float32)

def layer_norm(resid, gain, shift):
    center = resid - lax.optimization_barrier(jnp.mean(resid, axis=-1, keepdims=True))
    variance = lax.optimization_barrier(jnp.mean(center * center, axis=-1, keepdims=True))
    return center * lax.rsqrt(variance + EPSILON) * gain + shift

def attention(queries, keys, values, seq_lengths):
    scale = HD ** (-0.5)
    q_prompt = queries[:PROMPT]
    k_prompt = keys[:PROMPT]
    v_prompt = values[:PROMPT]
    prompt_scores = jnp.einsum('qhd,khd->hqk', q_prompt, k_prompt, precision=HIGHEST) * scale
    prompt_probs = jax.nn.softmax(prompt_scores, axis=-1)
    prompt_out = jnp.einsum('hqk,khd->qhd', prompt_probs, v_prompt, precision=HIGHEST)
    q_cont = queries[PROMPT:].reshape(CONT, CLEN, H, HD)
    k_cont = keys[PROMPT:].reshape(CONT, CLEN, H, HD)
    v_cont = values[PROMPT:].reshape(CONT, CLEN, H, HD)
    query_pos = jnp.arange(CLEN, dtype=jnp.int32)[:, None]
    key_pos = jnp.arange(CLEN, dtype=jnp.int32)[None, :]
    allowed = (key_pos <= query_pos)[None] & (key_pos[None] < seq_lengths[:, None, None])
    to_prompt = jnp.einsum('cqhd,khd->chqk', q_cont, k_prompt, precision=HIGHEST) * scale
    to_self = jnp.einsum('cqhd,ckhd->chqk', q_cont, k_cont, precision=HIGHEST) * scale
    to_self = jnp.where(allowed[:, None], to_self, MASKED)
    probs = jax.nn.softmax(jnp.concatenate([to_prompt, to_self], axis=-1), axis=-1)
    cont_out = jnp.einsum('chqk,khd->cqhd', probs[..., :PROMPT], v_prompt, precision=HIGHEST)
    cont_out = cont_out + jnp.einsum('chqk,ckhd->cqhd', probs[..., PROMPT:], v_cont, precision=HIGHEST)
    return jnp.concatenate([prompt_out.reshape(PROMPT, H * HD), cont_out.reshape(CONT * CLEN, H * HD)], axis=0)

def group_forward(params, inputs, target, seq_lengths):
    qkv_weight, qkv_bias, out_weight, out_bias, ln_gain, ln_shift, ffn_in, ffn_in_bias, ffn_out = params
    queries = (product(inputs, qkv_weight[0]) + qkv_bias[0]).reshape(GTOK, H, HD)
    keys = product(inputs, qkv_weight[1]).reshape(GTOK, H, HD)
    values = (product(inputs, qkv_weight[2]) + qkv_bias[1]).reshape(GTOK, H, HD)
    attended = attention(queries, keys, values, seq_lengths)
    first_norm = layer_norm(inputs + product(attended, out_weight) + out_bias[0], ln_gain[0], ln_shift[0])
    activated = jax.nn.gelu(product(first_norm, ffn_in) + ffn_in_bias, approximate=False)
    final = layer_norm(first_norm + product(activated, ffn_out) + out_bias[1], ln_gain[1], ln_shift[1])
    positions = jnp.arange(GTOK, dtype=jnp.int32)
    offsets = positions - PROMPT
    which = jnp.clip(offsets // CLEN, 0, CONT - 1)
    valid = ((positions < PROMPT) | (offsets % CLEN < seq_lengths[which])).astype(jnp.float32)
    error = (final - target) * valid[:, None]
    return (final, jnp.sum(error * error))

def reference(hidden_in, teacher, lengths, qkv_weight, qkv_bias, out_weight, out_bias, ln_gain, ln_shift, ffn_in, ffn_in_bias, ffn_out):
    params = (qkv_weight, qkv_bias, out_weight, out_bias, ln_gain, ln_shift, ffn_in, ffn_in_bias, ffn_out)

    def whole(inputs, weights):

        def one_group(running, items):
            block, target, seq_lengths = items
            final, squares = jax.checkpoint(group_forward)(weights, block, target, seq_lengths)
            return (running + squares, final)
        running, finals = lax.scan(one_group, jnp.zeros((), jnp.float32), (inputs, teacher, lengths))
        return (finals, running)
    (hidden_out, squares), pullback = jax.vjp(whole, hidden_in, params)
    count = (GROUPS * PROMPT + jnp.sum(lengths)).astype(jnp.float32)
    sum_weight = jnp.float32(TOKENS) / (2.0 * count)
    grad_in, weight_grads = pullback((jnp.zeros_like(hidden_out), sum_weight))
    loss = squares / (count * D)
    return (hidden_out, grad_in, weight_grads[0], weight_grads[1], weight_grads[2], weight_grads[3], weight_grads[4], weight_grads[5], weight_grads[6], weight_grads[7], weight_grads[8], loss)
```

```python
import functools

import jax
import jax.numpy as jnp
from jax import lax
from jax.experimental import pallas as pl
from jax.experimental.pallas import tpu as pltpu
from jax.sharding import PartitionSpec as P

HD = 64
PROMPT = 1024
CONT = 8
CLEN = 128
SEQ = 4
QB = 256

HIGH = lax.Precision.HIGH
EPSILON = 1e-05
MASKED = -1e30
INV_ROOT_TWO = 0.7071067811865476
INV_ROOT_TAU = 0.3989422804014327
BF = jnp.bfloat16
F32 = jnp.float32


def mm(left, right):
    return lax.dot_general(
        left, right, (((1,), (0,)), ((), ())), precision=HIGH, preferred_element_type=F32
    )


def mm_nt(left, right):
    return lax.dot_general(
        left, right, (((1,), (1,)), ((), ())), precision=HIGH, preferred_element_type=F32
    )


def mm_tn(left, right):
    return lax.dot_general(
        left, right, (((0,), (0,)), ((), ())), precision=HIGH, preferred_element_type=F32
    )


def swap_pair(value):
    return lax.ppermute(value, "seq", [(i, i ^ 1) for i in range(SEQ)])


def swap_group(value):
    return lax.ppermute(value, "seq", [(i, i ^ 2) for i in range(SEQ)])


def swap_dp(value, bit):
    count = lax.axis_size("dp")
    return lax.ppermute(value, "dp", [(i, i ^ (1 << bit)) for i in range(count)])


def ordered(bit, own, other, axis):
    first = jnp.where(bit == 0, own, other)
    second = jnp.where(bit == 0, other, own)
    return jnp.concatenate([first, second], axis=axis)


def pick(value, index, axis):
    return lax.dynamic_index_in_dim(value, index, axis, keepdims=False)


def dp_bits():
    return lax.axis_size("dp").bit_length() - 1


def gather_small(value):
    index = lax.axis_index("dp")
    for bit in range(dp_bits()):
        value = ordered((index >> bit) & 1, value, swap_dp(value, bit), 0)
    return value


def gather_blocks(piece, group):
    index = lax.axis_index("dp")
    own = pick(piece, group, 0)[None]
    for bit in range(1, dp_bits()):
        own = ordered((index >> bit) & 1, own, swap_dp(own, bit), 0)
    ybit = index & 1
    first, second = own[:, 0], own[:, 1]
    count, rows, cols = first.shape
    first_x = swap_group(first)
    second_y = swap_dp(second, 0)
    parts = [
        (first, 0, 0, 0),
        (first_x, 1, 0, 0),
        (swap_dp(first, 0), 0, 1, 0),
        (swap_dp(first_x, 0), 1, 1, 0),
        (second, 0, 0, 1),
        (second_y, 0, 1, 1),
        (swap_group(second), 1, 0, 1),
        (swap_group(second_y), 1, 1, 1),
    ]
    whole = jnp.zeros((count, 2, 2, 2, rows, cols), F32)
    for part, off_x, off_y, route in parts:
        whole = lax.dynamic_update_slice(
            whole, part[:, None, None, None], (0, ybit ^ off_y, group ^ off_x, route, 0, 0)
        )
    return whole.reshape(count * 2, 2, 2, rows, cols)


def scatter_blocks(grads, group):
    index = lax.axis_index("dp")
    ybit = index & 1
    count, _, _, rows, cols = grads.shape
    grads = grads.reshape(count // 2, 2, 2, 2, rows, cols)
    first, second = grads[:, :, :, 0], grads[:, :, :, 1]
    first = pick(first, ybit, 1) + swap_dp(pick(first, ybit ^ 1, 1), 0)
    second = pick(second, group, 2) + swap_group(pick(second, group ^ 1, 2))
    first = pick(first, group, 1) + swap_group(pick(first, group ^ 1, 1))
    second = pick(second, ybit, 1) + swap_dp(pick(second, ybit ^ 1, 1), 0)
    both = jnp.stack([first, second], axis=1)
    for bit in reversed(range(1, dp_bits())):
        both = both.reshape(2, -1, 2, rows, cols)
        mine = (index >> bit) & 1
        both = pick(both, mine, 0) + swap_dp(pick(both, mine ^ 1, 0), bit)
    own = both.reshape(1, 2, rows, cols)
    return ordered(group, own, swap_group(own), 0)


def scatter_small(value):
    index = lax.axis_index("dp")
    for bit in reversed(range(dp_bits())):
        halves = value.reshape(2, -1, value.shape[-1])
        mine = (index >> bit) & 1
        value = pick(halves, mine, 0) + swap_dp(pick(halves, mine ^ 1, 0), bit)
    value = value[0]
    value = value + swap_pair(value)
    return value + swap_group(value)


def sum_all(value):
    for bit in range(dp_bits()):
        value = value + swap_dp(value, bit)
    value = value + swap_pair(value)
    return value + swap_group(value)


def lane_ids(shape):
    return lax.broadcasted_iota(jnp.int32, shape, 1)


def high_low(value):
    high = value.astype(BF).astype(F32)
    return high, value - high


def packs(value, head):
    high, low = high_low(value)
    left = lane_ids(value.shape) < HD
    high_r = pltpu.roll(high, HD, 1)
    low_r = pltpu.roll(low, HD, 1)
    if head == 0:
        return (
            jnp.where(left, high, low_r).astype(BF),
            jnp.where(left, high, high_r).astype(BF),
            jnp.where(left, low, low_r).astype(BF),
        )
    return (
        jnp.where(left, high_r, low).astype(BF),
        jnp.where(left, high_r, high).astype(BF),
        jnp.where(left, low_r, low).astype(BF),
    )


def dot(left, right):
    return lax.dot_general(left, right, (((1,), (0,)), ((), ())), preferred_element_type=F32)


def dot_nt(left, right):
    return lax.dot_general(left, right, (((1,), (1,)), ((), ())), preferred_element_type=F32)


def split(value):
    high = value.astype(BF)
    return high, (value - high.astype(F32)).astype(BF)


def self_mask(lens_ref, block, query_axis):
    key_axis = 1 - query_axis
    query = lax.broadcasted_iota(jnp.int32, (QB, QB), query_axis)
    key = lax.broadcasted_iota(jnp.int32, (QB, QB), key_axis)
    per = QB // CLEN
    seen = jnp.zeros((QB, QB), jnp.bool_)
    for piece in range(per):
        low = piece * CLEN
        limit = low + lens_ref[block * per + piece]
        inside = (query >= low) & (query < low + CLEN) & (key >= low) & (key < limit)
        seen = seen | inside
    return seen & (key <= query)


def forward_kernel(lens_ref, q_ref, kp_ref, vp_ref, ks_ref, vs_ref, o_ref, lse_ref,
                   q4, k4p, k4s, v2p, v2s):
    rows = q_ref.shape[0]
    for head in range(2):
        _, hh, ll = packs(q_ref[...] * 0.125, head)
        q4[head, :, :128] = hh
        q4[head, :, 128:] = ll
        for src, dst in ((kp_ref, k4p), (ks_ref, k4s)):
            hl, _, _ = packs(src[...], head)
            dst[head, :, :128] = hl
            dst[head, :, 128:] = hl
        v2p[head] = packs(vp_ref[...], head)[0]
        v2s[head] = packs(vs_ref[...], head)[0]

    def step(block, carry):
        here = pl.ds(pl.multiple_of(block * QB, QB), QB)
        seen = self_mask(lens_ref, block, 0)
        results = []
        for head in range(2):
            query = q4[head, here, :]
            far = dot_nt(query, k4p[head])
            near = jnp.where(seen, dot_nt(query, k4s[head, here, :]), MASKED)
            top = jnp.maximum(
                jnp.max(far, axis=1, keepdims=True), jnp.max(near, axis=1, keepdims=True)
            )
            far = jnp.exp(far - top)
            near = jnp.exp(near - top)
            total = jnp.sum(far, axis=1, keepdims=True) + jnp.sum(near, axis=1, keepdims=True)
            far_h, far_l = split(far)
            near_h, near_l = split(near)
            out = dot(far_h, v2p[head]) + dot(far_l, v2p[head])
            value = v2s[head, here, :]
            out = out + dot(near_h, value) + dot(near_l, value)
            out = (out + pltpu.roll(out, HD, 1)) / total
            lse = top + jnp.log(total)
            lse_ref[head, :, here] = jnp.transpose(jnp.broadcast_to(lse, (QB, 128)))[:8]
            results.append(out)
        o_ref[here, :] = jnp.where(lane_ids((QB, 128)) < HD, results[0], results[1])
        return carry

    lax.fori_loop(0, rows // QB, step, 0)


def attend_forward(lens, q, kp, vp, ks, vs):
    rows, width = q.shape
    prompt = kp.shape[0]
    heads = width // HD
    spec = lambda n: pl.BlockSpec((n, 128), lambda j, lens: (0, j))
    flops = heads * 2 * rows * (prompt + QB) * (256 + 256)
    return pl.pallas_call(
        forward_kernel,
        grid_spec=pltpu.PrefetchScalarGridSpec(
            num_scalar_prefetch=1,
            grid=(heads // 2,),
            in_specs=[spec(rows), spec(prompt), spec(prompt), spec(rows), spec(rows)],
            out_specs=[spec(rows), pl.BlockSpec((2, 8, rows), lambda j, lens: (j, 0, 0))],
            scratch_shapes=[
                pltpu.VMEM((2, rows, 256), BF),
                pltpu.VMEM((2, prompt, 256), BF),
                pltpu.VMEM((2, rows, 256), BF),
                pltpu.VMEM((2, prompt, 128), BF),
                pltpu.VMEM((2, rows, 128), BF),
            ],
        ),
        out_shape=[
            jax.ShapeDtypeStruct((rows, width), F32),
            jax.ShapeDtypeStruct((heads, 8, rows), F32),
        ],
        compiler_params=pltpu.CompilerParams(vmem_limit_bytes=48 << 20),
        cost_estimate=pl.CostEstimate(
            flops=flops, bytes_accessed=6 * rows * width * 4, transcendentals=heads * rows * prompt
        ),
        name="attention_forward",
    )(lens, q, kp, vp, ks, vs)


def backward_kernel(lens_ref, q_ref, kp_ref, vp_ref, ks_ref, vs_ref, o_ref, g_ref, lse_ref,
                    dq_ref, dkp_ref, dvp_ref, dks_ref, dvs_ref,
                    q4, k4p, k4s, v4p, v4s, g4, q2, g2, k2tp, k2ts, delta):
    rows = q_ref.shape[0]
    prod = jnp.transpose(o_ref[...] * g_ref[...])
    for head in range(2):
        hl, hh, ll = packs(q_ref[...] * 0.125, head)
        q2[head] = hl
        q4[head, :, :128] = hh
        q4[head, :, 128:] = ll
        hl, hh, ll = packs(g_ref[...], head)
        g2[head] = hl
        g4[head, :, :128] = hh
        g4[head, :, 128:] = ll
        for src, dst in ((kp_ref, k4p), (ks_ref, k4s), (vp_ref, v4p), (vs_ref, v4s)):
            hl, _, _ = packs(src[...], head)
            dst[head, :, :128] = hl
            dst[head, :, 128:] = hl
        for src, dst in ((kp_ref, k2tp), (ks_ref, k2ts)):
            flipped = jnp.transpose(src[...])[head * HD : head * HD + HD]
            high, low = high_low(flipped)
            dst[head, :HD] = high.astype(BF)
            dst[head, HD:] = low.astype(BF)
        delta[head] = jnp.broadcast_to(
            jnp.sum(prod[head * HD : head * HD + HD], axis=0, keepdims=True), (8, rows)
        )
    dkp_ref[...] = jnp.zeros_like(dkp_ref)
    dvp_ref[...] = jnp.zeros_like(dvp_ref)

    def step(block, carry):
        here = pl.ds(pl.multiple_of(block * QB, QB), QB)
        seen = self_mask(lens_ref, block, 1)
        keep = {}
        for head in range(2):
            query = q4[head, here, :]
            grad = g4[head, here, :]
            lse = lse_ref[head, :1, here]
            low = delta[head, :1, here]
            far = jnp.exp(dot_nt(k4p[head], query) - lse)
            near = jnp.exp(jnp.where(seen, dot_nt(k4s[head, here, :], query), MASKED) - lse)
            far_g = far * (dot_nt(v4p[head], grad) - low)
            near_g = near * (dot_nt(v4s[head, here, :], grad) - low)
            grad2 = g2[head, here, :]
            query2 = q2[head, here, :]
            ph, p_l = split(far)
            dvp = dot(ph, grad2) + dot(p_l, grad2)
            ph, p_l = split(near)
            dvs = dot(ph, grad2) + dot(p_l, grad2)
            sh, sl = split(far_g)
            dkp = dot(sh, query2) + dot(sl, query2)
            dq = dot(k2tp[head], sh) + dot(k2tp[head], sl)
            sh, sl = split(near_g)
            dks = dot(sh, query2) + dot(sl, query2)
            side = k2ts[head, :, here]
            dq = dq + dot(side, sh) + dot(side, sl)
            dq = dq[:HD] + dq[HD:]
            keep[head] = (
                dq,
                dkp + pltpu.roll(dkp, HD, 1),
                dvp + pltpu.roll(dvp, HD, 1),
                dks + pltpu.roll(dks, HD, 1),
                dvs + pltpu.roll(dvs, HD, 1),
            )
        left = lane_ids((QB, 128)) < HD
        far_left = lane_ids(dkp_ref.shape) < HD
        dq_ref[here, :] = jnp.transpose(
            jnp.concatenate([keep[0][0], keep[1][0]], axis=0)
        ) * 0.125
        dkp_ref[...] += jnp.where(far_left, keep[0][1], keep[1][1])
        dvp_ref[...] += jnp.where(far_left, keep[0][2], keep[1][2])
        dks_ref[here, :] = jnp.where(left, keep[0][3], keep[1][3])
        dvs_ref[here, :] = jnp.where(left, keep[0][4], keep[1][4])
        return carry

    lax.fori_loop(0, rows // QB, step, 0)


def attend_backward(lens, q, kp, vp, ks, vs, out, grad, lse):
    rows, width = q.shape
    prompt = kp.shape[0]
    heads = width // HD
    spec = lambda n: pl.BlockSpec((n, 128), lambda j, lens: (0, j))
    flops = heads * 2 * rows * (prompt + QB) * (256 * 5)
    shape = lambda n: jax.ShapeDtypeStruct((n, width), F32)
    return pl.pallas_call(
        backward_kernel,
        grid_spec=pltpu.PrefetchScalarGridSpec(
            num_scalar_prefetch=1,
            grid=(heads // 2,),
            in_specs=[
                spec(rows), spec(prompt), spec(prompt), spec(rows), spec(rows),
                spec(rows), spec(rows), pl.BlockSpec((2, 8, rows), lambda j, lens: (j, 0, 0)),
            ],
            out_specs=[spec(rows), spec(prompt), spec(prompt), spec(rows), spec(rows)],
            scratch_shapes=[
                pltpu.VMEM((2, rows, 256), BF),
                pltpu.VMEM((2, prompt, 256), BF),
                pltpu.VMEM((2, rows, 256), BF),
                pltpu.VMEM((2, prompt, 256), BF),
                pltpu.VMEM((2, rows, 256), BF),
                pltpu.VMEM((2, rows, 256), BF),
                pltpu.VMEM((2, rows, 128), BF),
                pltpu.VMEM((2, rows, 128), BF),
                pltpu.VMEM((2, 128, prompt), BF),
                pltpu.VMEM((2, 128, rows), BF),
                pltpu.VMEM((2, 8, rows), F32),
            ],
        ),
        out_shape=[shape(rows), shape(prompt), shape(prompt), shape(rows), shape(rows)],
        compiler_params=pltpu.CompilerParams(vmem_limit_bytes=56 << 20),
        cost_estimate=pl.CostEstimate(
            flops=flops, bytes_accessed=12 * rows * width * 4, transcendentals=heads * rows * prompt
        ),
        name="attention_backward",
    )(lens, q, kp, vp, ks, vs, out, grad, lse)


def norm_forward(resid, gain, shift):
    center = resid - jnp.mean(resid, axis=-1, keepdims=True)
    inverse = lax.rsqrt(jnp.mean(center * center, axis=-1, keepdims=True) + EPSILON)
    normed = center * inverse
    return normed * gain + shift, normed, inverse


def norm_backward(grad_out, normed, inverse, gain):
    grad_normed = grad_out * gain
    first_term = jnp.mean(grad_normed, axis=-1, keepdims=True)
    second_term = jnp.mean(grad_normed * normed, axis=-1, keepdims=True)
    grad_resid = inverse * (grad_normed - first_term - normed * second_term)
    return grad_resid, jnp.sum(grad_out * normed, axis=0), jnp.sum(grad_out, axis=0)


def on_device(
    hidden_in,
    teacher,
    lengths,
    qkv_weight,
    qkv_bias,
    out_weight,
    out_bias,
    ln_gain,
    ln_shift,
    ffn_in,
    ffn_in_bias,
    ffn_out,
):
    _, rows, width = hidden_in.shape
    dp_count = lax.axis_size("dp")
    dp_index = lax.axis_index("dp")
    seq_index = lax.axis_index("seq")
    group, role = seq_index // 2, seq_index % 2
    total_tokens = dp_count * rows * SEQ
    shard = qkv_weight.shape[1]
    half = width // 2
    ffn = ffn_in.shape[1]
    ffn_shard = ffn // dp_count
    ffn_half = ffn_shard // 2

    x_own = hidden_in.reshape(rows, width)
    target = teacher.reshape(rows, width)
    lens = lengths.reshape(CONT)

    def role_columns(weight):
        return lax.dynamic_slice_in_dim(weight, role * half, half, 1)

    quarter = shard // 4
    piece = lambda weight: role_columns(weight).reshape(2, 2, quarter, half)
    full = lambda blocks: blocks.reshape(width, half)
    w_k = full(gather_blocks(piece(qkv_weight[1]), group))
    w_v = full(gather_blocks(piece(qkv_weight[2]), group))
    w_q = full(gather_blocks(piece(qkv_weight[0]), group))
    out_half = shard // 2
    out_piece = pick(out_weight.reshape(2, 2, out_half // 2, 2, half), role, 0)
    out_blocks = gather_blocks(out_piece.transpose(2, 0, 1, 3).reshape(2, 2, out_half // 2, half), group)
    out_blocks = out_blocks.transpose(0, 2, 3, 1, 4).reshape(2, dp_count // 2, out_half, width)
    out_mine = pick(out_blocks, role, 0)
    out_other = swap_pair(pick(out_blocks, 1 - role, 0))
    w_out = ordered(role, out_mine[:, None], out_other[:, None], 1).reshape(half, width)
    up_piece = pick(ffn_in.reshape(shard, dp_count, 2, ffn_half), role, 2)
    w_up = gather_blocks(up_piece.reshape(2, 2, quarter, ffn // 2), group).reshape(width, ffn // 2)
    down_piece = pick(ffn_out.reshape(2, ffn_half, width), role, 0)
    w_down = gather_blocks(down_piece.reshape(2, 2, ffn_half // 4, width), group)
    w_down = w_down.reshape(ffn // 2, width)

    length_sum = jnp.sum(lens).astype(F32)
    small = jnp.concatenate(
        [
            qkv_bias.reshape(-1),
            out_bias.reshape(-1),
            ln_gain.reshape(-1),
            ln_shift.reshape(-1),
            ffn_in_bias,
            jnp.full((128,), length_sum, F32),
        ]
    )[None]
    small = gather_small(small)
    vectors = small[:, : 8 * shard].reshape(dp_count, 4, 2, shard)
    vectors = vectors.transpose(1, 2, 0, 3).reshape(4, 2, width)
    b_qkv, b_out, gains, shifts = vectors[0], vectors[1], vectors[2], vectors[3]
    b_qkv = lax.dynamic_slice_in_dim(b_qkv, role * half, half, 1)
    b_up = small[:, 8 * shard : 8 * shard + ffn_shard].reshape(dp_count, 2, ffn_half)
    b_up = pick(b_up, role, 1).reshape(ffn // 2)
    count = float(dp_count * PROMPT) + jnp.sum(small[:, 8 * shard + ffn_shard])

    x_pair = swap_pair(x_own)
    x_group = jnp.concatenate([x_own, x_pair], axis=0)
    seen_own = lax.ppermute(x_own, "seq", [(0, 2), (1, 3)])
    seen_pair = swap_pair(seen_own)
    x_prompt = jnp.where(group == 0, x_group, jnp.concatenate([seen_own, seen_pair], axis=0))
    local_lens = jnp.where(role == 0, lens, jnp.roll(lens, CONT // 2))
    local_lens = jnp.where(group == 0, 0, local_lens)

    k_prompt = mm(x_prompt, w_k)
    k_self = mm(x_group, w_k)
    v_prompt = mm(x_prompt, w_v) + b_qkv[1]
    v_self = mm(x_group, w_v) + b_qkv[1]
    queries = mm(x_group, w_q) + b_qkv[0]

    attended, lse = attend_forward(local_lens, queries, k_prompt, v_prompt, k_self, v_self)

    def reduce_pair(partial):
        return partial[:rows] + swap_pair(partial[rows:])

    def both_halves(own):
        return jnp.concatenate([own, swap_pair(own)], axis=0)

    first_resid = x_own + reduce_pair(mm(attended, w_out)) + b_out[0]
    first_norm, first_hat, first_inv = norm_forward(first_resid, gains[0], shifts[0])
    norm_group = both_halves(first_norm)
    pre_act = mm(norm_group, w_up) + b_up
    normal_cdf = 0.5 * (1.0 + lax.erf(pre_act * INV_ROOT_TWO))
    activated = pre_act * normal_cdf
    slope = normal_cdf + pre_act * jnp.exp(-0.5 * pre_act * pre_act) * INV_ROOT_TAU
    second_resid = first_norm + reduce_pair(mm(activated, w_down)) + b_out[1]
    final, second_hat, second_inv = norm_forward(second_resid, gains[1], shifts[1])

    slot = seq_index * rows + jnp.arange(rows, dtype=jnp.int32) - PROMPT
    own_len = jnp.sum(
        jnp.where((slot // CLEN)[None] == jnp.arange(CONT, dtype=jnp.int32)[:, None], lens[:, None], 0),
        axis=0,
    )
    valid = ((slot < 0) | (slot % CLEN < own_len)).astype(F32)
    difference = (final - target) * valid[:, None]
    squares = jnp.sum(difference * difference)
    grad_final = difference * (total_tokens / count)
    grad_second, grad_gain_two, grad_shift_two = norm_backward(
        grad_final, second_hat, second_inv, gains[1]
    )
    grad_bias_down = jnp.sum(grad_second, axis=0)
    second_group = both_halves(grad_second)
    grad_w_down = mm_tn(activated, second_group)
    grad_pre = mm_nt(second_group, w_down) * slope
    grad_b_up = jnp.sum(grad_pre, axis=0)
    grad_w_up = mm_tn(norm_group, grad_pre)
    share_down = scatter_blocks(grad_w_down.reshape(dp_count, 2, 2, ffn_half // 4, width), group)
    share_up = scatter_blocks(grad_w_up.reshape(dp_count, 2, 2, quarter, ffn // 2), group)
    grad_first_norm = grad_second + reduce_pair(mm_nt(grad_pre, w_up))
    grad_first, grad_gain_one, grad_shift_one = norm_backward(
        grad_first_norm, first_hat, first_inv, gains[0]
    )
    grad_bias_out = jnp.sum(grad_first, axis=0)
    first_group = both_halves(grad_first)
    grad_attended = mm_nt(first_group, w_out)
    grad_w_out = mm_tn(attended, first_group)
    mine = grad_w_out.reshape(dp_count // 2, 2, out_half, width)
    received = swap_pair(pick(mine, 1 - role, 1))
    mine = ordered(role, pick(mine, role, 1), received, 0)
    mine = mine.reshape(dp_count, 2, out_half // 2, 2, half).transpose(0, 3, 1, 2, 4)
    share_out = scatter_blocks(mine, group)

    d_q, d_kp, d_vp, d_ks, d_vs = attend_backward(
        local_lens, queries, k_prompt, v_prompt, k_self, v_self, attended, grad_attended, lse
    )
    on_prompt = mm_nt(d_kp, w_k) + mm_nt(d_vp, w_v)
    on_prompt = reduce_pair(on_prompt)
    from_cont = lax.ppermute(on_prompt, "seq", [(2, 0), (3, 1)])
    x_both = jnp.concatenate([x_prompt, x_group], axis=0)
    grad_w_k = mm_tn(x_both, jnp.concatenate([d_kp, d_ks], axis=0))
    grad_w_v = mm_tn(x_both, jnp.concatenate([d_vp, d_vs], axis=0))
    grad_w_q = mm_tn(x_group, d_q)
    share_k = scatter_blocks(grad_w_k.reshape(dp_count, 2, 2, quarter, half), group)
    share_v = scatter_blocks(grad_w_v.reshape(dp_count, 2, 2, quarter, half), group)
    share_q = scatter_blocks(grad_w_q.reshape(dp_count, 2, 2, quarter, half), group)
    on_own = reduce_pair(mm_nt(d_q, w_q) + mm_nt(d_ks, w_k) + mm_nt(d_vs, w_v))
    grad_input = grad_first + on_own + jnp.where(group == 0, on_prompt + from_cont, 0.0)

    def join(share, axis):
        return ordered(role, share, swap_pair(share), axis)

    columns = lambda share: join(share.reshape(shard, half), 1)
    out_qkv = jnp.stack([columns(share_q), columns(share_k), columns(share_v)])
    out_out = share_out.transpose(1, 2, 0, 3).reshape(out_half, width)
    out_out = join(out_out, 0)
    out_up = join(share_up.reshape(shard, dp_count, 1, ffn_half), 2).reshape(shard, ffn)
    out_down = join(share_down.reshape(ffn_half, width), 0)

    def spread(value):
        blank = jnp.zeros((width,), F32)
        return lax.dynamic_update_slice(blank, value, (role * half,))

    vectors = jnp.stack(
        [
            spread(jnp.sum(d_q, axis=0)),
            spread(jnp.sum(d_vp, axis=0) + jnp.sum(d_vs, axis=0)),
            grad_bias_out,
            grad_bias_down,
            grad_gain_one,
            grad_gain_two,
            grad_shift_one,
            grad_shift_two,
        ]
    )
    vectors = vectors.reshape(8, dp_count, shard).transpose(1, 0, 2).reshape(dp_count, 8 * shard)
    up = jnp.zeros((dp_count, 2, ffn_half), F32)
    up = lax.dynamic_update_slice(up, grad_b_up.reshape(dp_count, 1, ffn_half), (0, role, 0))
    small = scatter_small(jnp.concatenate([vectors, up.reshape(dp_count, ffn_shard)], axis=1))
    pairs = small[: 8 * shard].reshape(4, 2, shard)
    loss = sum_all(jnp.full((8, 128), squares, F32))[0, 0] / (count * width)
    return (
        final[None],
        grad_input[None],
        out_qkv,
        pairs[0],
        out_out,
        pairs[1],
        pairs[2],
        pairs[3],
        out_up,
        small[8 * shard :],
        out_down,
        loss,
    )


def solution(mesh):
    return jax.shard_map(
        on_device,
        mesh=mesh,
        in_specs=(
            P("dp", "seq", None),
            P("dp", "seq", None),
            P("dp", None),
            P(None, "dp", None),
            P(None, "dp"),
            P("dp", None),
            P(None, "dp"),
            P(None, "dp"),
            P(None, "dp"),
            P("dp", None),
            P("dp"),
            P("dp", None),
        ),
        out_specs=(
            P("dp", "seq", None),
            P("dp", "seq", None),
            P(None, "dp", None),
            P(None, "dp"),
            P("dp", None),
            P(None, "dp"),
            P(None, "dp"),
            P(None, "dp"),
            P("dp", None),
            P("dp"),
            P("dp", None),
            P(),
        ),
        check_vma=False,
    )
```

```python
import functools

import jax
import jax.numpy as jnp
from jax import lax
from jax.experimental import pallas as pl
from jax.experimental.pallas import tpu as pltpu
from jax.sharding import PartitionSpec as P

HD = 64
PROMPT = 1024
CONT = 8
CLEN = 128
SEQ = 4
QB = 256

HIGH = lax.Precision.HIGH
EPSILON = 1e-05
MASKED = -1e30
INV_ROOT_TWO = 0.7071067811865476
INV_ROOT_TAU = 0.3989422804014327
BF = jnp.bfloat16
F32 = jnp.float32


def mm(left, right):
    return lax.dot_general(
        left, right, (((1,), (0,)), ((), ())), precision=HIGH, preferred_element_type=F32
    )


def mm_nt(left, right):
    return lax.dot_general(
        left, right, (((1,), (1,)), ((), ())), precision=HIGH, preferred_element_type=F32
    )


def mm_tn(left, right):
    return lax.dot_general(
        left, right, (((0,), (0,)), ((), ())), precision=HIGH, preferred_element_type=F32
    )


def swap_pair(value):
    return lax.ppermute(value, "seq", [(i, i ^ 1) for i in range(SEQ)])


def swap_group(value):
    return lax.ppermute(value, "seq", [(i, i ^ 2) for i in range(SEQ)])


def swap_dp(value, bit):
    count = lax.axis_size("dp")
    return lax.ppermute(value, "dp", [(i, i ^ (1 << bit)) for i in range(count)])


def ordered(bit, own, other, axis):
    first = jnp.where(bit == 0, own, other)
    second = jnp.where(bit == 0, other, own)
    return jnp.concatenate([first, second], axis=axis)


def pick(value, index, axis):
    return lax.dynamic_index_in_dim(value, index, axis, keepdims=False)


def dp_bits():
    return lax.axis_size("dp").bit_length() - 1


def gather_rows(piece, axis=0):
    return lax.all_gather(piece, "dp", axis=axis, tiled=True)


def scatter_rows(grads, axis=0):
    share = lax.psum_scatter(grads, "dp", scatter_dimension=axis, tiled=True)
    return share + swap_group(share)


def partner(dp_mask, seq_mask):
    return (lax.axis_index("dp") ^ dp_mask, lax.axis_index("seq") ^ seq_mask)


def remote(src, dst, send_sem, recv_sem, target):
    return pltpu.make_async_remote_copy(
        src_ref=src,
        dst_ref=dst,
        send_sem=send_sem,
        recv_sem=recv_sem,
        device_id=target,
        device_id_type=pl.DeviceIdType.MESH,
    )


def greet(bits):
    barrier = pltpu.get_barrier_semaphore()
    others = [partner(1 << bit, 0) for bit in range(bits)] + [partner(0, 1), partner(0, 2)]
    for other in others:
        pl.semaphore_signal(
            barrier, inc=1, device_id=other, device_id_type=pl.DeviceIdType.MESH
        )
    pl.semaphore_wait(barrier, len(others))


def hop_masks(bits):
    return [1 << bit for bit in range(1, bits)] + [1]


def slot_mask(bits, relative):
    masks = hop_masks(bits)
    return sum(masks[p] for p in range(bits) if relative >> p & 1)


def gather_kernel(bits, w_ref, s_ref, x_ref, w_all, s_all, x_pair, x_far, x_far_pair,
                  w_buf, s_buf, send_sem, recv_sem, x_send, x_recv, local_sem):
    me = lax.axis_index("dp")
    masks = hop_masks(bits)
    greet(bits)
    pair = remote(x_ref, x_pair, x_send.at[0], x_recv.at[0], partner(0, 1))
    far = remote(x_ref, x_far, x_send.at[1], x_recv.at[1], partner(0, 2))
    far_pair = remote(x_far, x_far_pair, x_send.at[2], x_recv.at[2], partner(0, 1))
    pair.start()
    far.start()
    started = []

    def blocks(relative):
        slot = me ^ slot_mask(bits, relative)
        return w_all.at[:, slot], s_all.at[slot]

    def forward(relative, first_hop):
        for hop in range(first_hop, bits):
            index = relative | (1 << hop)
            for kind, block in enumerate(blocks(relative)):
                source = block if relative else (w_ref, s_ref)[kind]
                copy = remote(
                    source, block, send_sem.at[kind, index], recv_sem.at[kind, index],
                    partner(masks[hop], 0),
                )
                copy.start()
                started.append(copy)

    forward(0, 0)
    copies = []
    own_w, own_s = blocks(0)
    for index, (src, buf) in enumerate(((w_ref, w_buf), (s_ref, s_buf))):
        copy = pltpu.make_async_copy(src, buf, local_sem.at[index])
        copy.start()
        copies.append(copy)
    for copy in copies:
        copy.wait()
    copies = []
    for index, (buf, dst) in enumerate(((w_buf, own_w), (s_buf, own_s))):
        copy = pltpu.make_async_copy(buf, dst, local_sem.at[index])
        copy.start()
        copies.append(copy)
    for relative in range(1, 1 << bits):
        top = relative.bit_length() - 1
        for kind, block in enumerate(blocks(relative)):
            remote(
                block, block, send_sem.at[kind, relative], recv_sem.at[kind, relative],
                partner(masks[top], 0),
            ).wait_recv()
        forward(relative, top + 1)
        if relative == (1 << bits) - 1:
            far.wait_recv()
            far_pair.start()
    for copy in copies:
        copy.wait()
    for copy in started:
        copy.wait_send()
    pair.wait()
    far.wait_send()
    far_pair.wait()


def gather_all(weights, small, tokens):
    bits = dp_bits()
    count = 1 << bits
    any_spec = pl.BlockSpec(memory_space=pl.ANY)
    three, shard, half = weights.shape
    like = jax.ShapeDtypeStruct(tokens.shape, F32)
    return pl.pallas_call(
        functools.partial(gather_kernel, bits),
        in_specs=[any_spec] * 3,
        out_specs=[any_spec] * 5,
        out_shape=[
            jax.ShapeDtypeStruct((three, count, shard, half), F32),
            jax.ShapeDtypeStruct((count,) + small.shape, F32),
            like,
            like,
            like,
        ],
        scratch_shapes=[
            pltpu.VMEM(weights.shape, F32),
            pltpu.VMEM(small.shape, F32),
            pltpu.SemaphoreType.DMA((2, count)),
            pltpu.SemaphoreType.DMA((2, count)),
            pltpu.SemaphoreType.DMA((3,)),
            pltpu.SemaphoreType.DMA((3,)),
            pltpu.SemaphoreType.DMA((2,)),
        ],
        compiler_params=pltpu.CompilerParams(collective_id=1, has_side_effects=True),
        cost_estimate=pl.CostEstimate(
            flops=0, bytes_accessed=weights.size * 4 * count * 12, transcendentals=0
        ),
        name="gather_attention_weights",
    )(weights, small, tokens)


def scatter_kernel(bits, *refs):
    kinds = 3
    grads, refs = refs[:kinds], refs[kinds:]
    mine, refs = refs[:kinds], refs[kinds:]
    other, refs = refs[: kinds - 1], refs[kinds - 1 :]
    acc, refs = refs[:kinds], refs[kinds:]
    hop_in, refs = refs[:kinds], refs[kinds:]
    x_in, refs = refs[:kinds], refs[kinds:]
    pair_in, send_sem, recv_sem, x_send, x_recv, load_sem, store_sem = refs
    me = lax.axis_index("dp")
    masks = hop_masks(bits)
    count = 1 << bits

    def source(kind, relative):
        slot = me ^ slot_mask(bits, relative)
        return grads[kind].at[:, slot] if kind == 0 else grads[kind].at[slot]

    def hop_copy(kind, relative, hop, from_input):
        index = relative ^ (1 << hop)
        src = source(kind, relative) if from_input else acc[kind].at[relative]
        place = (1 << hop) + index
        return remote(
            src, hop_in[kind].at[place], send_sem.at[kind, relative], recv_sem.at[kind, place],
            partner(masks[hop], 0),
        )

    loads = {}
    for relative in reversed(range(count // 2)):
        for kind in range(kinds):
            copy = pltpu.make_async_copy(
                source(kind, relative), acc[kind].at[relative], load_sem.at[kind, relative]
            )
            copy.start()
            loads[kind, relative] = copy
    greet(bits)
    started = []
    last = bits - 1
    for relative in reversed(range(count // 2, count)):
        for kind in range(kinds):
            copy = hop_copy(kind, relative, last, True)
            copy.start()
            started.append(copy)
    for relative in reversed(range(count // 2)):
        for kind in range(kinds):
            loads[kind, relative].wait()
        lowest = relative.bit_length() - 1
        for hop in reversed(range(max(lowest + 1, 0), bits)):
            for kind in range(kinds):
                hop_copy(kind, relative | (1 << hop), hop, hop == last).wait_recv()
                acc[kind][relative] += hop_in[kind][(1 << hop) + relative]
        if relative:
            for kind in range(kinds):
                copy = hop_copy(kind, relative, lowest, False)
                copy.start()
                started.append(copy)
    crossing = []
    for kind in range(kinds):
        copy = remote(acc[kind].at[0], x_in[kind], x_send.at[kind], x_recv.at[kind], partner(0, 2))
        copy.start()
        crossing.append(copy)
    for kind in range(kinds):
        crossing[kind].wait_recv()
        mine[kind][...] = acc[kind][0] + x_in[kind][...]
    handing = []
    for kind in range(kinds - 1):
        copy = remote(
            mine[kind], other[kind], x_send.at[kinds + kind], x_recv.at[kinds + kind], partner(0, 1)
        )
        copy.start()
        handing.append(copy)
    copy = remote(
        mine[kinds - 1], pair_in, x_send.at[2 * kinds - 1], x_recv.at[2 * kinds - 1], partner(0, 1)
    )
    copy.start()
    handing.append(copy)
    for copy in handing:
        copy.wait()
    mine[kinds - 1][...] += pair_in[...]
    for copy in started + crossing:
        copy.wait_send()


def scatter_all(qkv, out, small):
    bits = dp_bits()
    count = 1 << bits
    any_spec = pl.BlockSpec(memory_space=pl.ANY)
    vmem = pl.BlockSpec(memory_space=pltpu.VMEM)
    shapes = [(qkv.shape[0],) + qkv.shape[2:], out.shape[1:], small.shape[1:]]
    like = [jax.ShapeDtypeStruct(shape, F32) for shape in shapes]
    return pl.pallas_call(
        functools.partial(scatter_kernel, bits),
        in_specs=[any_spec] * 3,
        out_specs=[vmem] * 5,
        out_shape=like + like[:2],
        scratch_shapes=[pltpu.VMEM((count // 2,) + shape, F32) for shape in shapes]
        + [pltpu.VMEM((count,) + shape, F32) for shape in shapes]
        + [pltpu.VMEM(shape, F32) for shape in shapes]
        + [
            pltpu.VMEM(shapes[2], F32),
            pltpu.SemaphoreType.DMA((3, count)),
            pltpu.SemaphoreType.DMA((3, count)),
            pltpu.SemaphoreType.DMA((6,)),
            pltpu.SemaphoreType.DMA((6,)),
            pltpu.SemaphoreType.DMA((3, count // 2)),
            pltpu.SemaphoreType.DMA((1,)),
        ],
        compiler_params=pltpu.CompilerParams(
            collective_id=2, has_side_effects=True, vmem_limit_bytes=40 << 20
        ),
        cost_estimate=pl.CostEstimate(
            flops=0, bytes_accessed=(qkv.size + out.size) * 4 * 12, transcendentals=0
        ),
        name="scatter_attention_grads",
    )(qkv, out, small)


def lane_ids(shape):
    return lax.broadcasted_iota(jnp.int32, shape, 1)


def high_low(value):
    high = value.astype(BF).astype(F32)
    return high, value - high


def packs(value, head):
    high, low = high_low(value)
    left = lane_ids(value.shape) < HD
    high_r = pltpu.roll(high, HD, 1)
    low_r = pltpu.roll(low, HD, 1)
    if head == 0:
        return (
            jnp.where(left, high, low_r).astype(BF),
            jnp.where(left, high, high_r).astype(BF),
            jnp.where(left, low, low_r).astype(BF),
        )
    return (
        jnp.where(left, high_r, low).astype(BF),
        jnp.where(left, high_r, high).astype(BF),
        jnp.where(left, low_r, low).astype(BF),
    )


def dot(left, right):
    return lax.dot_general(left, right, (((1,), (0,)), ((), ())), preferred_element_type=F32)


def dot_nt(left, right):
    return lax.dot_general(left, right, (((1,), (1,)), ((), ())), preferred_element_type=F32)


def split(value):
    high = value.astype(BF)
    return high, (value - high.astype(F32)).astype(BF)


def self_mask(lens_ref, block, query_axis):
    key_axis = 1 - query_axis
    query = lax.broadcasted_iota(jnp.int32, (QB, QB), query_axis)
    key = lax.broadcasted_iota(jnp.int32, (QB, QB), key_axis)
    per = QB // CLEN
    seen = jnp.zeros((QB, QB), jnp.bool_)
    for piece in range(per):
        low = piece * CLEN
        limit = low + lens_ref[block * per + piece]
        inside = (query >= low) & (query < low + CLEN) & (key >= low) & (key < limit)
        seen = seen | inside
    return seen & (key <= query)


def forward_kernel(lens_ref, q_ref, kp_ref, vp_ref, ks_ref, vs_ref, o_ref, lse_ref,
                   q4, k4p, k4s, v2p, v2s):
    rows = q_ref.shape[0]
    for head in range(2):
        _, hh, ll = packs(q_ref[...] * 0.125, head)
        q4[head, :, :128] = hh
        q4[head, :, 128:] = ll
        for src, dst in ((kp_ref, k4p), (ks_ref, k4s)):
            hl, _, _ = packs(src[...], head)
            dst[head, :, :128] = hl
            dst[head, :, 128:] = hl
        v2p[head] = packs(vp_ref[...], head)[0]
        v2s[head] = packs(vs_ref[...], head)[0]

    def step(block, carry):
        here = pl.ds(pl.multiple_of(block * QB, QB), QB)
        seen = self_mask(lens_ref, block, 0)
        results = []
        for head in range(2):
            query = q4[head, here, :]
            far = dot_nt(query, k4p[head])
            near = jnp.where(seen, dot_nt(query, k4s[head, here, :]), MASKED)
            top = jnp.maximum(
                jnp.max(far, axis=1, keepdims=True), jnp.max(near, axis=1, keepdims=True)
            )
            far = jnp.exp(far - top)
            near = jnp.exp(near - top)
            total = jnp.sum(far, axis=1, keepdims=True) + jnp.sum(near, axis=1, keepdims=True)
            far_h, far_l = split(far)
            near_h, near_l = split(near)
            out = dot(far_h, v2p[head]) + dot(far_l, v2p[head])
            value = v2s[head, here, :]
            out = out + dot(near_h, value) + dot(near_l, value)
            out = (out + pltpu.roll(out, HD, 1)) / total
            lse = top + jnp.log(total)
            lse_ref[head, :, here] = jnp.transpose(jnp.broadcast_to(lse, (QB, 128)))[:8]
            results.append(out)
        o_ref[here, :] = jnp.where(lane_ids((QB, 128)) < HD, results[0], results[1])
        return carry

    lax.fori_loop(0, rows // QB, step, 0)


def attend_forward(lens, q, kp, vp, ks, vs):
    rows, width = q.shape
    prompt = kp.shape[0]
    heads = width // HD
    spec = lambda n: pl.BlockSpec((n, 128), lambda j, lens: (0, j))
    flops = heads * 2 * rows * (prompt + QB) * (256 + 256)
    return pl.pallas_call(
        forward_kernel,
        grid_spec=pltpu.PrefetchScalarGridSpec(
            num_scalar_prefetch=1,
            grid=(heads // 2,),
            in_specs=[spec(rows), spec(prompt), spec(prompt), spec(rows), spec(rows)],
            out_specs=[spec(rows), pl.BlockSpec((2, 8, rows), lambda j, lens: (j, 0, 0))],
            scratch_shapes=[
                pltpu.VMEM((2, rows, 256), BF),
                pltpu.VMEM((2, prompt, 256), BF),
                pltpu.VMEM((2, rows, 256), BF),
                pltpu.VMEM((2, prompt, 128), BF),
                pltpu.VMEM((2, rows, 128), BF),
            ],
        ),
        out_shape=[
            jax.ShapeDtypeStruct((rows, width), F32),
            jax.ShapeDtypeStruct((heads, 8, rows), F32),
        ],
        compiler_params=pltpu.CompilerParams(vmem_limit_bytes=48 << 20),
        cost_estimate=pl.CostEstimate(
            flops=flops, bytes_accessed=6 * rows * width * 4, transcendentals=heads * rows * prompt
        ),
        name="attention_forward",
    )(lens, q, kp, vp, ks, vs)


def backward_kernel(lens_ref, q_ref, kp_ref, vp_ref, ks_ref, vs_ref, o_ref, g_ref, lse_ref,
                    dq_ref, dkp_ref, dvp_ref, dks_ref, dvs_ref,
                    q4, k4p, k4s, v4p, v4s, g4, q2, g2, k2tp, k2ts, delta):
    rows = q_ref.shape[0]
    prod = jnp.transpose(o_ref[...] * g_ref[...])
    for head in range(2):
        hl, hh, ll = packs(q_ref[...] * 0.125, head)
        q2[head] = hl
        q4[head, :, :128] = hh
        q4[head, :, 128:] = ll
        hl, hh, ll = packs(g_ref[...], head)
        g2[head] = hl
        g4[head, :, :128] = hh
        g4[head, :, 128:] = ll
        for src, dst in ((kp_ref, k4p), (ks_ref, k4s), (vp_ref, v4p), (vs_ref, v4s)):
            hl, _, _ = packs(src[...], head)
            dst[head, :, :128] = hl
            dst[head, :, 128:] = hl
        for src, dst in ((kp_ref, k2tp), (ks_ref, k2ts)):
            flipped = jnp.transpose(src[...])[head * HD : head * HD + HD]
            high, low = high_low(flipped)
            dst[head, :HD] = high.astype(BF)
            dst[head, HD:] = low.astype(BF)
        delta[head] = jnp.broadcast_to(
            jnp.sum(prod[head * HD : head * HD + HD], axis=0, keepdims=True), (8, rows)
        )
    dkp_ref[...] = jnp.zeros_like(dkp_ref)
    dvp_ref[...] = jnp.zeros_like(dvp_ref)

    def step(block, carry):
        here = pl.ds(pl.multiple_of(block * QB, QB), QB)
        seen = self_mask(lens_ref, block, 1)
        keep = {}
        for head in range(2):
            query = q4[head, here, :]
            grad = g4[head, here, :]
            lse = lse_ref[head, :1, here]
            low = delta[head, :1, here]
            far = jnp.exp(dot_nt(k4p[head], query) - lse)
            near = jnp.exp(jnp.where(seen, dot_nt(k4s[head, here, :], query), MASKED) - lse)
            far_g = far * (dot_nt(v4p[head], grad) - low)
            near_g = near * (dot_nt(v4s[head, here, :], grad) - low)
            grad2 = g2[head, here, :]
            query2 = q2[head, here, :]
            ph, p_l = split(far)
            dvp = dot(ph, grad2) + dot(p_l, grad2)
            ph, p_l = split(near)
            dvs = dot(ph, grad2) + dot(p_l, grad2)
            sh, sl = split(far_g)
            dkp = dot(sh, query2) + dot(sl, query2)
            dq = dot(k2tp[head], sh) + dot(k2tp[head], sl)
            sh, sl = split(near_g)
            dks = dot(sh, query2) + dot(sl, query2)
            side = k2ts[head, :, here]
            dq = dq + dot(side, sh) + dot(side, sl)
            dq = dq[:HD] + dq[HD:]
            keep[head] = (
                dq,
                dkp + pltpu.roll(dkp, HD, 1),
                dvp + pltpu.roll(dvp, HD, 1),
                dks + pltpu.roll(dks, HD, 1),
                dvs + pltpu.roll(dvs, HD, 1),
            )
        left = lane_ids((QB, 128)) < HD
        far_left = lane_ids(dkp_ref.shape) < HD
        dq_ref[here, :] = jnp.transpose(
            jnp.concatenate([keep[0][0], keep[1][0]], axis=0)
        ) * 0.125
        dkp_ref[...] += jnp.where(far_left, keep[0][1], keep[1][1])
        dvp_ref[...] += jnp.where(far_left, keep[0][2], keep[1][2])
        dks_ref[here, :] = jnp.where(left, keep[0][3], keep[1][3])
        dvs_ref[here, :] = jnp.where(left, keep[0][4], keep[1][4])
        return carry

    lax.fori_loop(0, rows // QB, step, 0)


def attend_backward(lens, q, kp, vp, ks, vs, out, grad, lse):
    rows, width = q.shape
    prompt = kp.shape[0]
    heads = width // HD
    spec = lambda n: pl.BlockSpec((n, 128), lambda j, lens: (0, j))
    flops = heads * 2 * rows * (prompt + QB) * (256 * 5)
    shape = lambda n: jax.ShapeDtypeStruct((n, width), F32)
    return pl.pallas_call(
        backward_kernel,
        grid_spec=pltpu.PrefetchScalarGridSpec(
            num_scalar_prefetch=1,
            grid=(heads // 2,),
            in_specs=[
                spec(rows), spec(prompt), spec(prompt), spec(rows), spec(rows),
                spec(rows), spec(rows), pl.BlockSpec((2, 8, rows), lambda j, lens: (j, 0, 0)),
            ],
            out_specs=[spec(rows), spec(prompt), spec(prompt), spec(rows), spec(rows)],
            scratch_shapes=[
                pltpu.VMEM((2, rows, 256), BF),
                pltpu.VMEM((2, prompt, 256), BF),
                pltpu.VMEM((2, rows, 256), BF),
                pltpu.VMEM((2, prompt, 256), BF),
                pltpu.VMEM((2, rows, 256), BF),
                pltpu.VMEM((2, rows, 256), BF),
                pltpu.VMEM((2, rows, 128), BF),
                pltpu.VMEM((2, rows, 128), BF),
                pltpu.VMEM((2, 128, prompt), BF),
                pltpu.VMEM((2, 128, rows), BF),
                pltpu.VMEM((2, 8, rows), F32),
            ],
        ),
        out_shape=[shape(rows), shape(prompt), shape(prompt), shape(rows), shape(rows)],
        compiler_params=pltpu.CompilerParams(vmem_limit_bytes=56 << 20),
        cost_estimate=pl.CostEstimate(
            flops=flops, bytes_accessed=12 * rows * width * 4, transcendentals=heads * rows * prompt
        ),
        name="attention_backward",
    )(lens, q, kp, vp, ks, vs, out, grad, lse)


def norm_forward(resid, gain, shift):
    center = resid - jnp.mean(resid, axis=-1, keepdims=True)
    inverse = lax.rsqrt(jnp.mean(center * center, axis=-1, keepdims=True) + EPSILON)
    normed = center * inverse
    return normed * gain + shift, normed, inverse


def norm_backward(grad_out, normed, inverse, gain):
    grad_normed = grad_out * gain
    first_term = jnp.mean(grad_normed, axis=-1, keepdims=True)
    second_term = jnp.mean(grad_normed * normed, axis=-1, keepdims=True)
    grad_resid = inverse * (grad_normed - first_term - normed * second_term)
    return grad_resid, jnp.sum(grad_out * normed, axis=0), jnp.sum(grad_out, axis=0)


def on_device(
    hidden_in,
    teacher,
    lengths,
    qkv_weight,
    qkv_bias,
    out_weight,
    out_bias,
    ln_gain,
    ln_shift,
    ffn_in,
    ffn_in_bias,
    ffn_out,
):
    _, rows, width = hidden_in.shape
    dp_count = lax.axis_size("dp")
    dp_index = lax.axis_index("dp")
    seq_index = lax.axis_index("seq")
    group, role = seq_index // 2, seq_index % 2
    total_tokens = dp_count * rows * SEQ
    shard = qkv_weight.shape[1]
    half = width // 2
    ffn = ffn_in.shape[1]
    ffn_shard = ffn // dp_count
    ffn_half = ffn_shard // 2

    x_own = hidden_in.reshape(rows, width)
    target = teacher.reshape(rows, width)
    lens = lengths.reshape(CONT)

    length_sum = jnp.sum(lens).astype(F32)
    used = 8 * shard + ffn_shard
    small_rows = -(-(used + 1) // 1024) * 8
    small = jnp.concatenate(
        [
            qkv_bias.reshape(-1),
            out_bias.reshape(-1),
            ln_gain.reshape(-1),
            ln_shift.reshape(-1),
            ffn_in_bias,
            jnp.full((small_rows * 128 - used,), length_sum, F32),
        ]
    ).reshape(small_rows, 128)
    w_qkv, small, x_pair, x_far, x_far_pair = gather_all(
        lax.dynamic_slice_in_dim(qkv_weight, role * half, half, 2), small, x_own
    )
    w_qkv = w_qkv.reshape(3, width, half)
    w_q, w_k, w_v = w_qkv[0], w_qkv[1], w_qkv[2]
    small = small.reshape(dp_count, small_rows * 128)
    vectors = small[:, : 8 * shard].reshape(dp_count, 4, 2, shard)
    vectors = vectors.transpose(1, 2, 0, 3).reshape(4, 2, width)
    b_qkv, b_out, gains, shifts = vectors[0], vectors[1], vectors[2], vectors[3]
    b_qkv = lax.dynamic_slice_in_dim(b_qkv, role * half, half, 1)
    b_up = small[:, 8 * shard : used].reshape(dp_count, 2, ffn_half)
    b_up = pick(b_up, role, 1).reshape(ffn // 2)
    count = float(dp_count * PROMPT) + jnp.sum(small[:, used])

    out_half = shard // 2
    up_piece = pick(ffn_in.reshape(shard, dp_count, 2, ffn_half), role, 2).reshape(shard, ffn // 2)
    out_piece = pick(out_weight.reshape(2, out_half, width), role, 0)
    out_lines = out_half * width // (ffn // 2)
    both = lax.all_gather(
        jnp.concatenate([out_piece.reshape(out_lines, ffn // 2), up_piece], axis=0), "dp", axis=0
    )
    w_up = both[:, out_lines:].reshape(width, ffn // 2)
    out_blocks = both[:, :out_lines].reshape(2, dp_count // 2, out_half, width)
    out_mine = pick(out_blocks, role, 0)
    out_other = swap_pair(pick(out_blocks, 1 - role, 0))
    w_out = ordered(role, out_mine[:, None], out_other[:, None], 1).reshape(half, width)
    w_down = gather_rows(pick(ffn_out.reshape(2, ffn_half, width), role, 0))

    x_group = jnp.concatenate([x_own, x_pair], axis=0)
    x_prompt = jnp.where(group == 0, x_group, jnp.concatenate([x_far, x_far_pair], axis=0))
    local_lens = jnp.where(role == 0, lens, jnp.roll(lens, CONT // 2))
    local_lens = jnp.where(group == 0, 0, local_lens)

    k_prompt = mm(x_prompt, w_k)
    k_self = mm(x_group, w_k)
    v_prompt = mm(x_prompt, w_v) + b_qkv[1]
    v_self = mm(x_group, w_v) + b_qkv[1]
    queries = mm(x_group, w_q) + b_qkv[0]

    attended, lse = attend_forward(local_lens, queries, k_prompt, v_prompt, k_self, v_self)

    def reduce_pair(partial):
        return partial[:rows] + swap_pair(partial[rows:])

    def both_halves(own):
        return jnp.concatenate([own, swap_pair(own)], axis=0)

    first_resid = x_own + reduce_pair(mm(attended, w_out)) + b_out[0]
    first_norm, first_hat, first_inv = norm_forward(first_resid, gains[0], shifts[0])
    norm_group = both_halves(first_norm)
    pre_act = mm(norm_group, w_up) + b_up
    normal_cdf = 0.5 * (1.0 + lax.erf(pre_act * INV_ROOT_TWO))
    activated = pre_act * normal_cdf
    slope = normal_cdf + pre_act * jnp.exp(-0.5 * pre_act * pre_act) * INV_ROOT_TAU
    second_resid = first_norm + reduce_pair(mm(activated, w_down)) + b_out[1]
    final, second_hat, second_inv = norm_forward(second_resid, gains[1], shifts[1])

    slot = seq_index * rows + jnp.arange(rows, dtype=jnp.int32) - PROMPT
    own_len = jnp.sum(
        jnp.where((slot // CLEN)[None] == jnp.arange(CONT, dtype=jnp.int32)[:, None], lens[:, None], 0),
        axis=0,
    )
    valid = ((slot < 0) | (slot % CLEN < own_len)).astype(F32)
    difference = (final - target) * valid[:, None]
    squares = jnp.sum(difference * difference)
    grad_final = difference * (total_tokens / count)
    grad_second, grad_gain_two, grad_shift_two = norm_backward(
        grad_final, second_hat, second_inv, gains[1]
    )
    grad_bias_down = jnp.sum(grad_second, axis=0)
    second_group = both_halves(grad_second)
    grad_w_down = mm_tn(activated, second_group)
    grad_pre = mm_nt(second_group, w_down) * slope
    grad_b_up = jnp.sum(grad_pre, axis=0)
    grad_w_up = mm_tn(norm_group, grad_pre)
    share_down = scatter_rows(grad_w_down)
    share_up = scatter_rows(grad_w_up)
    grad_first_norm = grad_second + reduce_pair(mm_nt(grad_pre, w_up))
    grad_first, grad_gain_one, grad_shift_one = norm_backward(
        grad_first_norm, first_hat, first_inv, gains[0]
    )
    grad_bias_out = jnp.sum(grad_first, axis=0)
    first_group = both_halves(grad_first)
    grad_attended = mm_nt(first_group, w_out)
    grad_w_out = mm_tn(attended, first_group)
    mine = grad_w_out.reshape(dp_count // 2, 2, out_half, width)
    received = swap_pair(pick(mine, 1 - role, 1))
    mine = ordered(role, pick(mine, role, 1), received, 0)
    d_q, d_kp, d_vp, d_ks, d_vs = attend_backward(
        local_lens, queries, k_prompt, v_prompt, k_self, v_self, attended, grad_attended, lse
    )
    on_prompt = mm_nt(d_kp, w_k) + mm_nt(d_vp, w_v)
    on_prompt = reduce_pair(on_prompt)
    from_cont = lax.ppermute(on_prompt, "seq", [(2, 0), (3, 1)])
    x_both = jnp.concatenate([x_prompt, x_group], axis=0)
    grad_w_k = mm_tn(x_both, jnp.concatenate([d_kp, d_ks], axis=0))
    grad_w_v = mm_tn(x_both, jnp.concatenate([d_vp, d_vs], axis=0))
    grad_w_q = mm_tn(x_group, d_q)
    on_own = reduce_pair(mm_nt(d_q, w_q) + mm_nt(d_ks, w_k) + mm_nt(d_vs, w_v))
    grad_input = grad_first + on_own + jnp.where(group == 0, on_prompt + from_cont, 0.0)

    def spread(value):
        blank = jnp.zeros((width,), F32)
        return lax.dynamic_update_slice(blank, value, (role * half,))

    vectors = jnp.stack(
        [
            spread(jnp.sum(d_q, axis=0)),
            spread(jnp.sum(d_vp, axis=0) + jnp.sum(d_vs, axis=0)),
            grad_bias_out,
            grad_bias_down,
            grad_gain_one,
            grad_gain_two,
            grad_shift_one,
            grad_shift_two,
        ]
    )
    vectors = vectors.reshape(8, dp_count, shard).transpose(1, 0, 2).reshape(dp_count, 8 * shard)
    up = jnp.zeros((dp_count, 2, ffn_half), F32)
    up = lax.dynamic_update_slice(up, grad_b_up.reshape(dp_count, 1, ffn_half), (0, role, 0))
    small = jnp.concatenate(
        [
            vectors,
            up.reshape(dp_count, ffn_shard),
            jnp.full((dp_count, small_rows * 128 - used), squares, F32),
        ],
        axis=1,
    ).reshape(dp_count, small_rows, 128)
    share_qkv, share_out, small, other_qkv, other_out = scatter_all(
        jnp.stack([grad_w_q, grad_w_k, grad_w_v]).reshape(3, dp_count, shard, half),
        mine.reshape(dp_count, out_half, width),
        small,
    )
    small = small.reshape(small_rows * 128)
    pairs = small[: 8 * shard].reshape(4, 2, shard)
    loss = small[used] / (count * width)

    def join(share, axis):
        return ordered(role, share, swap_pair(share), axis)

    out_qkv = ordered(role, share_qkv, other_qkv, 2)
    out_out = ordered(role, share_out, other_out, 0)
    out_up = join(share_up.reshape(shard, dp_count, 1, ffn_half), 2).reshape(shard, ffn)
    out_down = join(share_down.reshape(ffn_half, width), 0)
    return (
        final[None],
        grad_input[None],
        out_qkv,
        pairs[0],
        out_out,
        pairs[1],
        pairs[2],
        pairs[3],
        out_up,
        small[8 * shard : used],
        out_down,
        loss,
    )


def solution(mesh):
    return jax.shard_map(
        on_device,
        mesh=mesh,
        in_specs=(
            P("dp", "seq", None),
            P("dp", "seq", None),
            P("dp", None),
            P(None, "dp", None),
            P(None, "dp"),
            P("dp", None),
            P(None, "dp"),
            P(None, "dp"),
            P(None, "dp"),
            P("dp", None),
            P("dp"),
            P("dp", None),
        ),
        out_specs=(
            P("dp", "seq", None),
            P("dp", "seq", None),
            P(None, "dp", None),
            P(None, "dp"),
            P("dp", None),
            P(None, "dp"),
            P(None, "dp"),
            P(None, "dp"),
            P("dp", None),
            P("dp"),
            P("dp", None),
            P(),
        ),
        check_vma=False,
    )
```

```python
import functools

import jax
import jax.numpy as jnp
from jax import lax
from jax.experimental import pallas as pl
from jax.experimental.pallas import tpu as pltpu
from jax.sharding import PartitionSpec as P

HD = 64
PROMPT = 1024
CONT = 8
CLEN = 128
SEQ = 4
QB = 256

HIGH = lax.Precision.HIGH
EPSILON = 1e-05
MASKED = -1e30
INV_ROOT_TWO = 0.7071067811865476
INV_ROOT_TAU = 0.3989422804014327
BF = jnp.bfloat16
F32 = jnp.float32


def mm(left, right):
    return lax.dot_general(
        left, right, (((1,), (0,)), ((), ())), precision=HIGH, preferred_element_type=F32
    )


def mm_nt(left, right):
    return lax.dot_general(
        left, right, (((1,), (1,)), ((), ())), precision=HIGH, preferred_element_type=F32
    )


def mm_tn(left, right):
    return lax.dot_general(
        left, right, (((0,), (0,)), ((), ())), precision=HIGH, preferred_element_type=F32
    )


def swap_pair(value):
    return lax.ppermute(value, "seq", [(i, i ^ 1) for i in range(SEQ)])


def swap_group(value):
    return lax.ppermute(value, "seq", [(i, i ^ 2) for i in range(SEQ)])


def swap_dp(value, bit):
    count = lax.axis_size("dp")
    return lax.ppermute(value, "dp", [(i, i ^ (1 << bit)) for i in range(count)])


def ordered(bit, own, other, axis):
    first = jnp.where(bit == 0, own, other)
    second = jnp.where(bit == 0, other, own)
    return jnp.concatenate([first, second], axis=axis)


def pick(value, index, axis):
    return lax.dynamic_index_in_dim(value, index, axis, keepdims=False)


def dp_bits():
    return lax.axis_size("dp").bit_length() - 1


def gather_rows(piece, axis=0):
    return lax.all_gather(piece, "dp", axis=axis, tiled=True)


def scatter_rows(grads, axis=0):
    share = lax.psum_scatter(grads, "dp", scatter_dimension=axis, tiled=True)
    return share + swap_group(share)


def partner(dp_mask, seq_mask):
    return (lax.axis_index("dp") ^ dp_mask, lax.axis_index("seq") ^ seq_mask)


def remote(src, dst, send_sem, recv_sem, target):
    return pltpu.make_async_remote_copy(
        src_ref=src,
        dst_ref=dst,
        send_sem=send_sem,
        recv_sem=recv_sem,
        device_id=target,
        device_id_type=pl.DeviceIdType.MESH,
    )


def greet(bits):
    barrier = pltpu.get_barrier_semaphore()
    others = [partner(1 << bit, 0) for bit in range(bits)] + [partner(0, 1), partner(0, 2)]
    for other in others:
        pl.semaphore_signal(
            barrier, inc=1, device_id=other, device_id_type=pl.DeviceIdType.MESH
        )
    pl.semaphore_wait(barrier, len(others))


def hop_masks(bits):
    return [1 << bit for bit in range(1, bits)] + [1]


def slot_mask(bits, relative):
    masks = hop_masks(bits)
    return sum(masks[p] for p in range(bits) if relative >> p & 1)


def scatter_kernel(bits, *refs):
    kinds = 3
    grads, refs = refs[:kinds], refs[kinds:]
    mine, refs = refs[:kinds], refs[kinds:]
    other, refs = refs[: kinds - 1], refs[kinds - 1 :]
    acc, refs = refs[:kinds], refs[kinds:]
    hop_in, refs = refs[:kinds], refs[kinds:]
    x_in, refs = refs[:kinds], refs[kinds:]
    pair_in, send_sem, recv_sem, x_send, x_recv, load_sem, store_sem = refs
    me = lax.axis_index("dp")
    masks = hop_masks(bits)
    count = 1 << bits

    def source(kind, relative):
        slot = me ^ slot_mask(bits, relative)
        return grads[kind].at[:, slot] if kind == 0 else grads[kind].at[slot]

    def hop_copy(kind, relative, hop, from_input):
        index = relative ^ (1 << hop)
        src = source(kind, relative) if from_input else acc[kind].at[relative]
        place = (1 << hop) + index
        return remote(
            src, hop_in[kind].at[place], send_sem.at[kind, relative], recv_sem.at[kind, place],
            partner(masks[hop], 0),
        )

    loads = {}
    for relative in reversed(range(count // 2)):
        for kind in range(kinds):
            copy = pltpu.make_async_copy(
                source(kind, relative), acc[kind].at[relative], load_sem.at[kind, relative]
            )
            copy.start()
            loads[kind, relative] = copy
    greet(bits)
    started = []
    last = bits - 1
    for relative in reversed(range(count // 2, count)):
        for kind in range(kinds):
            copy = hop_copy(kind, relative, last, True)
            copy.start()
            started.append(copy)
    for relative in reversed(range(count // 2)):
        for kind in range(kinds):
            loads[kind, relative].wait()
        lowest = relative.bit_length() - 1
        for hop in reversed(range(max(lowest + 1, 0), bits)):
            for kind in range(kinds):
                hop_copy(kind, relative | (1 << hop), hop, hop == last).wait_recv()
                acc[kind][relative] += hop_in[kind][(1 << hop) + relative]
        if relative:
            for kind in range(kinds):
                copy = hop_copy(kind, relative, lowest, False)
                copy.start()
                started.append(copy)
    crossing = []
    for kind in range(kinds):
        copy = remote(acc[kind].at[0], x_in[kind], x_send.at[kind], x_recv.at[kind], partner(0, 2))
        copy.start()
        crossing.append(copy)
    for kind in range(kinds):
        crossing[kind].wait_recv()
        mine[kind][...] = acc[kind][0] + x_in[kind][...]
    handing = []
    for kind in range(kinds - 1):
        copy = remote(
            mine[kind], other[kind], x_send.at[kinds + kind], x_recv.at[kinds + kind], partner(0, 1)
        )
        copy.start()
        handing.append(copy)
    copy = remote(
        mine[kinds - 1], pair_in, x_send.at[2 * kinds - 1], x_recv.at[2 * kinds - 1], partner(0, 1)
    )
    copy.start()
    handing.append(copy)
    for copy in handing:
        copy.wait()
    mine[kinds - 1][...] += pair_in[...]
    for copy in started + crossing:
        copy.wait_send()


def scatter_all(qkv, out, small):
    bits = dp_bits()
    count = 1 << bits
    any_spec = pl.BlockSpec(memory_space=pl.ANY)
    vmem = pl.BlockSpec(memory_space=pltpu.VMEM)
    shapes = [(qkv.shape[0],) + qkv.shape[2:], out.shape[1:], small.shape[1:]]
    like = [jax.ShapeDtypeStruct(shape, F32) for shape in shapes]
    return pl.pallas_call(
        functools.partial(scatter_kernel, bits),
        in_specs=[any_spec] * 3,
        out_specs=[vmem] * 5,
        out_shape=like + like[:2],
        scratch_shapes=[pltpu.VMEM((count // 2,) + shape, F32) for shape in shapes]
        + [pltpu.VMEM((count,) + shape, F32) for shape in shapes]
        + [pltpu.VMEM(shape, F32) for shape in shapes]
        + [
            pltpu.VMEM(shapes[2], F32),
            pltpu.SemaphoreType.DMA((3, count)),
            pltpu.SemaphoreType.DMA((3, count)),
            pltpu.SemaphoreType.DMA((6,)),
            pltpu.SemaphoreType.DMA((6,)),
            pltpu.SemaphoreType.DMA((3, count // 2)),
            pltpu.SemaphoreType.DMA((1,)),
        ],
        compiler_params=pltpu.CompilerParams(
            collective_id=2, has_side_effects=True, vmem_limit_bytes=40 << 20
        ),
        cost_estimate=pl.CostEstimate(
            flops=0, bytes_accessed=(qkv.size + out.size) * 4 * 12, transcendentals=0
        ),
        name="scatter_attention_grads",
    )(qkv, out, small)


def lane_ids(shape):
    return lax.broadcasted_iota(jnp.int32, shape, 1)


def high_low(value):
    high = value.astype(BF).astype(F32)
    return high, value - high


def packs(value, head):
    high, low = high_low(value)
    left = lane_ids(value.shape) < HD
    high_r = pltpu.roll(high, HD, 1)
    low_r = pltpu.roll(low, HD, 1)
    if head == 0:
        return (
            jnp.where(left, high, low_r).astype(BF),
            jnp.where(left, high, high_r).astype(BF),
            jnp.where(left, low, low_r).astype(BF),
        )
    return (
        jnp.where(left, high_r, low).astype(BF),
        jnp.where(left, high_r, high).astype(BF),
        jnp.where(left, low_r, low).astype(BF),
    )


def dot(left, right):
    return lax.dot_general(left, right, (((1,), (0,)), ((), ())), preferred_element_type=F32)


def dot_nt(left, right):
    return lax.dot_general(left, right, (((1,), (1,)), ((), ())), preferred_element_type=F32)


def split(value):
    high = value.astype(BF)
    return high, (value - high.astype(F32)).astype(BF)


def self_mask(lens_ref, block, query_axis):
    key_axis = 1 - query_axis
    query = lax.broadcasted_iota(jnp.int32, (QB, QB), query_axis)
    key = lax.broadcasted_iota(jnp.int32, (QB, QB), key_axis)
    per = QB // CLEN
    seen = jnp.zeros((QB, QB), jnp.bool_)
    for piece in range(per):
        low = piece * CLEN
        limit = low + lens_ref[block * per + piece]
        inside = (query >= low) & (query < low + CLEN) & (key >= low) & (key < limit)
        seen = seen | inside
    return seen & (key <= query)


THIRDS = ((0, 1), (1, 2))


def forward_kernel(bits, lens_ref, w_ref, s_ref, x_ref, out_ref, up_ref, down_ref,
                   w_all, s_all, x_both, k_both, v_both, q_all, o_all, lse_all,
                   out_all, up_all, down_all, out_other,
                   x_high, x_low, w_high, w_low, q4, k4p, k4s, v2p, v2s,
                   out_buf, up_buf, down_buf,
                   send_sem, recv_sem, x_send, x_recv, own_sem, hop_send, hop_recv, pair_sem):
    me = lax.axis_index("dp")
    seq = lax.axis_index("seq")
    group, role = seq // 2, seq % 2
    masks = hop_masks(bits)
    rows, width = x_ref.shape
    half = w_ref.shape[2]
    layers = 1 << (bits - 1)
    quarter = layers // 4
    greet(bits)

    pieces = ((out_ref, out_buf, out_all), (up_ref, up_buf, up_all), (down_ref, down_buf, down_all))
    loads = [pltpu.make_async_copy(src, buf, own_sem.at[i]) for i, (src, buf, _) in enumerate(pieces)]
    own_w = pltpu.make_async_copy(w_ref, w_all.at[:, me], own_sem.at[3])
    own_s = pltpu.make_async_copy(s_ref, s_all.at[me], own_sem.at[4])
    own_x = pltpu.make_async_copy(x_ref, x_both.at[pl.ds(2 * rows, rows)], own_sem.at[5])
    for copy in loads + [own_w, own_s, own_x]:
        copy.start()
    to_pair = remote(
        x_ref, x_both.at[pl.ds(3 * rows, rows)], x_send.at[0], x_recv.at[0], partner(0, 1)
    )
    to_far = remote(x_ref, x_both.at[pl.ds(0, rows)], x_send.at[1], x_recv.at[1], partner(0, 2))
    far_pair = remote(
        x_both.at[pl.ds(0, rows)], x_both.at[pl.ds(rows, rows)], x_send.at[2], x_recv.at[2],
        partner(0, 1),
    )
    to_pair.start()

    @pl.when(group == 0)
    def _():
        to_far.start()

    def blocks(relative):
        slot = me ^ slot_mask(bits, relative)
        return w_all.at[:, slot], s_all.at[slot]

    started = []

    def forward(relative, first_hop):
        for hop in range(first_hop, bits):
            index = relative | (1 << hop)
            for kind, block in enumerate(blocks(relative)):
                source = block if relative else (w_ref, s_ref)[kind]
                copy = remote(
                    source, block, send_sem.at[kind, index], recv_sem.at[kind, index],
                    partner(masks[hop], 0),
                )
                copy.start()
                started.append(copy)

    forward(0, 0)
    for copy in loads:
        copy.wait()
    stores = [pltpu.make_async_copy(buf, dst.at[me], own_sem.at[i]) for i, (_, buf, dst) in enumerate(pieces)]
    for copy in stores:
        copy.start()

    def part(kind, layer, last, other_x, piece):
        slot = me ^ (layer * 2) ^ last
        first, count = THIRDS[piece]
        return pieces[kind][2].at[slot, group ^ other_x, pl.ds(first, count)]

    def sent(kind, layer, last, other_x, piece, step, dp_mask, seq_mask):
        region = part(kind, layer, last, other_x, piece)
        return remote(
            region, region, hop_send.at[kind, layer, step], hop_recv.at[kind, layer, step],
            partner(dp_mask, seq_mask),
        )

    steps = {
        1: (0, 0, 0, 0, 2),
        2: (0, 0, 0, 1, 0),
        3: (0, 1, 0, 1, 0),
        4: (0, 0, 1, 1, 0),
        5: (0, 0, 1, 0, 2),
        6: (1, 0, 1, 0, 2),
    }

    def give(kind, layer, step):
        last, other_x, piece, dp_mask, seq_mask = steps[step]
        return sent(kind, layer, last, other_x, piece, step, dp_mask, seq_mask)

    def take(kind, layer, step):
        last, other_x, piece, dp_mask, seq_mask = steps[step]
        return sent(
            kind, layer, last ^ dp_mask, other_x ^ (seq_mask // 2), piece, step, dp_mask, seq_mask
        )

    def climb(kind, layer, index, hop):
        region = pieces[kind][2].at[me ^ (layer * 2), group]
        return remote(
            region, region, hop_send.at[kind, index, 0], hop_recv.at[kind, index, 0],
            partner(2 << hop, 0),
        )

    def each_hop(kind, layer, action):
        for hop in range(bits - 1):
            @pl.when(layer < (1 << hop))
            def _():
                action(climb(kind, layer, layer | (1 << hop), hop))

    def begin(kind):
        for hop in range(bits - 1):
            climb(kind, 0, 1 << hop, hop).start()

    def spread(kind, layer):
        @pl.when(layer > 0)
        def _():
            climb(kind, layer, layer, 0).wait_recv()
            each_hop(kind, layer, lambda copy: copy.start())
            give(kind, layer, 1).start()
            give(kind, layer, 5).start()

        give(kind, layer, 2).start()
        give(kind, layer, 4).start()

    def relay(kind, layer):
        @pl.when(layer > 0)
        def _():
            take(kind, layer, 1).wait_recv()

        give(kind, layer, 3).start()
        take(kind, layer, 4).wait_recv()
        give(kind, layer, 6).start()

    def settle(kind, layer):
        take(kind, layer, 2).wait_recv()
        take(kind, layer, 3).wait_recv()
        take(kind, layer, 6).wait_recv()

        @pl.when(layer > 0)
        def _():
            take(kind, layer, 5).wait_recv()

    def drained(kind, layer):
        @pl.when(layer > 0)
        def _():
            give(kind, layer, 1).wait_send()
            give(kind, layer, 5).wait_send()

        for step in (2, 3, 4, 6):
            give(kind, layer, step).wait_send()
        each_hop(kind, layer, lambda copy: copy.wait_send())

    def over(action, kind, position):
        def body(index, carry):
            action(kind, position * quarter + index)
            return carry

        lax.fori_loop(0, quarter, body, 0)

    for copy in stores:
        copy.wait()
    for relative in range(1, 1 << bits):
        top = relative.bit_length() - 1
        for kind, block in enumerate(blocks(relative)):
            remote(
                block, block, send_sem.at[kind, relative], recv_sem.at[kind, relative],
                partner(masks[top], 0),
            ).wait_recv()
        forward(relative, top + 1)
        if relative == layers - 1:
            for kind in range(3):
                begin(kind)

    own_x.wait()
    to_pair.wait_recv()

    @pl.when(group == 1)
    def _():
        to_far.wait_recv()
        far_pair.start()
        far_pair.wait_recv()

    def halves(index, carry):
        here = pl.ds(pl.multiple_of(index * QB, QB), QB)

        @pl.when((group == 0) & (index < 2 * rows // QB))
        def _():
            x_both[here, :] = x_both[pl.ds(pl.multiple_of(index * QB + 2 * rows, QB), QB), :]

        high, low = split(x_both[here, :])
        x_high[here, :] = high
        x_low[here, :] = low
        return carry

    lax.fori_loop(0, 4 * rows // QB, halves, 0)
    own_w.wait()
    own_s.wait()
    count = 1 << bits
    shard = width // count
    for index in range(3):
        for slot in range(count):
            high, low = split(w_all[index, slot])
            w_high[index, pl.ds(slot * shard, shard), :] = high
            w_low[index, pl.ds(slot * shard, shard), :] = low
    bias = jnp.zeros((8, width), F32)
    blank = jnp.zeros((8, width - 128), F32)
    for slot in range(count):
        row = jnp.concatenate([s_all[slot, :8, :], blank], axis=1)
        bias = bias + (pltpu.roll(row, shard * slot, 1) if slot else row)
    bias = jnp.where(role == 0, bias[:2, :half], bias[:2, half:])

    def project(index, here):
        high, low = x_high[here, :], x_low[here, :]
        return (
            dot(high, w_high[index]) + dot(high, w_low[index]) + dot(low, w_high[index])
        )

    blocks_each = rows // QB

    def keys_values(index, carry):
        here = pl.ds(pl.multiple_of(index * QB, QB), QB)
        if blocks_each * 4 == 8:
            @pl.when(index < 4)
            def _():
                over(spread, 0, index)

            @pl.when(index >= 4)
            def _():
                over(spread, 1, index - 4)

        k_both[here, :] = project(1, here)
        v_both[here, :] = project(2, here) + bias[1:2]
        return carry

    lax.fori_loop(0, 8, keys_values, 0)

    def queries(index, carry):
        here = pl.ds(pl.multiple_of(index * QB, QB), QB)
        over(relay, 0, index)
        q_all[here, :] = project(0, pl.ds(pl.multiple_of(index * QB + 2 * rows, QB), QB)) + bias[:1]
        return carry

    lax.fori_loop(0, 4, queries, 0)

    for pair in range(half // 128):
        lanes = pl.ds(pair * 128, 128)
        for head in range(2):
            _, hh, ll = packs(q_all[:, lanes] * 0.125, head)
            q4[head, :, :128] = hh
            q4[head, :, 128:] = ll
            for start, key4, value2 in ((0, k4p, v2p), (2 * rows, k4s, v2s)):
                hl, _, _ = packs(k_both[pl.ds(start, 2 * rows), lanes], head)
                key4[head, :, :128] = hl
                key4[head, :, 128:] = hl
                value2[head] = packs(v_both[pl.ds(start, 2 * rows), lanes], head)[0]

        def attend(block, carry):
            if pair == 0:
                over(spread, 2, block)
                over(relay, 1, block)
            if pair == 1:
                over(relay, 2, block)
            here = pl.ds(pl.multiple_of(block * QB, QB), QB)
            seen = self_mask(lens_ref, block, 0)
            results = []
            for head in range(2):
                query = q4[head, here, :]
                far = dot_nt(query, k4p[head])
                near = jnp.where(seen, dot_nt(query, k4s[head, here, :]), MASKED)
                top = jnp.maximum(
                    jnp.max(far, axis=1, keepdims=True), jnp.max(near, axis=1, keepdims=True)
                )
                far = jnp.exp(far - top)
                near = jnp.exp(near - top)
                total = jnp.sum(far, axis=1, keepdims=True) + jnp.sum(near, axis=1, keepdims=True)
                far_h, far_l = split(far)
                near_h, near_l = split(near)
                out = dot(far_h, v2p[head]) + dot(far_l, v2p[head])
                value = v2s[head, here, :]
                out = out + dot(near_h, value) + dot(near_l, value)
                out = (out + pltpu.roll(out, HD, 1)) / total
                lse = top + jnp.log(total)
                lse_all[2 * pair + head, :, here] = jnp.transpose(
                    jnp.broadcast_to(lse, (QB, 128))
                )[:8]
                results.append(out)
            o_all[here, lanes] = jnp.where(lane_ids((QB, 128)) < HD, results[0], results[1])
            return carry

        lax.fori_loop(0, 4, attend, 0)

    def last(index, carry):
        for kind in range(3):
            settle(kind, index)
        return carry

    lax.fori_loop(0, layers, last, 0)
    part_count = count // 2
    swap = remote(
        out_all.at[pl.ds((1 - role) * part_count, part_count)], out_other, pair_sem.at[0],
        pair_sem.at[1], partner(0, 1),
    )
    swap.start()

    def ended(index, carry):
        for kind in range(3):
            drained(kind, index)
        return carry

    lax.fori_loop(0, layers, ended, 0)
    for copy in started:
        copy.wait_send()
    to_pair.wait_send()

    @pl.when(group == 0)
    def _():
        to_far.wait_send()

    @pl.when(group == 1)
    def _():
        far_pair.wait_send()

    swap.wait()


def run_forward(lens, weights, small, tokens, out_piece, up_piece, down_piece):
    bits = dp_bits()
    count = 1 << bits
    layers = count // 2
    anywhere = pl.BlockSpec(memory_space=pl.ANY)
    vmem = pl.BlockSpec(memory_space=pltpu.VMEM)
    three, shard, half = weights.shape
    rows, width = tokens.shape
    heads = half // HD
    shape = lambda *dims: jax.ShapeDtypeStruct(dims, F32)
    whole = lambda piece: shape(count, *piece.shape)
    return pl.pallas_call(
        functools.partial(forward_kernel, bits),
        in_specs=[pl.BlockSpec(memory_space=pltpu.SMEM)] + [anywhere] * 6,
        out_specs=[vmem] * 8 + [anywhere] * 4,
        out_shape=[
            shape(three, count, shard, half),
            shape(count, *small.shape),
            shape(4 * rows, width),
            shape(4 * rows, half),
            shape(4 * rows, half),
            shape(2 * rows, half),
            shape(2 * rows, half),
            shape(heads, 8, 2 * rows),
            whole(out_piece),
            whole(up_piece),
            whole(down_piece),
            shape(count // 2, *out_piece.shape),
        ],
        scratch_shapes=[
            pltpu.VMEM((4 * rows, width), BF),
            pltpu.VMEM((4 * rows, width), BF),
            pltpu.VMEM((three, width, half), BF),
            pltpu.VMEM((three, width, half), BF),
            pltpu.VMEM((2, 2 * rows, 256), BF),
            pltpu.VMEM((2, 2 * rows, 256), BF),
            pltpu.VMEM((2, 2 * rows, 256), BF),
            pltpu.VMEM((2, 2 * rows, 128), BF),
            pltpu.VMEM((2, 2 * rows, 128), BF),
            pltpu.VMEM(out_piece.shape, F32),
            pltpu.VMEM(up_piece.shape, F32),
            pltpu.VMEM(down_piece.shape, F32),
            pltpu.SemaphoreType.DMA((2, count)),
            pltpu.SemaphoreType.DMA((2, count)),
            pltpu.SemaphoreType.DMA((3,)),
            pltpu.SemaphoreType.DMA((3,)),
            pltpu.SemaphoreType.DMA((6,)),
            pltpu.SemaphoreType.DMA((3, layers, 7)),
            pltpu.SemaphoreType.DMA((3, layers, 7)),
            pltpu.SemaphoreType.DMA((2,)),
        ],
        compiler_params=pltpu.CompilerParams(
            collective_id=1, has_side_effects=True, vmem_limit_bytes=60 << 20
        ),
        name="gather_weights_and_attend",
    )(lens, weights, small, tokens, out_piece, up_piece, down_piece)


def backward_kernel(lens_ref, q_ref, kp_ref, vp_ref, ks_ref, vs_ref, o_ref, g_ref, lse_ref,
                    dq_ref, dkp_ref, dvp_ref, dks_ref, dvs_ref,
                    q4, k4p, k4s, v4p, v4s, g4, q2, g2, k2tp, k2ts, delta):
    rows = q_ref.shape[0]
    prod = jnp.transpose(o_ref[...] * g_ref[...])
    for head in range(2):
        hl, hh, ll = packs(q_ref[...] * 0.125, head)
        q2[head] = hl
        q4[head, :, :128] = hh
        q4[head, :, 128:] = ll
        hl, hh, ll = packs(g_ref[...], head)
        g2[head] = hl
        g4[head, :, :128] = hh
        g4[head, :, 128:] = ll
        for src, dst in ((kp_ref, k4p), (ks_ref, k4s), (vp_ref, v4p), (vs_ref, v4s)):
            hl, _, _ = packs(src[...], head)
            dst[head, :, :128] = hl
            dst[head, :, 128:] = hl
        for src, dst in ((kp_ref, k2tp), (ks_ref, k2ts)):
            flipped = jnp.transpose(src[...])[head * HD : head * HD + HD]
            high, low = high_low(flipped)
            dst[head, :HD] = high.astype(BF)
            dst[head, HD:] = low.astype(BF)
        delta[head] = jnp.broadcast_to(
            jnp.sum(prod[head * HD : head * HD + HD], axis=0, keepdims=True), (8, rows)
        )
    dkp_ref[...] = jnp.zeros_like(dkp_ref)
    dvp_ref[...] = jnp.zeros_like(dvp_ref)

    def step(block, carry):
        here = pl.ds(pl.multiple_of(block * QB, QB), QB)
        seen = self_mask(lens_ref, block, 1)
        keep = {}
        for head in range(2):
            query = q4[head, here, :]
            grad = g4[head, here, :]
            lse = lse_ref[head, :1, here]
            low = delta[head, :1, here]
            far = jnp.exp(dot_nt(k4p[head], query) - lse)
            near = jnp.exp(jnp.where(seen, dot_nt(k4s[head, here, :], query), MASKED) - lse)
            far_g = far * (dot_nt(v4p[head], grad) - low)
            near_g = near * (dot_nt(v4s[head, here, :], grad) - low)
            grad2 = g2[head, here, :]
            query2 = q2[head, here, :]
            ph, p_l = split(far)
            dvp = dot(ph, grad2) + dot(p_l, grad2)
            ph, p_l = split(near)
            dvs = dot(ph, grad2) + dot(p_l, grad2)
            sh, sl = split(far_g)
            dkp = dot(sh, query2) + dot(sl, query2)
            dq = dot(k2tp[head], sh) + dot(k2tp[head], sl)
            sh, sl = split(near_g)
            dks = dot(sh, query2) + dot(sl, query2)
            side = k2ts[head, :, here]
            dq = dq + dot(side, sh) + dot(side, sl)
            dq = dq[:HD] + dq[HD:]
            keep[head] = (
                dq,
                dkp + pltpu.roll(dkp, HD, 1),
                dvp + pltpu.roll(dvp, HD, 1),
                dks + pltpu.roll(dks, HD, 1),
                dvs + pltpu.roll(dvs, HD, 1),
            )
        left = lane_ids((QB, 128)) < HD
        far_left = lane_ids(dkp_ref.shape) < HD
        dq_ref[here, :] = jnp.transpose(
            jnp.concatenate([keep[0][0], keep[1][0]], axis=0)
        ) * 0.125
        dkp_ref[...] += jnp.where(far_left, keep[0][1], keep[1][1])
        dvp_ref[...] += jnp.where(far_left, keep[0][2], keep[1][2])
        dks_ref[here, :] = jnp.where(left, keep[0][3], keep[1][3])
        dvs_ref[here, :] = jnp.where(left, keep[0][4], keep[1][4])
        return carry

    lax.fori_loop(0, rows // QB, step, 0)


def attend_backward(lens, q, k_both, v_both, out, grad, lse):
    rows, width = q.shape
    heads = width // HD
    near = pl.BlockSpec((rows, 128), lambda j, lens: (0, j))
    group = pl.BlockSpec((rows, 128), lambda j, lens: (1, j))
    flops = heads * 2 * rows * (rows + QB) * (256 * 5)
    shape = jax.ShapeDtypeStruct((rows, width), F32)
    return pl.pallas_call(
        backward_kernel,
        grid_spec=pltpu.PrefetchScalarGridSpec(
            num_scalar_prefetch=1,
            grid=(heads // 2,),
            in_specs=[
                near, near, near, group, group, near, near,
                pl.BlockSpec((2, 8, rows), lambda j, lens: (j, 0, 0)),
            ],
            out_specs=[near] * 5,
            scratch_shapes=[
                pltpu.VMEM((2, rows, 256), BF),
                pltpu.VMEM((2, rows, 256), BF),
                pltpu.VMEM((2, rows, 256), BF),
                pltpu.VMEM((2, rows, 256), BF),
                pltpu.VMEM((2, rows, 256), BF),
                pltpu.VMEM((2, rows, 256), BF),
                pltpu.VMEM((2, rows, 128), BF),
                pltpu.VMEM((2, rows, 128), BF),
                pltpu.VMEM((2, 128, rows), BF),
                pltpu.VMEM((2, 128, rows), BF),
                pltpu.VMEM((2, 8, rows), F32),
            ],
        ),
        out_shape=[shape] * 5,
        compiler_params=pltpu.CompilerParams(vmem_limit_bytes=56 << 20),
        cost_estimate=pl.CostEstimate(
            flops=flops, bytes_accessed=12 * rows * width * 4, transcendentals=heads * rows * rows
        ),
        name="attention_backward",
    )(lens, q, k_both, v_both, k_both, v_both, out, grad, lse)


def norm_forward(resid, gain, shift):
    center = resid - jnp.mean(resid, axis=-1, keepdims=True)
    inverse = lax.rsqrt(jnp.mean(center * center, axis=-1, keepdims=True) + EPSILON)
    normed = center * inverse
    return normed * gain + shift, normed, inverse


def norm_backward(grad_out, normed, inverse, gain):
    grad_normed = grad_out * gain
    first_term = jnp.mean(grad_normed, axis=-1, keepdims=True)
    second_term = jnp.mean(grad_normed * normed, axis=-1, keepdims=True)
    grad_resid = inverse * (grad_normed - first_term - normed * second_term)
    return grad_resid, jnp.sum(grad_out * normed, axis=0), jnp.sum(grad_out, axis=0)


def on_device(
    hidden_in,
    teacher,
    lengths,
    qkv_weight,
    qkv_bias,
    out_weight,
    out_bias,
    ln_gain,
    ln_shift,
    ffn_in,
    ffn_in_bias,
    ffn_out,
):
    _, rows, width = hidden_in.shape
    dp_count = lax.axis_size("dp")
    dp_index = lax.axis_index("dp")
    seq_index = lax.axis_index("seq")
    group, role = seq_index // 2, seq_index % 2
    total_tokens = dp_count * rows * SEQ
    shard = qkv_weight.shape[1]
    half = width // 2
    ffn = ffn_in.shape[1]
    ffn_shard = ffn // dp_count
    ffn_half = ffn_shard // 2

    x_own = hidden_in.reshape(rows, width)
    target = teacher.reshape(rows, width)
    lens = lengths.reshape(CONT)

    length_sum = jnp.sum(lens).astype(F32)
    lanes = lambda value: jnp.pad(value, ((0, 0), (0, 128 - value.shape[1])))
    up_rows = -(-ffn_shard // 128)
    up_bias = jnp.pad(ffn_in_bias, (0, up_rows * 128 - ffn_shard)).reshape(up_rows, 128)
    small_rows = -(-(9 + up_rows) // 8) * 8
    small = jnp.concatenate(
        [
            lanes(qkv_bias),
            lanes(out_bias),
            lanes(ln_gain),
            lanes(ln_shift),
            up_bias,
            jnp.full((small_rows - 8 - up_rows, 128), length_sum, F32),
        ]
    )
    local_lens = jnp.where(role == 0, lens, jnp.roll(lens, CONT // 2))
    local_lens = jnp.where(group == 0, 0, local_lens)
    out_half = shard // 2
    up_piece = pick(ffn_in.reshape(shard, dp_count, 2, ffn_half), role, 2)
    out_piece = pick(out_weight.reshape(2, out_half, width), role, 0)
    down_piece = pick(ffn_out.reshape(2, ffn_half, width), role, 0)
    (w_qkv, small, x_both, k_both, v_both, queries, attended, lse,
     out_blocks, w_up, w_down, out_other) = run_forward(
        local_lens,
        lax.dynamic_slice_in_dim(qkv_weight, role * half, half, 2),
        small,
        x_own,
        out_piece.reshape(2, 3, out_half // 6, width),
        up_piece.reshape(2, 3, shard // 6, ffn // 2),
        down_piece.reshape(2, 3, ffn_half // 6, width),
    )
    w_up = w_up.reshape(width, ffn // 2)
    w_down = w_down.reshape(ffn // 2, width)
    w_qkv = w_qkv.reshape(3, width, half)
    w_q, w_k, w_v = w_qkv[0], w_qkv[1], w_qkv[2]
    out_mine = pick(out_blocks.reshape(2, dp_count // 2, out_half, width), role, 0)
    out_other = out_other.reshape(dp_count // 2, out_half, width)
    w_out = ordered(role, out_mine[:, None], out_other[:, None], 1).reshape(half, width)
    vectors = small[:, :8, :shard].transpose(1, 0, 2).reshape(4, 2, width)
    b_out, gains, shifts = vectors[1], vectors[2], vectors[3]
    b_up = small[:, 8 : 8 + up_rows].reshape(dp_count, up_rows * 128)[:, :ffn_shard]
    b_up = pick(b_up.reshape(dp_count, 2, ffn_half), role, 1).reshape(ffn // 2)
    count = float(dp_count * PROMPT) + jnp.sum(small[:, small_rows - 1, 0])
    x_prompt, x_group = x_both[: 2 * rows], x_both[2 * rows :]

    def reduce_pair(partial):
        return partial[:rows] + swap_pair(partial[rows:])

    def both_halves(own):
        return jnp.concatenate([own, swap_pair(own)], axis=0)

    first_resid = x_own + reduce_pair(mm(attended, w_out)) + b_out[0]
    first_norm, first_hat, first_inv = norm_forward(first_resid, gains[0], shifts[0])
    norm_group = both_halves(first_norm)
    pre_act = mm(norm_group, w_up) + b_up
    normal_cdf = 0.5 * (1.0 + lax.erf(pre_act * INV_ROOT_TWO))
    activated = pre_act * normal_cdf
    slope = normal_cdf + pre_act * jnp.exp(-0.5 * pre_act * pre_act) * INV_ROOT_TAU
    second_resid = first_norm + reduce_pair(mm(activated, w_down)) + b_out[1]
    final, second_hat, second_inv = norm_forward(second_resid, gains[1], shifts[1])

    slot = seq_index * rows + jnp.arange(rows, dtype=jnp.int32) - PROMPT
    own_len = jnp.sum(
        jnp.where((slot // CLEN)[None] == jnp.arange(CONT, dtype=jnp.int32)[:, None], lens[:, None], 0),
        axis=0,
    )
    valid = ((slot < 0) | (slot % CLEN < own_len)).astype(F32)
    difference = (final - target) * valid[:, None]
    squares = jnp.sum(difference * difference)
    grad_final = difference * (total_tokens / count)
    grad_second, grad_gain_two, grad_shift_two = norm_backward(
        grad_final, second_hat, second_inv, gains[1]
    )
    grad_bias_down = jnp.sum(grad_second, axis=0)
    second_group = both_halves(grad_second)
    grad_w_down = mm_tn(activated, second_group)
    grad_pre = mm_nt(second_group, w_down) * slope
    grad_b_up = jnp.sum(grad_pre, axis=0)
    grad_w_up = mm_tn(norm_group, grad_pre)
    share_down = scatter_rows(grad_w_down)
    share_up = scatter_rows(grad_w_up)
    grad_first_norm = grad_second + reduce_pair(mm_nt(grad_pre, w_up))
    grad_first, grad_gain_one, grad_shift_one = norm_backward(
        grad_first_norm, first_hat, first_inv, gains[0]
    )
    grad_bias_out = jnp.sum(grad_first, axis=0)
    first_group = both_halves(grad_first)
    grad_attended = mm_nt(first_group, w_out)
    grad_w_out = mm_tn(attended, first_group)
    mine = grad_w_out.reshape(dp_count // 2, 2, out_half, width)
    received = swap_pair(pick(mine, 1 - role, 1))
    mine = ordered(role, pick(mine, role, 1), received, 0)
    d_q, d_kp, d_vp, d_ks, d_vs = attend_backward(
        local_lens, queries, k_both, v_both, attended, grad_attended, lse
    )
    on_prompt = mm_nt(d_kp, w_k) + mm_nt(d_vp, w_v)
    on_prompt = reduce_pair(on_prompt)
    from_cont = lax.ppermute(on_prompt, "seq", [(2, 0), (3, 1)])
    grad_w_k = mm_tn(x_both, jnp.concatenate([d_kp, d_ks], axis=0))
    grad_w_v = mm_tn(x_both, jnp.concatenate([d_vp, d_vs], axis=0))
    grad_w_q = mm_tn(x_group, d_q)
    on_own = reduce_pair(mm_nt(d_q, w_q) + mm_nt(d_ks, w_k) + mm_nt(d_vs, w_v))
    grad_input = grad_first + on_own + jnp.where(group == 0, on_prompt + from_cont, 0.0)

    def spread(value):
        blank = jnp.zeros((width,), F32)
        return lax.dynamic_update_slice(blank, value, (role * half,))

    vectors = jnp.stack(
        [
            spread(jnp.sum(d_q, axis=0)),
            spread(jnp.sum(d_vp, axis=0) + jnp.sum(d_vs, axis=0)),
            grad_bias_out,
            grad_bias_down,
            grad_gain_one,
            grad_gain_two,
            grad_shift_one,
            grad_shift_two,
        ]
    )
    vectors = vectors.reshape(8, dp_count, shard).transpose(1, 0, 2).reshape(dp_count, 8 * shard)
    up = jnp.zeros((dp_count, 2, ffn_half), F32)
    up = lax.dynamic_update_slice(up, grad_b_up.reshape(dp_count, 1, ffn_half), (0, role, 0))
    used = 8 * shard + ffn_shard
    small_rows = -(-(used + 1) // 1024) * 8
    small = jnp.concatenate(
        [
            vectors,
            up.reshape(dp_count, ffn_shard),
            jnp.full((dp_count, small_rows * 128 - used), squares, F32),
        ],
        axis=1,
    ).reshape(dp_count, small_rows, 128)
    share_qkv, share_out, small, other_qkv, other_out = scatter_all(
        jnp.stack([grad_w_q, grad_w_k, grad_w_v]).reshape(3, dp_count, shard, half),
        mine.reshape(dp_count, out_half, width),
        small,
    )
    small = small.reshape(small_rows * 128)
    pairs = small[: 8 * shard].reshape(4, 2, shard)
    loss = small[used] / (count * width)

    def join(share, axis):
        return ordered(role, share, swap_pair(share), axis)

    out_qkv = ordered(role, share_qkv, other_qkv, 2)
    out_out = ordered(role, share_out, other_out, 0)
    out_up = join(share_up.reshape(shard, dp_count, 1, ffn_half), 2).reshape(shard, ffn)
    out_down = join(share_down.reshape(ffn_half, width), 0)
    return (
        final[None],
        grad_input[None],
        out_qkv,
        pairs[0],
        out_out,
        pairs[1],
        pairs[2],
        pairs[3],
        out_up,
        small[8 * shard : used],
        out_down,
        loss,
    )


def solution(mesh):
    return jax.shard_map(
        on_device,
        mesh=mesh,
        in_specs=(
            P("dp", "seq", None),
            P("dp", "seq", None),
            P("dp", None),
            P(None, "dp", None),
            P(None, "dp"),
            P("dp", None),
            P(None, "dp"),
            P(None, "dp"),
            P(None, "dp"),
            P("dp", None),
            P("dp"),
            P("dp", None),
        ),
        out_specs=(
            P("dp", "seq", None),
            P("dp", "seq", None),
            P(None, "dp", None),
            P(None, "dp"),
            P("dp", None),
            P(None, "dp"),
            P(None, "dp"),
            P(None, "dp"),
            P("dp", None),
            P("dp"),
            P("dp", None),
            P(),
        ),
        check_vma=False,
    )
```

```python
import functools

import jax
import jax.numpy as jnp
from jax import lax
from jax.experimental import pallas as pl
from jax.experimental.pallas import tpu as pltpu
from jax.sharding import PartitionSpec as P

HD = 64
PROMPT = 1024
CONT = 8
CLEN = 128
SEQ = 4
QB = 256

HIGH = lax.Precision.HIGH
EPSILON = 1e-05
MASKED = -1e30
INV_ROOT_TWO = 0.7071067811865476
INV_ROOT_TAU = 0.3989422804014327
BF = jnp.bfloat16
F32 = jnp.float32


def mm(left, right):
    return lax.dot_general(
        left, right, (((1,), (0,)), ((), ())), precision=HIGH, preferred_element_type=F32
    )


def mm_nt(left, right):
    return lax.dot_general(
        left, right, (((1,), (1,)), ((), ())), precision=HIGH, preferred_element_type=F32
    )


def mm_tn(left, right):
    return lax.dot_general(
        left, right, (((0,), (0,)), ((), ())), precision=HIGH, preferred_element_type=F32
    )


def swap_pair(value):
    return lax.ppermute(value, "seq", [(i, i ^ 1) for i in range(SEQ)])


def swap_group(value):
    return lax.ppermute(value, "seq", [(i, i ^ 2) for i in range(SEQ)])


def swap_dp(value, bit):
    count = lax.axis_size("dp")
    return lax.ppermute(value, "dp", [(i, i ^ (1 << bit)) for i in range(count)])


def ordered(bit, own, other, axis):
    first = jnp.where(bit == 0, own, other)
    second = jnp.where(bit == 0, other, own)
    return jnp.concatenate([first, second], axis=axis)


def pick(value, index, axis):
    return lax.dynamic_index_in_dim(value, index, axis, keepdims=False)


def dp_bits():
    return lax.axis_size("dp").bit_length() - 1


def gather_rows(piece, axis=0):
    return lax.all_gather(piece, "dp", axis=axis, tiled=True)


def scatter_rows(grads, axis=0):
    share = lax.psum_scatter(grads, "dp", scatter_dimension=axis, tiled=True)
    return share + swap_group(share)


def partner(dp_mask, seq_mask):
    return (lax.axis_index("dp") ^ dp_mask, lax.axis_index("seq") ^ seq_mask)


def remote(src, dst, send_sem, recv_sem, target):
    return pltpu.make_async_remote_copy(
        src_ref=src,
        dst_ref=dst,
        send_sem=send_sem,
        recv_sem=recv_sem,
        device_id=target,
        device_id_type=pl.DeviceIdType.MESH,
    )


def greet(bits):
    barrier = pltpu.get_barrier_semaphore()
    others = [partner(1 << bit, 0) for bit in range(bits)] + [partner(0, 1), partner(0, 2)]
    for other in others:
        pl.semaphore_signal(
            barrier, inc=1, device_id=other, device_id_type=pl.DeviceIdType.MESH
        )
    pl.semaphore_wait(barrier, len(others))


def hop_masks(bits):
    return [1 << bit for bit in range(1, bits)] + [1]


def slot_mask(bits, relative):
    masks = hop_masks(bits)
    return sum(masks[p] for p in range(bits) if relative >> p & 1)


def scatter_kernel(bits, *refs):
    kinds = 3
    grads, refs = refs[:kinds], refs[kinds:]
    mine, refs = refs[:kinds], refs[kinds:]
    other, refs = refs[: kinds - 1], refs[kinds - 1 :]
    acc, refs = refs[:kinds], refs[kinds:]
    hop_in, refs = refs[:kinds], refs[kinds:]
    x_in, refs = refs[:kinds], refs[kinds:]
    pair_in, send_sem, recv_sem, x_send, x_recv, load_sem, store_sem = refs
    me = lax.axis_index("dp")
    masks = hop_masks(bits)
    count = 1 << bits

    def source(kind, relative):
        slot = me ^ slot_mask(bits, relative)
        return grads[kind].at[:, slot] if kind == 0 else grads[kind].at[slot]

    def hop_copy(kind, relative, hop, from_input):
        index = relative ^ (1 << hop)
        src = source(kind, relative) if from_input else acc[kind].at[relative]
        place = (1 << hop) + index
        return remote(
            src, hop_in[kind].at[place], send_sem.at[kind, relative], recv_sem.at[kind, place],
            partner(masks[hop], 0),
        )

    loads = {}
    for relative in reversed(range(count // 2)):
        for kind in range(kinds):
            copy = pltpu.make_async_copy(
                source(kind, relative), acc[kind].at[relative], load_sem.at[kind, relative]
            )
            copy.start()
            loads[kind, relative] = copy
    greet(bits)
    started = []
    last = bits - 1
    for relative in reversed(range(count // 2, count)):
        for kind in range(kinds):
            copy = hop_copy(kind, relative, last, True)
            copy.start()
            started.append(copy)
    for relative in reversed(range(count // 2)):
        for kind in range(kinds):
            loads[kind, relative].wait()
        lowest = relative.bit_length() - 1
        for hop in reversed(range(max(lowest + 1, 0), bits)):
            for kind in range(kinds):
                hop_copy(kind, relative | (1 << hop), hop, hop == last).wait_recv()
                acc[kind][relative] += hop_in[kind][(1 << hop) + relative]
        if relative:
            for kind in range(kinds):
                copy = hop_copy(kind, relative, lowest, False)
                copy.start()
                started.append(copy)
    crossing = []
    for kind in range(kinds):
        copy = remote(acc[kind].at[0], x_in[kind], x_send.at[kind], x_recv.at[kind], partner(0, 2))
        copy.start()
        crossing.append(copy)
    for kind in range(kinds):
        crossing[kind].wait_recv()
        mine[kind][...] = acc[kind][0] + x_in[kind][...]
    handing = []
    for kind in range(kinds - 1):
        copy = remote(
            mine[kind], other[kind], x_send.at[kinds + kind], x_recv.at[kinds + kind], partner(0, 1)
        )
        copy.start()
        handing.append(copy)
    copy = remote(
        mine[kinds - 1], pair_in, x_send.at[2 * kinds - 1], x_recv.at[2 * kinds - 1], partner(0, 1)
    )
    copy.start()
    handing.append(copy)
    for copy in handing:
        copy.wait()
    mine[kinds - 1][...] += pair_in[...]
    for copy in started + crossing:
        copy.wait_send()


def scatter_all(qkv, out, small):
    bits = dp_bits()
    count = 1 << bits
    any_spec = pl.BlockSpec(memory_space=pl.ANY)
    vmem = pl.BlockSpec(memory_space=pltpu.VMEM)
    shapes = [(qkv.shape[0],) + qkv.shape[2:], out.shape[1:], small.shape[1:]]
    like = [jax.ShapeDtypeStruct(shape, F32) for shape in shapes]
    return pl.pallas_call(
        functools.partial(scatter_kernel, bits),
        in_specs=[any_spec] * 3,
        out_specs=[vmem] * 5,
        out_shape=like + like[:2],
        scratch_shapes=[pltpu.VMEM((count // 2,) + shape, F32) for shape in shapes]
        + [pltpu.VMEM((count,) + shape, F32) for shape in shapes]
        + [pltpu.VMEM(shape, F32) for shape in shapes]
        + [
            pltpu.VMEM(shapes[2], F32),
            pltpu.SemaphoreType.DMA((3, count)),
            pltpu.SemaphoreType.DMA((3, count)),
            pltpu.SemaphoreType.DMA((6,)),
            pltpu.SemaphoreType.DMA((6,)),
            pltpu.SemaphoreType.DMA((3, count // 2)),
            pltpu.SemaphoreType.DMA((1,)),
        ],
        compiler_params=pltpu.CompilerParams(
            collective_id=2, has_side_effects=True, vmem_limit_bytes=40 << 20
        ),
        cost_estimate=pl.CostEstimate(
            flops=0, bytes_accessed=(qkv.size + out.size) * 4 * 12, transcendentals=0
        ),
        name="scatter_attention_grads",
    )(qkv, out, small)


def lane_ids(shape):
    return lax.broadcasted_iota(jnp.int32, shape, 1)


def high_low(value):
    high = value.astype(BF).astype(F32)
    return high, value - high


def packs(value, head):
    high, low = high_low(value)
    left = lane_ids(value.shape) < HD
    high_r = pltpu.roll(high, HD, 1)
    low_r = pltpu.roll(low, HD, 1)
    if head == 0:
        return (
            jnp.where(left, high, low_r).astype(BF),
            jnp.where(left, high, high_r).astype(BF),
            jnp.where(left, low, low_r).astype(BF),
        )
    return (
        jnp.where(left, high_r, low).astype(BF),
        jnp.where(left, high_r, high).astype(BF),
        jnp.where(left, low_r, low).astype(BF),
    )


def dot(left, right):
    return lax.dot_general(left, right, (((1,), (0,)), ((), ())), preferred_element_type=F32)


def dot_nt(left, right):
    return lax.dot_general(left, right, (((1,), (1,)), ((), ())), preferred_element_type=F32)


def split(value):
    high = value.astype(BF)
    return high, (value - high.astype(F32)).astype(BF)


def self_mask(lens_ref, block, query_axis):
    key_axis = 1 - query_axis
    query = lax.broadcasted_iota(jnp.int32, (QB, QB), query_axis)
    key = lax.broadcasted_iota(jnp.int32, (QB, QB), key_axis)
    per = QB // CLEN
    seen = jnp.zeros((QB, QB), jnp.bool_)
    for piece in range(per):
        low = piece * CLEN
        limit = low + lens_ref[block * per + piece]
        inside = (query >= low) & (query < low + CLEN) & (key >= low) & (key < limit)
        seen = seen | inside
    return seen & (key <= query)


THIRDS = ((0, 1), (1, 2))


def forward_kernel(bits, lens_ref, w_ref, s_ref, x_ref, out_ref, up_ref, down_ref,
                   w_high, w_low, s_all, xt_high, xt_low, k_both, v_both, q_all, o_all, lse_all,
                   out_all, up_all, down_all, out_other,
                   w_all, x_both, x_high, x_low, q4, k4p, k4s, v2p, v2s,
                   out_buf, up_buf, down_buf,
                   send_sem, recv_sem, x_send, x_recv, own_sem, hop_send, hop_recv, pair_sem):
    me = lax.axis_index("dp")
    seq = lax.axis_index("seq")
    group, role = seq // 2, seq % 2
    masks = hop_masks(bits)
    rows, width = x_ref.shape
    half = w_ref.shape[2]
    layers = 1 << (bits - 1)
    quarter = layers // 4
    greet(bits)

    pieces = ((out_ref, out_buf, out_all), (up_ref, up_buf, up_all), (down_ref, down_buf, down_all))
    loads = [pltpu.make_async_copy(src, buf, own_sem.at[i]) for i, (src, buf, _) in enumerate(pieces)]
    own_w = pltpu.make_async_copy(w_ref, w_all.at[:, me], own_sem.at[3])
    own_s = pltpu.make_async_copy(s_ref, s_all.at[me], own_sem.at[4])
    own_x = pltpu.make_async_copy(x_ref, x_both.at[pl.ds(2 * rows, rows)], own_sem.at[5])
    for copy in loads + [own_w, own_s, own_x]:
        copy.start()
    to_pair = remote(
        x_ref, x_both.at[pl.ds(3 * rows, rows)], x_send.at[0], x_recv.at[0], partner(0, 1)
    )
    to_far = remote(x_ref, x_both.at[pl.ds(0, rows)], x_send.at[1], x_recv.at[1], partner(0, 2))
    far_pair = remote(
        x_both.at[pl.ds(0, rows)], x_both.at[pl.ds(rows, rows)], x_send.at[2], x_recv.at[2],
        partner(0, 1),
    )
    to_pair.start()

    @pl.when(group == 0)
    def _():
        to_far.start()

    def blocks(relative):
        slot = me ^ slot_mask(bits, relative)
        return w_all.at[:, slot], s_all.at[slot]

    started = []

    def forward(relative, first_hop):
        for hop in range(first_hop, bits):
            index = relative | (1 << hop)
            for kind, block in enumerate(blocks(relative)):
                source = block if relative else (w_ref, s_ref)[kind]
                copy = remote(
                    source, block, send_sem.at[kind, index], recv_sem.at[kind, index],
                    partner(masks[hop], 0),
                )
                copy.start()
                started.append(copy)

    forward(0, 0)
    for copy in loads:
        copy.wait()
    stores = [pltpu.make_async_copy(buf, dst.at[me], own_sem.at[i]) for i, (_, buf, dst) in enumerate(pieces)]
    for copy in stores:
        copy.start()

    def part(kind, layer, last, other_x, piece):
        slot = me ^ (layer * 2) ^ last
        first, count = THIRDS[piece]
        return pieces[kind][2].at[slot, group ^ other_x, pl.ds(first, count)]

    def sent(kind, layer, last, other_x, piece, step, dp_mask, seq_mask):
        region = part(kind, layer, last, other_x, piece)
        return remote(
            region, region, hop_send.at[kind, layer, step], hop_recv.at[kind, layer, step],
            partner(dp_mask, seq_mask),
        )

    steps = {
        1: (0, 0, 0, 0, 2),
        2: (0, 0, 0, 1, 0),
        3: (0, 1, 0, 1, 0),
        4: (0, 0, 1, 1, 0),
        5: (0, 0, 1, 0, 2),
        6: (1, 0, 1, 0, 2),
    }

    def give(kind, layer, step):
        last, other_x, piece, dp_mask, seq_mask = steps[step]
        return sent(kind, layer, last, other_x, piece, step, dp_mask, seq_mask)

    def take(kind, layer, step):
        last, other_x, piece, dp_mask, seq_mask = steps[step]
        return sent(
            kind, layer, last ^ dp_mask, other_x ^ (seq_mask // 2), piece, step, dp_mask, seq_mask
        )

    def climb(kind, layer, index, hop):
        region = pieces[kind][2].at[me ^ (layer * 2), group]
        return remote(
            region, region, hop_send.at[kind, index, 0], hop_recv.at[kind, index, 0],
            partner(2 << hop, 0),
        )

    def each_hop(kind, layer, action):
        for hop in range(bits - 1):
            @pl.when(layer < (1 << hop))
            def _():
                action(climb(kind, layer, layer | (1 << hop), hop))

    def begin(kind):
        for hop in range(bits - 1):
            climb(kind, 0, 1 << hop, hop).start()

    def spread(kind, layer):
        @pl.when(layer > 0)
        def _():
            climb(kind, layer, layer, 0).wait_recv()
            each_hop(kind, layer, lambda copy: copy.start())
            give(kind, layer, 1).start()
            give(kind, layer, 5).start()

        give(kind, layer, 2).start()
        give(kind, layer, 4).start()

    def relay(kind, layer):
        @pl.when(layer > 0)
        def _():
            take(kind, layer, 1).wait_recv()

        give(kind, layer, 3).start()
        take(kind, layer, 4).wait_recv()
        give(kind, layer, 6).start()

    def settle(kind, layer):
        take(kind, layer, 2).wait_recv()
        take(kind, layer, 3).wait_recv()
        take(kind, layer, 6).wait_recv()

        @pl.when(layer > 0)
        def _():
            take(kind, layer, 5).wait_recv()

    def drained(kind, layer):
        @pl.when(layer > 0)
        def _():
            give(kind, layer, 1).wait_send()
            give(kind, layer, 5).wait_send()

        for step in (2, 3, 4, 6):
            give(kind, layer, step).wait_send()
        each_hop(kind, layer, lambda copy: copy.wait_send())

    def over(action, kind, position):
        def body(index, carry):
            action(kind, position * quarter + index)
            return carry

        lax.fori_loop(0, quarter, body, 0)

    for copy in stores:
        copy.wait()
    for relative in range(1, 1 << bits):
        top = relative.bit_length() - 1
        for kind, block in enumerate(blocks(relative)):
            remote(
                block, block, send_sem.at[kind, relative], recv_sem.at[kind, relative],
                partner(masks[top], 0),
            ).wait_recv()
        forward(relative, top + 1)
        if relative == layers - 1:
            for kind in range(3):
                begin(kind)

    own_x.wait()
    to_pair.wait_recv()

    @pl.when(group == 1)
    def _():
        to_far.wait_recv()
        far_pair.start()
        far_pair.wait_recv()

    def halves(index, carry):
        here = pl.ds(pl.multiple_of(index * QB, QB), QB)

        @pl.when((group == 0) & (index < 2 * rows // QB))
        def _():
            x_both[here, :] = x_both[pl.ds(pl.multiple_of(index * QB + 2 * rows, QB), QB), :]

        high, low = split(x_both[here, :])
        x_high[here, :] = high
        x_low[here, :] = low
        high, low = split(jnp.transpose(x_both[here, :]))
        xt_high[:, here] = high
        xt_low[:, here] = low
        return carry

    lax.fori_loop(0, 4 * rows // QB, halves, 0)
    own_w.wait()
    own_s.wait()
    count = 1 << bits
    shard = width // count
    for index in range(3):
        for slot in range(count):
            high, low = split(w_all[index, slot])
            w_high[index, pl.ds(slot * shard, shard), :] = high
            w_low[index, pl.ds(slot * shard, shard), :] = low
    bias = jnp.zeros((8, width), F32)
    blank = jnp.zeros((8, width - 128), F32)
    for slot in range(count):
        row = jnp.concatenate([s_all[slot, :8, :], blank], axis=1)
        bias = bias + (pltpu.roll(row, shard * slot, 1) if slot else row)
    bias = jnp.where(role == 0, bias[:2, :half], bias[:2, half:])

    def project(index, here):
        high, low = x_high[here, :], x_low[here, :]
        return (
            dot(high, w_high[index]) + dot(high, w_low[index]) + dot(low, w_high[index])
        )

    blocks_each = rows // QB

    def keys_values(index, carry):
        here = pl.ds(pl.multiple_of(index * QB, QB), QB)
        if blocks_each * 4 == 8:
            @pl.when(index < 4)
            def _():
                over(spread, 0, index)

            @pl.when(index >= 4)
            def _():
                over(spread, 1, index - 4)

        k_both[here, :] = project(1, here)
        v_both[here, :] = project(2, here) + bias[1:2]
        return carry

    lax.fori_loop(0, 8, keys_values, 0)

    def queries(index, carry):
        here = pl.ds(pl.multiple_of(index * QB, QB), QB)
        over(relay, 0, index)
        q_all[here, :] = project(0, pl.ds(pl.multiple_of(index * QB + 2 * rows, QB), QB)) + bias[:1]
        return carry

    lax.fori_loop(0, 4, queries, 0)

    for pair in range(half // 128):
        lanes = pl.ds(pair * 128, 128)
        for head in range(2):
            _, hh, ll = packs(q_all[:, lanes] * 0.125, head)
            q4[head, :, :128] = hh
            q4[head, :, 128:] = ll
            for start, key4, value2 in ((0, k4p, v2p), (2 * rows, k4s, v2s)):
                hl, _, _ = packs(k_both[pl.ds(start, 2 * rows), lanes], head)
                key4[head, :, :128] = hl
                key4[head, :, 128:] = hl
                value2[head] = packs(v_both[pl.ds(start, 2 * rows), lanes], head)[0]

        def attend(block, carry):
            if pair == 0:
                over(spread, 2, block)
                over(relay, 1, block)
            if pair == 1:
                over(relay, 2, block)
            here = pl.ds(pl.multiple_of(block * QB, QB), QB)
            seen = self_mask(lens_ref, block, 0)
            results = []
            for head in range(2):
                query = q4[head, here, :]
                far = dot_nt(query, k4p[head])
                near = jnp.where(seen, dot_nt(query, k4s[head, here, :]), MASKED)
                top = jnp.maximum(
                    jnp.max(far, axis=1, keepdims=True), jnp.max(near, axis=1, keepdims=True)
                )
                far = jnp.exp(far - top)
                near = jnp.exp(near - top)
                total = jnp.sum(far, axis=1, keepdims=True) + jnp.sum(near, axis=1, keepdims=True)
                far_h, far_l = split(far)
                near_h, near_l = split(near)
                out = dot(far_h, v2p[head]) + dot(far_l, v2p[head])
                value = v2s[head, here, :]
                out = out + dot(near_h, value) + dot(near_l, value)
                out = (out + pltpu.roll(out, HD, 1)) / total
                lse = top + jnp.log(total)
                lse_all[2 * pair + head, :, here] = jnp.transpose(
                    jnp.broadcast_to(lse, (QB, 128))
                )[:8]
                results.append(out)
            o_all[here, lanes] = jnp.where(lane_ids((QB, 128)) < HD, results[0], results[1])
            return carry

        lax.fori_loop(0, 4, attend, 0)

    def last(index, carry):
        for kind in range(3):
            settle(kind, index)
        return carry

    lax.fori_loop(0, layers, last, 0)
    part_count = count // 2
    swap = remote(
        out_all.at[pl.ds((1 - role) * part_count, part_count)], out_other, pair_sem.at[0],
        pair_sem.at[1], partner(0, 1),
    )
    swap.start()

    def ended(index, carry):
        for kind in range(3):
            drained(kind, index)
        return carry

    lax.fori_loop(0, layers, ended, 0)
    for copy in started:
        copy.wait_send()
    to_pair.wait_send()

    @pl.when(group == 0)
    def _():
        to_far.wait_send()

    @pl.when(group == 1)
    def _():
        far_pair.wait_send()

    swap.wait()


def run_forward(lens, weights, small, tokens, out_piece, up_piece, down_piece):
    bits = dp_bits()
    count = 1 << bits
    layers = count // 2
    anywhere = pl.BlockSpec(memory_space=pl.ANY)
    vmem = pl.BlockSpec(memory_space=pltpu.VMEM)
    three, shard, half = weights.shape
    rows, width = tokens.shape
    heads = half // HD
    shape = lambda *dims: jax.ShapeDtypeStruct(dims, F32)
    whole = lambda piece: shape(count, *piece.shape)
    return pl.pallas_call(
        functools.partial(forward_kernel, bits),
        in_specs=[pl.BlockSpec(memory_space=pltpu.SMEM)] + [anywhere] * 6,
        out_specs=[vmem] * 10 + [anywhere] * 4,
        out_shape=[
            jax.ShapeDtypeStruct((three, width, half), BF),
            jax.ShapeDtypeStruct((three, width, half), BF),
            shape(count, *small.shape),
            jax.ShapeDtypeStruct((width, 4 * rows), BF),
            jax.ShapeDtypeStruct((width, 4 * rows), BF),
            shape(4 * rows, half),
            shape(4 * rows, half),
            shape(2 * rows, half),
            shape(2 * rows, half),
            shape(heads, 8, 2 * rows),
            whole(out_piece),
            whole(up_piece),
            whole(down_piece),
            shape(count // 2, *out_piece.shape),
        ],
        scratch_shapes=[
            pltpu.VMEM((three, count, shard, half), F32),
            pltpu.VMEM((4 * rows, width), F32),
            pltpu.VMEM((4 * rows, width), BF),
            pltpu.VMEM((4 * rows, width), BF),
            pltpu.VMEM((2, 2 * rows, 256), BF),
            pltpu.VMEM((2, 2 * rows, 256), BF),
            pltpu.VMEM((2, 2 * rows, 256), BF),
            pltpu.VMEM((2, 2 * rows, 128), BF),
            pltpu.VMEM((2, 2 * rows, 128), BF),
            pltpu.VMEM(out_piece.shape, F32),
            pltpu.VMEM(up_piece.shape, F32),
            pltpu.VMEM(down_piece.shape, F32),
            pltpu.SemaphoreType.DMA((2, count)),
            pltpu.SemaphoreType.DMA((2, count)),
            pltpu.SemaphoreType.DMA((3,)),
            pltpu.SemaphoreType.DMA((3,)),
            pltpu.SemaphoreType.DMA((6,)),
            pltpu.SemaphoreType.DMA((3, layers, 7)),
            pltpu.SemaphoreType.DMA((3, layers, 7)),
            pltpu.SemaphoreType.DMA((2,)),
        ],
        compiler_params=pltpu.CompilerParams(
            collective_id=1, has_side_effects=True, vmem_limit_bytes=60 << 20
        ),
        name="gather_weights_and_attend",
    )(lens, weights, small, tokens, out_piece, up_piece, down_piece)


def backward_kernel(lens_ref, q_ref, kp_ref, vp_ref, ks_ref, vs_ref, o_ref, g_ref, lse_ref,
                    dq_ref, dkp_ref, dvp_ref, dks_ref, dvs_ref,
                    q4, k4p, k4s, v4p, v4s, g4, q2, g2, k2tp, k2ts, delta):
    rows = q_ref.shape[0]
    prod = jnp.transpose(o_ref[...] * g_ref[...])
    for head in range(2):
        hl, hh, ll = packs(q_ref[...] * 0.125, head)
        q2[head] = hl
        q4[head, :, :128] = hh
        q4[head, :, 128:] = ll
        hl, hh, ll = packs(g_ref[...], head)
        g2[head] = hl
        g4[head, :, :128] = hh
        g4[head, :, 128:] = ll
        for src, dst in ((kp_ref, k4p), (ks_ref, k4s), (vp_ref, v4p), (vs_ref, v4s)):
            hl, _, _ = packs(src[...], head)
            dst[head, :, :128] = hl
            dst[head, :, 128:] = hl
        for src, dst in ((kp_ref, k2tp), (ks_ref, k2ts)):
            flipped = jnp.transpose(src[...])[head * HD : head * HD + HD]
            high, low = high_low(flipped)
            dst[head, :HD] = high.astype(BF)
            dst[head, HD:] = low.astype(BF)
        delta[head] = jnp.broadcast_to(
            jnp.sum(prod[head * HD : head * HD + HD], axis=0, keepdims=True), (8, rows)
        )
    dkp_ref[...] = jnp.zeros_like(dkp_ref)
    dvp_ref[...] = jnp.zeros_like(dvp_ref)

    def step(block, carry):
        here = pl.ds(pl.multiple_of(block * QB, QB), QB)
        seen = self_mask(lens_ref, block, 1)
        keep = {}
        for head in range(2):
            query = q4[head, here, :]
            grad = g4[head, here, :]
            lse = lse_ref[head, :1, here]
            low = delta[head, :1, here]
            far = jnp.exp(dot_nt(k4p[head], query) - lse)
            near = jnp.exp(jnp.where(seen, dot_nt(k4s[head, here, :], query), MASKED) - lse)
            far_g = far * (dot_nt(v4p[head], grad) - low)
            near_g = near * (dot_nt(v4s[head, here, :], grad) - low)
            grad2 = g2[head, here, :]
            query2 = q2[head, here, :]
            ph, p_l = split(far)
            dvp = dot(ph, grad2) + dot(p_l, grad2)
            ph, p_l = split(near)
            dvs = dot(ph, grad2) + dot(p_l, grad2)
            sh, sl = split(far_g)
            dkp = dot(sh, query2) + dot(sl, query2)
            dq = dot(k2tp[head], sh) + dot(k2tp[head], sl)
            sh, sl = split(near_g)
            dks = dot(sh, query2) + dot(sl, query2)
            side = k2ts[head, :, here]
            dq = dq + dot(side, sh) + dot(side, sl)
            dq = dq[:HD] + dq[HD:]
            keep[head] = (
                dq,
                dkp + pltpu.roll(dkp, HD, 1),
                dvp + pltpu.roll(dvp, HD, 1),
                dks + pltpu.roll(dks, HD, 1),
                dvs + pltpu.roll(dvs, HD, 1),
            )
        left = lane_ids((QB, 128)) < HD
        far_left = lane_ids(dkp_ref.shape) < HD
        dq_ref[here, :] = jnp.transpose(
            jnp.concatenate([keep[0][0], keep[1][0]], axis=0)
        ) * 0.125
        dkp_ref[...] += jnp.where(far_left, keep[0][1], keep[1][1])
        dvp_ref[...] += jnp.where(far_left, keep[0][2], keep[1][2])
        dks_ref[here, :] = jnp.where(left, keep[0][3], keep[1][3])
        dvs_ref[here, :] = jnp.where(left, keep[0][4], keep[1][4])
        return carry

    lax.fori_loop(0, rows // QB, step, 0)


def attend_backward(lens, q, k_both, v_both, out, grad, lse):
    rows, width = q.shape
    heads = width // HD
    near = pl.BlockSpec((rows, 128), lambda j, lens: (0, j))
    group = pl.BlockSpec((rows, 128), lambda j, lens: (1, j))
    flops = heads * 2 * rows * (rows + QB) * (256 * 5)
    shape = jax.ShapeDtypeStruct((rows, width), F32)
    return pl.pallas_call(
        backward_kernel,
        grid_spec=pltpu.PrefetchScalarGridSpec(
            num_scalar_prefetch=1,
            grid=(heads // 2,),
            in_specs=[
                near, near, near, group, group, near, near,
                pl.BlockSpec((2, 8, rows), lambda j, lens: (j, 0, 0)),
            ],
            out_specs=[near] * 5,
            scratch_shapes=[
                pltpu.VMEM((2, rows, 256), BF),
                pltpu.VMEM((2, rows, 256), BF),
                pltpu.VMEM((2, rows, 256), BF),
                pltpu.VMEM((2, rows, 256), BF),
                pltpu.VMEM((2, rows, 256), BF),
                pltpu.VMEM((2, rows, 256), BF),
                pltpu.VMEM((2, rows, 128), BF),
                pltpu.VMEM((2, rows, 128), BF),
                pltpu.VMEM((2, 128, rows), BF),
                pltpu.VMEM((2, 128, rows), BF),
                pltpu.VMEM((2, 8, rows), F32),
            ],
        ),
        out_shape=[shape] * 5,
        compiler_params=pltpu.CompilerParams(vmem_limit_bytes=56 << 20),
        cost_estimate=pl.CostEstimate(
            flops=flops, bytes_accessed=12 * rows * width * 4, transcendentals=heads * rows * rows
        ),
        name="attention_backward",
    )(lens, q, k_both, v_both, k_both, v_both, out, grad, lse)


TRANSFERS = {
    (0, 2): [("first", 0, 3), ("send", 0, 1)],
    (0, 4): [("first", 0, 2), ("send", 0, 0)],
    (1, 0): [("second", 0, 3)],
    (1, 1): [("first", 0, 1)],
    (1, 2): [("second", 0, 2)],
    (1, 3): [("first", 0, 0), ("send", 1, 3), ("send", 1, 2), ("send", 1, 1), ("send", 1, 0)],
    (1, 4): [("second", 0, 1)],
    (2, 0): [("second", 0, 0), ("qkv", 0, 3)],
    (2, 1): [("qkv", 0, 2)],
    (2, 2): [("first", 1, 3), ("first", 1, 2), ("qkv", 0, 1)],
    (2, 3): [("first", 1, 1), ("first", 1, 0), ("qkv", 0, 0)],
}


def backward_all_kernel(
    bits, lens_ref, lse_ref, xt_high, xt_low, w_high, w_low, small_ref,
    q_hbm, k_hbm, v_hbm, o_hbm, g_hbm, first_hbm, up_hbm, out_hbm,
    grad_in, up_mine, up_other, out_mine, out_other, qkv_mine, qkv_other, small_out,
    q_in, k_in, v_in, o_in, g_in, q4, g4, k2p, k2s, v2p, v2s, q2, g2, k2tp, k2ts, delta,
    d_q, d_k, d_v, d_kv, d_q2, on_prompt, on_own, prompt_in, far_in,
    up_a, up_b, up_ra, up_rax, up_rb, up_rby, up_s, up_rz,
    out_a, out_b, out_ra, out_rax, out_rb, out_rby, out_s, out_rz,
    qkv_g, qkv_in, qkv_x, sm, sm_in, sm_x, sm_pair,
    load_sem, acc_sem, xy_send, xy_recv, z_send, z_recv, end_send, end_recv,
    q_send, q_recv, qx_send, qx_recv, s_send, s_recv, sx_send, sx_recv, t_send, t_recv,
):
    me = lax.axis_index("dp")
    seq = lax.axis_index("seq")
    group, role = seq // 2, seq % 2
    masks = hop_masks(bits)
    count = 1 << bits
    layers = count // 2
    zbits = bits - 1
    width, both_rows = xt_high.shape
    half = w_high.shape[2]
    rows = both_rows // 2
    own = rows // 2
    shard = width // count
    pairs = half // 128
    kinds = (
        (up_hbm, up_a, up_b, up_ra, up_rax, up_rb, up_rby, up_s, up_rz, up_mine, up_other),
        (out_hbm, out_a, out_b, out_ra, out_rax, out_rb, out_rby, out_s, out_rz, out_mine, out_other),
    )

    def stage(pair):
        lanes = pl.ds(pair * 128, 128)
        copies = []
        for index, (src, dst) in enumerate(
            ((q_hbm, q_in), (k_hbm, k_in), (v_hbm, v_in), (o_hbm, o_in), (g_hbm, g_in))
        ):
            copies.append(pltpu.make_async_copy(src.at[:, lanes], dst, load_sem.at[index]))
        return copies

    for copy in stage(0):
        copy.start()
    first_copy = pltpu.make_async_copy(first_hbm, on_own.at[pl.ds(0, own)], load_sem.at[5])
    first_copy.start()
    kept = {}
    for kind in range(2):
        grads, acc_a, acc_b = kinds[kind][:3]
        for layer in reversed(range(layers)):
            slot = me ^ (layer * 2)
            for index, copy in enumerate(
                (
                    (grads.at[slot, :, pl.ds(0, 2)], acc_a.at[layer]),
                    (grads.at[slot, group, pl.ds(2, 1)], acc_b.at[layer, 0]),
                    (grads.at[slot ^ 1, group, pl.ds(2, 1)], acc_b.at[layer, 1]),
                )
            ):
                kept[kind, layer, index] = pltpu.make_async_copy(
                    *copy, acc_sem.at[kind, layer, index]
                )
                kept[kind, layer, index].start()
    greet(bits)
    started = []

    def go(make, *which):
        make(*which).start()
        started.append((make, which))

    def xy(kind, layer, step):
        grads, acc_a, acc_b, ra, rax, rb, rby = kinds[kind][:7]
        slot = me ^ (layer * 2)
        src, dst, target = (
            (grads.at[slot ^ 1, :, pl.ds(0, 2)], ra.at[layer], partner(1, 0)),
            (grads.at[slot, group ^ 1, pl.ds(2, 1)], rb.at[layer, 0], partner(0, 2)),
            (grads.at[slot ^ 1, group ^ 1, pl.ds(2, 1)], rb.at[layer, 1], partner(0, 2)),
            (acc_a.at[layer, group ^ 1], rax.at[layer], partner(0, 2)),
            (acc_b.at[layer, 1], rby.at[layer], partner(1, 0)),
        )[step]
        return remote(
            src, dst, xy_send.at[kind, layer, step], xy_recv.at[kind, layer, step], target
        )

    def send(kind, layer):
        for step in range(3):
            go(xy, kind, layer, step)

    def first(kind, layer):
        _, acc_a, acc_b, ra, _, rb = kinds[kind][:6]
        for index in range(3):
            kept[kind, layer, index].wait()
        for step in range(3):
            xy(kind, layer, step).wait_recv()
        acc_a[layer] += ra[layer]
        acc_b[layer] += rb[layer]
        go(xy, kind, layer, 3)
        go(xy, kind, layer, 4)

    def climb(kind, layer, hop):
        index = layer ^ (1 << hop)
        total, landing = kinds[kind][7], kinds[kind][8]
        place = (1 << hop) + index
        return remote(
            total.at[layer], landing.at[place], z_send.at[kind, layer], z_recv.at[kind, place],
            partner(2 << hop, 0),
        )

    def second(kind, layer):
        _, acc_a, acc_b, _, rax, _, rby, total, landing = kinds[kind][:9]
        xy(kind, layer, 3).wait_recv()
        xy(kind, layer, 4).wait_recv()
        total[layer, pl.ds(0, 2)] = acc_a[layer, group] + rax[layer]
        total[layer, pl.ds(2, 1)] = acc_b[layer, 0] + rby[layer]
        top = layer.bit_length() - 1
        for hop in reversed(range(top + 1, zbits)):
            climb(kind, layer | (1 << hop), hop).wait_recv()
            total[layer] += landing[(1 << hop) + layer]
        if layer:
            go(climb, kind, layer, top)

    def cross(kind):
        total, mine = kinds[kind][7], kinds[kind][9]
        return remote(
            total.at[0], mine.at[group], end_send.at[kind, 0], end_recv.at[kind, 0], partner(0, 2)
        )

    def cross_in(kind):
        total, mine = kinds[kind][7], kinds[kind][9]
        return remote(
            total.at[0], mine.at[group ^ 1], end_send.at[kind, 0], end_recv.at[kind, 0], partner(0, 2)
        )

    def hand(kind):
        mine, other = kinds[kind][9:]
        return remote(mine, other, end_send.at[kind, 1], end_recv.at[kind, 1], partner(0, 1))

    def block(pair, relative):
        return qkv_g.at[pair, :, me ^ slot_mask(bits, relative)]

    def step_down(pair, relative, hop):
        index = relative ^ (1 << hop)
        place = (1 << hop) + index
        return remote(
            block(pair, relative), qkv_in.at[pair, place], q_send.at[pair, relative],
            q_recv.at[pair, place], partner(masks[hop], 0),
        )

    def leave(pair, relative, hop):
        go(step_down, pair, relative, hop)

    def qkv_begin(pair):
        for relative in reversed(range(count // 2, count)):
            leave(pair, relative, bits - 1)

    def qkv(pair, relative):
        here = block(pair, relative)
        top = relative.bit_length() - 1
        for hop in reversed(range(top + 1, bits)):
            step_down(pair, relative | (1 << hop), hop).wait_recv()
            here[...] += qkv_in[pair, (1 << hop) + relative]
        if relative:
            leave(pair, relative, top)

    def qkv_cross(pair):
        return remote(
            block(pair, 0), qkv_x.at[pair], qx_send.at[pair, 0], qx_recv.at[pair, 0], partner(0, 2)
        )

    def qkv_hand(pair):
        return remote(
            qkv_mine.at[pair], qkv_other.at[pair], qx_send.at[pair, 1], qx_recv.at[pair, 1],
            partner(0, 1),
        )

    def qkv_finish(pair):
        qkv_cross(pair).wait_recv()
        qkv_mine[pair] = block(pair, 0)[...] + qkv_x[pair]
        go(qkv_hand, pair)

    actions = {"send": send, "first": first, "second": second, "qkv": qkv}

    def run(events):
        for name, kind, index in events:
            actions[name](kind, index)

    def prepare(pair):
        prod = jnp.transpose(o_in[...] * g_in[...])
        for head in range(2):
            hl, hh, ll = packs(q_in[...] * 0.125, head)
            q2[head] = hl
            q4[head, :, :128] = hh
            q4[head, :, 128:] = ll
            hl, hh, ll = packs(g_in[...], head)
            g2[head] = hl
            g4[head, :, :128] = hh
            g4[head, :, 128:] = ll
            for src, start, dst in (
                (k_in, 0, k2p), (k_in, rows, k2s), (v_in, 0, v2p), (v_in, rows, v2s),
            ):
                dst[head] = packs(src[pl.ds(start, rows), :], head)[0]
            for start, dst in ((0, k2tp), (rows, k2ts)):
                flipped = jnp.transpose(k_in[pl.ds(start, rows), :])[head * HD : head * HD + HD]
                high, low = high_low(flipped)
                dst[head, :HD] = high.astype(BF)
                dst[head, HD:] = low.astype(BF)
            delta[head] = jnp.broadcast_to(
                jnp.sum(prod[head * HD : head * HD + HD], axis=0, keepdims=True), (8, rows)
            )

    def twice(value):
        return jnp.concatenate([value, value], axis=1)

    def attend(pair):
        d_k[pl.ds(0, rows), :] = jnp.zeros((rows, 128), F32)
        d_v[pl.ds(0, rows), :] = jnp.zeros((rows, 128), F32)

        def body(step, carry):
            for position in range(4):
                events = TRANSFERS.get((pair, position))
                if events:
                    @pl.when(step == position)
                    def _():
                        run(events)

            here = pl.ds(pl.multiple_of(step * QB, QB), QB)
            there = pl.ds(pl.multiple_of(step * QB + rows, QB), QB)
            seen = self_mask(lens_ref, step, 1)
            keep = {}
            for head in range(2):
                query = q4[head, here, :]
                grad = g4[head, here, :]
                lse = lse_ref[2 * pair + head, :1, here]
                low = delta[head, :1, here]
                far = jnp.exp(dot_nt(twice(k2p[head]), query) - lse)
                near = jnp.exp(
                    jnp.where(seen, dot_nt(twice(k2s[head, here, :]), query), MASKED) - lse
                )
                far_g = far * (dot_nt(twice(v2p[head]), grad) - low)
                near_g = near * (dot_nt(twice(v2s[head, here, :]), grad) - low)
                grad2 = g2[head, here, :]
                query2 = q2[head, here, :]
                ph, p_l = split(far)
                dvp = dot(ph, grad2) + dot(p_l, grad2)
                ph, p_l = split(near)
                dvs = dot(ph, grad2) + dot(p_l, grad2)
                sh, sl = split(far_g)
                dkp = dot(sh, query2) + dot(sl, query2)
                dq = dot(k2tp[head], sh) + dot(k2tp[head], sl)
                sh, sl = split(near_g)
                dks = dot(sh, query2) + dot(sl, query2)
                side = k2ts[head, :, here]
                dq = dq + dot(side, sh) + dot(side, sl)
                keep[head] = (
                    dq[:HD] + dq[HD:],
                    dkp + pltpu.roll(dkp, HD, 1),
                    dvp + pltpu.roll(dvp, HD, 1),
                    dks + pltpu.roll(dks, HD, 1),
                    dvs + pltpu.roll(dvs, HD, 1),
                )
            left = lane_ids((QB, 128)) < HD
            far_left = lane_ids((rows, 128)) < HD
            d_q[here, :] = jnp.transpose(
                jnp.concatenate([keep[0][0], keep[1][0]], axis=0)
            ) * 0.125
            d_k[pl.ds(0, rows), :] += jnp.where(far_left, keep[0][1], keep[1][1])
            d_v[pl.ds(0, rows), :] += jnp.where(far_left, keep[0][2], keep[1][2])
            d_k[there, :] = jnp.where(left, keep[0][3], keep[1][3])
            d_v[there, :] = jnp.where(left, keep[0][4], keep[1][4])
            return carry

        lax.fori_loop(0, 4, body, 0)

    def divide():
        def body(index, carry):
            here = pl.ds(pl.multiple_of(index * QB, QB), QB)
            high, low = split(d_k[here, :])
            d_kv[here, 0:128] = high
            d_kv[here, 256:384] = low
            high, low = split(d_v[here, :])
            d_kv[here, 128:256] = high
            d_kv[here, 384:512] = low

            @pl.when(index < 4)
            def _():
                high, low = split(d_q[here, :])
                d_q2[here, 0:128] = high
                d_q2[here, 128:256] = low

            return carry

        lax.fori_loop(0, 8, body, 0)

    def to_prompt(pair):
        lanes = pl.ds(pair * 128, 128)
        high_w = jnp.concatenate([w_high[1, :, lanes], w_high[2, :, lanes]], axis=1)
        low_w = jnp.concatenate([w_low[1, :, lanes], w_low[2, :, lanes]], axis=1)

        def body(index, carry):
            here = pl.ds(pl.multiple_of(index * QB, QB), QB)
            high, low = d_kv[here, 0:256], d_kv[here, 256:512]
            result = dot_nt(high, high_w) + dot_nt(high, low_w) + dot_nt(low, high_w)
            on_prompt[here, :] = result if pair == 0 else on_prompt[here, :] + result
            return carry

        lax.fori_loop(0, 4, body, 0)

    def to_own(pair):
        lanes = pl.ds(pair * 128, 128)
        order = (1, 2, 0)
        high_w = jnp.concatenate([w_high[i, :, lanes] for i in order], axis=1)
        low_w = jnp.concatenate([w_low[i, :, lanes] for i in order], axis=1)

        def body(index, carry):
            here = pl.ds(pl.multiple_of(index * QB, QB), QB)
            there = pl.ds(pl.multiple_of(index * QB + rows, QB), QB)
            high = jnp.concatenate([d_kv[there, 0:256], d_q2[here, 0:128]], axis=1)
            low = jnp.concatenate([d_kv[there, 256:512], d_q2[here, 128:256]], axis=1)
            result = dot_nt(high, high_w) + dot_nt(high, low_w) + dot_nt(low, high_w)
            on_own[here, :] += result
            return carry

        lax.fori_loop(0, 4, body, 0)

    def weight_grads(pair):
        each = count // 2
        size = each * shard

        def body(index, carry):
            here = pl.ds(pl.multiple_of(index * size, size), size)
            high, low = xt_high[here, :], xt_low[here, :]
            first_kv = dot(high, d_kv[...])
            kv = first_kv[:, :256] + first_kv[:, 256:] + dot(low, d_kv[:, 0:256])
            high, low = high[:, rows:], low[:, rows:]
            first_q = dot(high, d_q2[...])
            query = first_q[:, :128] + first_q[:, 128:] + dot(low, d_q2[:, 0:128])
            for slot in range(each):
                part = slice(slot * shard, slot * shard + shard)
                qkv_g[pair, 0, index * each + slot] = query[part]
                qkv_g[pair, 1, index * each + slot] = kv[part, :128]
                qkv_g[pair, 2, index * each + slot] = kv[part, 128:]
            return carry

        lax.fori_loop(0, 2, body, 0)

    sums_q, sums_v = [], []
    send(0, 3)
    send(0, 2)
    on_own[pl.ds(own, own), :] = jnp.zeros((own, width), F32)
    for pair in range(pairs):
        for copy in stage(pair):
            copy.wait()
        prepare(pair)
        if pair + 1 < pairs:
            for copy in stage(pair + 1):
                copy.start()
        attend(pair)
        run(TRANSFERS.get((pair, 4), []))
        divide()
        sums_q.append(jnp.sum(d_q[...], axis=0, keepdims=True))
        sums_v.append(jnp.sum(d_v[...], axis=0, keepdims=True))
        if pair == 0:
            first_copy.wait()
        if pair + 1 < pairs:
            weight_grads(pair)
            qkv_begin(pair)
            to_prompt(pair)
            to_own(pair)

    def swap(src, dst, index):
        return remote(src, dst, t_send.at[index], t_recv.at[index], partner(0, 1))

    last = pairs - 1
    to_prompt(last)
    prompt_swap = swap(on_prompt.at[pl.ds(own, own)], prompt_in, 0)
    go(lambda: prompt_swap)
    go(qkv_cross, 0)
    go(cross, 0)
    weight_grads(last)
    qkv_begin(last)
    prompt_swap.wait_recv()
    on_prompt[pl.ds(0, own), :] += prompt_in[...]
    far = remote(on_prompt.at[pl.ds(0, own)], far_in, t_send.at[1], t_recv.at[1], partner(0, 2))

    @pl.when(group == 1)
    def _():
        far.start()

    qkv(1, 3)
    qkv(1, 2)
    to_own(last)
    own_swap = swap(on_own.at[pl.ds(own, own)], grad_in, 2)
    go(lambda: own_swap)

    bias_q = jnp.concatenate(sums_q, axis=1)
    bias_v = jnp.concatenate(sums_v, axis=1)
    bias = jnp.concatenate([bias_q, bias_v, jnp.zeros((6, half), F32)], axis=0)
    nothing = jnp.zeros((8, half), F32)
    bias = jnp.where(
        role == 0,
        jnp.concatenate([bias, nothing], axis=1),
        jnp.concatenate([nothing, bias], axis=1),
    )
    inside = lane_ids((8, 128)) < shard
    for slot in range(count):
        turned = pltpu.roll(bias, (width - shard * slot) % width, 1) if slot else bias
        sm[slot] = small_ref[slot]
        sm[slot, pl.ds(0, 8), :] += jnp.where(inside, turned[:, :128], 0.0)

    def small_step(relative, hop):
        index = relative ^ (1 << hop)
        place = (1 << hop) + index
        return remote(
            sm.at[me ^ slot_mask(bits, relative)], sm_in.at[place], s_send.at[relative],
            s_recv.at[place], partner(masks[hop], 0),
        )

    for relative in reversed(range(count // 2, count)):
        go(small_step, relative, bits - 1)
    second(1, 3)
    second(1, 2)
    qkv(1, 1)
    qkv(last, 3)
    qkv(last, 2)
    qkv(1, 0)
    go(qkv_cross, 1)
    second(1, 1)
    second(1, 0)
    go(cross, 1)
    qkv_finish(0)
    for relative in reversed(range(count // 2)):
        top = relative.bit_length() - 1
        slot = me ^ slot_mask(bits, relative)
        for hop in reversed(range(top + 1, bits)):
            small_step(relative | (1 << hop), hop).wait_recv()
            sm[slot] += sm_in[(1 << hop) + relative]
        if relative:
            go(small_step, relative, top)
    small_x = remote(sm.at[me], sm_x, sx_send.at[0], sx_recv.at[0], partner(0, 2))
    go(lambda: small_x)
    for kind in range(2):
        kinds[kind][9][group] = kinds[kind][7][0]
        cross_in(kind).wait_recv()
        go(hand, kind)
    qkv_finish(1)
    small_x.wait_recv()
    small_out[...] = sm[me] + sm_x[...]
    small_pair = remote(small_out, sm_pair, sx_send.at[1], sx_recv.at[1], partner(0, 1))
    go(lambda: small_pair)
    qkv(last, 1)
    qkv(last, 0)
    go(qkv_cross, last)
    own_swap.wait_recv()
    grad_in[...] += on_own[pl.ds(0, own), :]
    qkv_finish(last)

    @pl.when(group == 0)
    def _():
        far.wait_recv()
        grad_in[...] += on_prompt[pl.ds(0, own), :] + far_in[...]

    small_pair.wait_recv()
    for kind in range(2):
        hand(kind).wait_recv()
    for pair in range(pairs):
        qkv_hand(pair).wait_recv()
    for make, which in started:
        make(*which).wait_send()
    small_out[...] += sm_pair[...]

    @pl.when(group == 1)
    def _():
        far.wait_send()


def run_backward(lens, lse, xt_high, xt_low, w_high, w_low, small, q, k, v, o, g, first_grad,
                 up_grads, out_grads):
    bits = dp_bits()
    count = 1 << bits
    layers = count // 2
    anywhere = pl.BlockSpec(memory_space=pl.ANY)
    vmem = pl.BlockSpec(memory_space=pltpu.VMEM)
    width, both_rows = xt_high.shape
    rows, half = q.shape
    own = rows // 2
    pairs = half // 128
    shard = width // count
    shape = lambda *dims: jax.ShapeDtypeStruct(dims, F32)
    space = lambda *dims: pltpu.VMEM(dims, F32)
    short = lambda *dims: pltpu.VMEM(dims, BF)
    dma = lambda *dims: pltpu.SemaphoreType.DMA(dims)

    def buffers(unit):
        return [
            space(layers, 2, 2, *unit),
            space(layers, 2, 1, *unit),
            space(layers, 2, 2, *unit),
            space(layers, 2, *unit),
            space(layers, 2, 1, *unit),
            space(layers, 1, *unit),
            space(layers, 3, *unit),
            space(layers, 3, *unit),
        ]

    up_unit, out_unit = up_grads.shape[3:], out_grads.shape[3:]
    tiny = small.shape[1:]
    return pl.pallas_call(
        functools.partial(backward_all_kernel, bits),
        in_specs=[pl.BlockSpec(memory_space=pltpu.SMEM)] + [vmem] * 6 + [anywhere] * 8,
        out_specs=[vmem] * 8,
        out_shape=[
            shape(own, width),
            shape(2, 3, *up_unit),
            shape(2, 3, *up_unit),
            shape(2, 3, *out_unit),
            shape(2, 3, *out_unit),
            shape(pairs, 3, shard, 128),
            shape(pairs, 3, shard, 128),
            shape(*tiny),
        ],
        scratch_shapes=[
            space(rows, 128),
            space(both_rows, 128),
            space(both_rows, 128),
            space(rows, 128),
            space(rows, 128),
            short(2, rows, 256),
            short(2, rows, 256),
            short(2, rows, 128),
            short(2, rows, 128),
            short(2, rows, 128),
            short(2, rows, 128),
            short(2, rows, 128),
            short(2, rows, 128),
            short(2, 128, rows),
            short(2, 128, rows),
            space(2, 8, rows),
            space(rows, 128),
            space(both_rows, 128),
            space(both_rows, 128),
            short(both_rows, 512),
            short(rows, 256),
            space(rows, width),
            space(rows, width),
            space(own, width),
            space(own, width),
        ]
        + buffers(up_unit)
        + buffers(out_unit)
        + [
            space(pairs, 3, count, shard, 128),
            space(pairs, count, 3, shard, 128),
            space(pairs, 3, shard, 128),
            space(count, *tiny),
            space(count, *tiny),
            space(*tiny),
            space(*tiny),
            dma(6),
            dma(2, layers, 3),
            dma(2, layers, 5),
            dma(2, layers, 5),
            dma(2, layers),
            dma(2, layers),
            dma(2, 2),
            dma(2, 2),
            dma(pairs, count),
            dma(pairs, count),
            dma(pairs, 2),
            dma(pairs, 2),
            dma(count),
            dma(count),
            dma(2),
            dma(2),
            dma(3),
            dma(3),
        ],
        compiler_params=pltpu.CompilerParams(
            collective_id=3, has_side_effects=True, vmem_limit_bytes=67043328
        ),
        name="attention_backward_and_scatter",
    )(lens, lse, xt_high, xt_low, w_high, w_low, small, q, k, v, o, g, first_grad, up_grads, out_grads)


def norm_forward(resid, gain, shift):
    center = resid - jnp.mean(resid, axis=-1, keepdims=True)
    inverse = lax.rsqrt(jnp.mean(center * center, axis=-1, keepdims=True) + EPSILON)
    normed = center * inverse
    return normed * gain + shift, normed, inverse


def norm_backward(grad_out, normed, inverse, gain):
    grad_normed = grad_out * gain
    first_term = jnp.mean(grad_normed, axis=-1, keepdims=True)
    second_term = jnp.mean(grad_normed * normed, axis=-1, keepdims=True)
    grad_resid = inverse * (grad_normed - first_term - normed * second_term)
    return grad_resid, jnp.sum(grad_out * normed, axis=0), jnp.sum(grad_out, axis=0)


def on_device(
    hidden_in,
    teacher,
    lengths,
    qkv_weight,
    qkv_bias,
    out_weight,
    out_bias,
    ln_gain,
    ln_shift,
    ffn_in,
    ffn_in_bias,
    ffn_out,
):
    _, rows, width = hidden_in.shape
    dp_count = lax.axis_size("dp")
    dp_index = lax.axis_index("dp")
    seq_index = lax.axis_index("seq")
    group, role = seq_index // 2, seq_index % 2
    total_tokens = dp_count * rows * SEQ
    shard = qkv_weight.shape[1]
    half = width // 2
    ffn = ffn_in.shape[1]
    ffn_shard = ffn // dp_count
    ffn_half = ffn_shard // 2

    x_own = hidden_in.reshape(rows, width)
    target = teacher.reshape(rows, width)
    lens = lengths.reshape(CONT)

    length_sum = jnp.sum(lens).astype(F32)
    lanes = lambda value: jnp.pad(value, ((0, 0), (0, 128 - value.shape[1])))
    up_rows = -(-ffn_shard // 128)
    up_bias = jnp.pad(ffn_in_bias, (0, up_rows * 128 - ffn_shard)).reshape(up_rows, 128)
    small_rows = -(-(9 + up_rows) // 8) * 8
    small = jnp.concatenate(
        [
            lanes(qkv_bias),
            lanes(out_bias),
            lanes(ln_gain),
            lanes(ln_shift),
            up_bias,
            jnp.full((small_rows - 8 - up_rows, 128), length_sum, F32),
        ]
    )
    local_lens = jnp.where(role == 0, lens, jnp.roll(lens, CONT // 2))
    local_lens = jnp.where(group == 0, 0, local_lens)
    out_half = shard // 2
    up_piece = pick(ffn_in.reshape(shard, dp_count, 2, ffn_half), role, 2)
    out_piece = pick(out_weight.reshape(2, out_half, width), role, 0)
    down_piece = pick(ffn_out.reshape(2, ffn_half, width), role, 0)
    (w_high, w_low, small, xt_high, xt_low, k_both, v_both, queries, attended, lse,
     out_blocks, w_up, w_down, out_other) = run_forward(
        local_lens,
        lax.dynamic_slice_in_dim(qkv_weight, role * half, half, 2),
        small,
        x_own,
        out_piece.reshape(2, 3, out_half // 6, width),
        up_piece.reshape(2, 3, shard // 6, ffn // 2),
        down_piece.reshape(2, 3, ffn_half // 6, width),
    )
    w_up = w_up.reshape(width, ffn // 2)
    w_down = w_down.reshape(ffn // 2, width)
    out_mine = pick(out_blocks.reshape(2, dp_count // 2, out_half, width), role, 0)
    out_other = out_other.reshape(dp_count // 2, out_half, width)
    w_out = ordered(role, out_mine[:, None], out_other[:, None], 1).reshape(half, width)
    vectors = small[:, :8, :shard].transpose(1, 0, 2).reshape(4, 2, width)
    b_out, gains, shifts = vectors[1], vectors[2], vectors[3]
    b_up = small[:, 8 : 8 + up_rows].reshape(dp_count, up_rows * 128)[:, :ffn_shard]
    b_up = pick(b_up.reshape(dp_count, 2, ffn_half), role, 1).reshape(ffn // 2)
    count = float(dp_count * PROMPT) + jnp.sum(small[:, small_rows - 1, 0])

    def reduce_pair(partial):
        return partial[:rows] + swap_pair(partial[rows:])

    def both_halves(own):
        return jnp.concatenate([own, swap_pair(own)], axis=0)

    first_resid = x_own + reduce_pair(mm(attended, w_out)) + b_out[0]
    first_norm, first_hat, first_inv = norm_forward(first_resid, gains[0], shifts[0])
    norm_group = both_halves(first_norm)
    pre_act = mm(norm_group, w_up) + b_up
    normal_cdf = 0.5 * (1.0 + lax.erf(pre_act * INV_ROOT_TWO))
    activated = pre_act * normal_cdf
    slope = normal_cdf + pre_act * jnp.exp(-0.5 * pre_act * pre_act) * INV_ROOT_TAU
    second_resid = first_norm + reduce_pair(mm(activated, w_down)) + b_out[1]
    final, second_hat, second_inv = norm_forward(second_resid, gains[1], shifts[1])

    slot = seq_index * rows + jnp.arange(rows, dtype=jnp.int32) - PROMPT
    own_len = jnp.sum(
        jnp.where((slot // CLEN)[None] == jnp.arange(CONT, dtype=jnp.int32)[:, None], lens[:, None], 0),
        axis=0,
    )
    valid = ((slot < 0) | (slot % CLEN < own_len)).astype(F32)
    difference = (final - target) * valid[:, None]
    squares = jnp.sum(difference * difference)
    grad_final = difference * (total_tokens / count)
    grad_second, grad_gain_two, grad_shift_two = norm_backward(
        grad_final, second_hat, second_inv, gains[1]
    )
    grad_bias_down = jnp.sum(grad_second, axis=0)
    second_group = both_halves(grad_second)
    grad_w_down = mm_tn(activated, second_group)
    grad_pre = mm_nt(second_group, w_down) * slope
    grad_b_up = jnp.sum(grad_pre, axis=0)
    grad_w_up = mm_tn(norm_group, grad_pre)
    share_down = scatter_rows(grad_w_down)
    grad_first_norm = grad_second + reduce_pair(mm_nt(grad_pre, w_up))
    grad_first, grad_gain_one, grad_shift_one = norm_backward(
        grad_first_norm, first_hat, first_inv, gains[0]
    )
    grad_bias_out = jnp.sum(grad_first, axis=0)
    first_group = both_halves(grad_first)
    grad_attended = mm_nt(first_group, w_out)
    grad_w_out = mm_tn(attended, first_group)
    mine = grad_w_out.reshape(dp_count // 2, 2, out_half, width)
    received = swap_pair(pick(mine, 1 - role, 1))
    mine = ordered(role, pick(mine, role, 1), received, 0)
    up = jnp.zeros((dp_count, 2, ffn_half), F32)
    up = lax.dynamic_update_slice(up, grad_b_up.reshape(dp_count, 1, ffn_half), (0, role, 0))
    up = jnp.pad(up.reshape(dp_count, ffn_shard), ((0, 0), (0, up_rows * 128 - ffn_shard)))

    def small_block(bias_q, bias_v):
        vectors = jnp.stack(
            [
                bias_q,
                bias_v,
                grad_bias_out,
                grad_bias_down,
                grad_gain_one,
                grad_gain_two,
                grad_shift_one,
                grad_shift_two,
            ]
        )
        vectors = vectors.reshape(8, dp_count, shard).transpose(1, 0, 2)
        return jnp.concatenate(
            [
                jnp.pad(vectors, ((0, 0), (0, 0), (0, 128 - shard))),
                up.reshape(dp_count, up_rows, 128),
                jnp.full((dp_count, small_rows - 8 - up_rows, 128), squares, F32),
            ],
            axis=1,
        )

    def join(share, axis):
        return ordered(role, share, swap_pair(share), axis)

    if dp_count <= 8:
        (grad_input, up_mine, up_other, out_mine, out_other, qkv_mine, qkv_other, small) = run_backward(
            local_lens, lse, xt_high, xt_low, w_high, w_low,
            small_block(jnp.zeros((width,), F32), jnp.zeros((width,), F32)),
            queries, k_both, v_both, attended, grad_attended, grad_first,
            grad_w_up.reshape(dp_count, 2, 3, shard // 6, ffn // 2),
            mine.reshape(dp_count, 2, 3, out_half // 6, width),
        )
        lay = lambda value: value.transpose(1, 2, 0, 3).reshape(3, shard, half)
        out_qkv = ordered(role, lay(qkv_mine), lay(qkv_other), 2)
        out_out = ordered(
            role, out_mine.reshape(out_half, width), out_other.reshape(out_half, width), 0
        )
        lay = lambda value: value.reshape(shard, dp_count, 1, ffn_half)
        out_up = ordered(role, lay(up_mine), lay(up_other), 2).reshape(shard, ffn)
    else:
        share_up = scatter_rows(grad_w_up)
        d_q, d_kp, d_vp, d_ks, d_vs = attend_backward(
            local_lens, queries, k_both, v_both, attended, grad_attended, lse
        )
        weights = w_high.astype(F32) + w_low.astype(F32)
        w_q, w_k, w_v = weights[0], weights[1], weights[2]
        x_t = xt_high.astype(F32) + xt_low.astype(F32)
        on_prompt = reduce_pair(mm_nt(d_kp, w_k) + mm_nt(d_vp, w_v))
        from_cont = lax.ppermute(on_prompt, "seq", [(2, 0), (3, 1)])
        grad_w_k = mm(x_t, jnp.concatenate([d_kp, d_ks], axis=0))
        grad_w_v = mm(x_t, jnp.concatenate([d_vp, d_vs], axis=0))
        grad_w_q = mm(x_t[:, 2 * rows :], d_q)
        on_own = reduce_pair(mm_nt(d_q, w_q) + mm_nt(d_ks, w_k) + mm_nt(d_vs, w_v))
        grad_input = grad_first + on_own + jnp.where(group == 0, on_prompt + from_cont, 0.0)

        def widen(value):
            return lax.dynamic_update_slice(jnp.zeros((width,), F32), value, (role * half,))

        share_qkv, share_out, small, other_qkv, other_out = scatter_all(
            jnp.stack([grad_w_q, grad_w_k, grad_w_v]).reshape(3, dp_count, shard, half),
            mine.reshape(dp_count, out_half, width),
            small_block(
                widen(jnp.sum(d_q, axis=0)),
                widen(jnp.sum(d_vp, axis=0) + jnp.sum(d_vs, axis=0)),
            ),
        )
        out_qkv = ordered(role, share_qkv, other_qkv, 2)
        out_out = ordered(role, share_out, other_out, 0)
        out_up = join(share_up.reshape(shard, dp_count, 1, ffn_half), 2).reshape(shard, ffn)
    out_down = join(share_down.reshape(ffn_half, width), 0)
    pairs = small[:8, :shard].reshape(4, 2, shard)
    out_b_up = small[8 : 8 + up_rows].reshape(up_rows * 128)[:ffn_shard]
    loss = small[small_rows - 1, 0] / (count * width)
    return (
        final[None],
        grad_input[None],
        out_qkv,
        pairs[0],
        out_out,
        pairs[1],
        pairs[2],
        pairs[3],
        out_up,
        out_b_up,
        out_down,
        loss,
    )


def solution(mesh):
    return jax.shard_map(
        on_device,
        mesh=mesh,
        in_specs=(
            P("dp", "seq", None),
            P("dp", "seq", None),
            P("dp", None),
            P(None, "dp", None),
            P(None, "dp"),
            P("dp", None),
            P(None, "dp"),
            P(None, "dp"),
            P(None, "dp"),
            P("dp", None),
            P("dp"),
            P("dp", None),
        ),
        out_specs=(
            P("dp", "seq", None),
            P("dp", "seq", None),
            P(None, "dp", None),
            P(None, "dp"),
            P("dp", None),
            P(None, "dp"),
            P(None, "dp"),
            P(None, "dp"),
            P("dp", None),
            P("dp"),
            P("dp", None),
            P(),
        ),
        check_vma=False,
    )
```

```python
import functools

import jax
import jax.numpy as jnp
from jax import lax
from jax.experimental import pallas as pl
from jax.experimental.pallas import tpu as pltpu
from jax.sharding import PartitionSpec as P

HD = 64
PROMPT = 1024
CONT = 8
CLEN = 128
SEQ = 4
QB = 256

HIGH = lax.Precision.HIGH
EPSILON = 1e-05
MASKED = -1e30
INV_ROOT_TWO = 0.7071067811865476
INV_ROOT_TAU = 0.3989422804014327
BF = jnp.bfloat16
F32 = jnp.float32


def mm(left, right):
    return lax.dot_general(
        left, right, (((1,), (0,)), ((), ())), precision=HIGH, preferred_element_type=F32
    )


def mm_nt(left, right):
    return lax.dot_general(
        left, right, (((1,), (1,)), ((), ())), precision=HIGH, preferred_element_type=F32
    )


def mm_tn(left, right):
    return lax.dot_general(
        left, right, (((0,), (0,)), ((), ())), precision=HIGH, preferred_element_type=F32
    )


def swap_pair(value):
    return lax.ppermute(value, "seq", [(i, i ^ 1) for i in range(SEQ)])


def swap_group(value):
    return lax.ppermute(value, "seq", [(i, i ^ 2) for i in range(SEQ)])


def swap_dp(value, bit):
    count = lax.axis_size("dp")
    return lax.ppermute(value, "dp", [(i, i ^ (1 << bit)) for i in range(count)])


def ordered(bit, own, other, axis):
    first = jnp.where(bit == 0, own, other)
    second = jnp.where(bit == 0, other, own)
    return jnp.concatenate([first, second], axis=axis)


def pick(value, index, axis):
    return lax.dynamic_index_in_dim(value, index, axis, keepdims=False)


def dp_bits():
    return lax.axis_size("dp").bit_length() - 1


def gather_rows(piece, axis=0):
    return lax.all_gather(piece, "dp", axis=axis, tiled=True)


def scatter_rows(grads, axis=0):
    share = lax.psum_scatter(grads, "dp", scatter_dimension=axis, tiled=True)
    return share + swap_group(share)


def partner(dp_mask, seq_mask):
    return (lax.axis_index("dp") ^ dp_mask, lax.axis_index("seq") ^ seq_mask)


def remote(src, dst, send_sem, recv_sem, target):
    return pltpu.make_async_remote_copy(
        src_ref=src,
        dst_ref=dst,
        send_sem=send_sem,
        recv_sem=recv_sem,
        device_id=target,
        device_id_type=pl.DeviceIdType.MESH,
    )


def greet(bits):
    barrier = pltpu.get_barrier_semaphore()
    others = [partner(1 << bit, 0) for bit in range(bits)] + [partner(0, 1), partner(0, 2)]
    for other in others:
        pl.semaphore_signal(
            barrier, inc=1, device_id=other, device_id_type=pl.DeviceIdType.MESH
        )
    pl.semaphore_wait(barrier, len(others))


def hop_masks(bits):
    return [1 << bit for bit in range(1, bits)] + [1]


def slot_mask(bits, relative):
    masks = hop_masks(bits)
    return sum(masks[p] for p in range(bits) if relative >> p & 1)


def scatter_kernel(bits, *refs):
    kinds = 3
    grads, refs = refs[:kinds], refs[kinds:]
    mine, refs = refs[:kinds], refs[kinds:]
    other, refs = refs[: kinds - 1], refs[kinds - 1 :]
    acc, refs = refs[:kinds], refs[kinds:]
    hop_in, refs = refs[:kinds], refs[kinds:]
    x_in, refs = refs[:kinds], refs[kinds:]
    pair_in, send_sem, recv_sem, x_send, x_recv, load_sem, store_sem = refs
    me = lax.axis_index("dp")
    masks = hop_masks(bits)
    count = 1 << bits

    def source(kind, relative):
        slot = me ^ slot_mask(bits, relative)
        return grads[kind].at[:, slot] if kind == 0 else grads[kind].at[slot]

    def hop_copy(kind, relative, hop, from_input):
        index = relative ^ (1 << hop)
        src = source(kind, relative) if from_input else acc[kind].at[relative]
        place = (1 << hop) + index
        return remote(
            src, hop_in[kind].at[place], send_sem.at[kind, relative], recv_sem.at[kind, place],
            partner(masks[hop], 0),
        )

    loads = {}
    for relative in reversed(range(count // 2)):
        for kind in range(kinds):
            copy = pltpu.make_async_copy(
                source(kind, relative), acc[kind].at[relative], load_sem.at[kind, relative]
            )
            copy.start()
            loads[kind, relative] = copy
    greet(bits)
    started = []
    last = bits - 1
    for relative in reversed(range(count // 2, count)):
        for kind in range(kinds):
            copy = hop_copy(kind, relative, last, True)
            copy.start()
            started.append(copy)
    for relative in reversed(range(count // 2)):
        for kind in range(kinds):
            loads[kind, relative].wait()
        lowest = relative.bit_length() - 1
        for hop in reversed(range(max(lowest + 1, 0), bits)):
            for kind in range(kinds):
                hop_copy(kind, relative | (1 << hop), hop, hop == last).wait_recv()
                acc[kind][relative] += hop_in[kind][(1 << hop) + relative]
        if relative:
            for kind in range(kinds):
                copy = hop_copy(kind, relative, lowest, False)
                copy.start()
                started.append(copy)
    crossing = []
    for kind in range(kinds):
        copy = remote(acc[kind].at[0], x_in[kind], x_send.at[kind], x_recv.at[kind], partner(0, 2))
        copy.start()
        crossing.append(copy)
    for kind in range(kinds):
        crossing[kind].wait_recv()
        mine[kind][...] = acc[kind][0] + x_in[kind][...]
    handing = []
    for kind in range(kinds - 1):
        copy = remote(
            mine[kind], other[kind], x_send.at[kinds + kind], x_recv.at[kinds + kind], partner(0, 1)
        )
        copy.start()
        handing.append(copy)
    copy = remote(
        mine[kinds - 1], pair_in, x_send.at[2 * kinds - 1], x_recv.at[2 * kinds - 1], partner(0, 1)
    )
    copy.start()
    handing.append(copy)
    for copy in handing:
        copy.wait()
    mine[kinds - 1][...] += pair_in[...]
    for copy in started + crossing:
        copy.wait_send()


def scatter_all(qkv, out, small):
    bits = dp_bits()
    count = 1 << bits
    any_spec = pl.BlockSpec(memory_space=pl.ANY)
    vmem = pl.BlockSpec(memory_space=pltpu.VMEM)
    shapes = [(qkv.shape[0],) + qkv.shape[2:], out.shape[1:], small.shape[1:]]
    like = [jax.ShapeDtypeStruct(shape, F32) for shape in shapes]
    return pl.pallas_call(
        functools.partial(scatter_kernel, bits),
        in_specs=[any_spec] * 3,
        out_specs=[vmem] * 5,
        out_shape=like + like[:2],
        scratch_shapes=[pltpu.VMEM((count // 2,) + shape, F32) for shape in shapes]
        + [pltpu.VMEM((count,) + shape, F32) for shape in shapes]
        + [pltpu.VMEM(shape, F32) for shape in shapes]
        + [
            pltpu.VMEM(shapes[2], F32),
            pltpu.SemaphoreType.DMA((3, count)),
            pltpu.SemaphoreType.DMA((3, count)),
            pltpu.SemaphoreType.DMA((6,)),
            pltpu.SemaphoreType.DMA((6,)),
            pltpu.SemaphoreType.DMA((3, count // 2)),
            pltpu.SemaphoreType.DMA((1,)),
        ],
        compiler_params=pltpu.CompilerParams(
            collective_id=2, has_side_effects=True, vmem_limit_bytes=40 << 20
        ),
        cost_estimate=pl.CostEstimate(
            flops=0, bytes_accessed=(qkv.size + out.size) * 4 * 12, transcendentals=0
        ),
        name="scatter_attention_grads",
    )(qkv, out, small)


def lane_ids(shape):
    return lax.broadcasted_iota(jnp.int32, shape, 1)


def high_low(value):
    high = value.astype(BF).astype(F32)
    return high, value - high


def packs(value, head):
    high, low = high_low(value)
    left = lane_ids(value.shape) < HD
    high_r = pltpu.roll(high, HD, 1)
    low_r = pltpu.roll(low, HD, 1)
    if head == 0:
        return (
            jnp.where(left, high, low_r).astype(BF),
            jnp.where(left, high, high_r).astype(BF),
            jnp.where(left, low, low_r).astype(BF),
        )
    return (
        jnp.where(left, high_r, low).astype(BF),
        jnp.where(left, high_r, high).astype(BF),
        jnp.where(left, low_r, low).astype(BF),
    )


def dot(left, right):
    return lax.dot_general(left, right, (((1,), (0,)), ((), ())), preferred_element_type=F32)


def dot_nt(left, right):
    return lax.dot_general(left, right, (((1,), (1,)), ((), ())), preferred_element_type=F32)


def split(value):
    high = value.astype(BF)
    return high, (value - high.astype(F32)).astype(BF)


def self_mask(lens_ref, block, query_axis):
    key_axis = 1 - query_axis
    query = lax.broadcasted_iota(jnp.int32, (QB, QB), query_axis)
    key = lax.broadcasted_iota(jnp.int32, (QB, QB), key_axis)
    per = QB // CLEN
    seen = jnp.zeros((QB, QB), jnp.bool_)
    for piece in range(per):
        low = piece * CLEN
        limit = low + lens_ref[block * per + piece]
        inside = (query >= low) & (query < low + CLEN) & (key >= low) & (key < limit)
        seen = seen | inside
    return seen & (key <= query)


THIRDS = ((0, 1), (1, 2))


def forward_kernel(bits, lens_ref, w_ref, s_ref, x_ref, out_ref, up_ref, down_ref,
                   w_high, w_low, s_all, xt_high, xt_low, k_both, v_both, q_all, o_all, lse_all,
                   out_all, up_all, down_all, out_other,
                   w_all, x_both, x_high, x_low, q4, k4p, k4s, v2p, v2s,
                   out_buf, up_buf, down_buf,
                   send_sem, recv_sem, x_send, x_recv, own_sem, hop_send, hop_recv, pair_sem):
    me = lax.axis_index("dp")
    seq = lax.axis_index("seq")
    group, role = seq // 2, seq % 2
    rows, width = x_ref.shape
    half = w_ref.shape[2]
    layers = 1 << (bits - 1)
    quarter = layers // 4
    level, side = me // 2, me % 2
    has_up, has_down = level < layers - 1, level > 0
    above, below = (me + 2, seq), (me - 2, seq)
    barrier = pltpu.get_barrier_semaphore()

    def hello(other):
        pl.semaphore_signal(
            barrier, inc=1, device_id=other, device_id_type=pl.DeviceIdType.MESH
        )

    for other in (partner(1, 0), partner(0, 1), partner(0, 2)):
        hello(other)
    for there, other in ((has_up, above), (has_down, below)):
        @pl.when(there)
        def _(other=other):
            hello(other)
    ends = jnp.where(has_up, 1, 0) + jnp.where(has_down, 1, 0)
    pl.semaphore_wait(barrier, 3 + ends)
    both_sides = jnp.minimum(level, layers - 1 - level)

    def arrival(index):
        paired = index <= 2 * both_sides
        distance = jnp.where(paired, (index + 1) // 2, index - both_sides)
        upward = jnp.where(paired, index % 2 == 0, level < layers - 1 - level)
        return jnp.where(upward, level + distance, level - distance)

    pieces = ((out_ref, out_buf, out_all), (up_ref, up_buf, up_all), (down_ref, down_buf, down_all))
    loads = [pltpu.make_async_copy(src, buf, own_sem.at[i]) for i, (src, buf, _) in enumerate(pieces)]
    own_w = pltpu.make_async_copy(w_ref, w_all.at[:, me], own_sem.at[3])
    own_s = pltpu.make_async_copy(s_ref, s_all.at[me], own_sem.at[4])
    own_x = pltpu.make_async_copy(x_ref, x_both.at[pl.ds(2 * rows, rows)], own_sem.at[5])
    for copy in loads + [own_w, own_s, own_x]:
        copy.start()
    to_pair = remote(
        x_ref, x_both.at[pl.ds(3 * rows, rows)], x_send.at[0], x_recv.at[0], partner(0, 1)
    )
    to_far = remote(x_ref, x_both.at[pl.ds(0, rows)], x_send.at[1], x_recv.at[1], partner(0, 2))
    far_pair = remote(
        x_both.at[pl.ds(0, rows)], x_both.at[pl.ds(rows, rows)], x_send.at[2], x_recv.at[2],
        partner(0, 1),
    )
    to_pair.start()

    @pl.when(group == 0)
    def _():
        to_far.start()

    def attention_copies(slot, step, from_input=False):
        target = (above, below, partner(1, 0))[step]
        regions = (w_all.at[:, slot], s_all.at[slot])
        return [
            remote(
                (w_ref, s_ref)[kind] if from_input else region, region,
                send_sem.at[kind, slot, step], recv_sem.at[kind, slot], target,
            )
            for kind, region in enumerate(regions)
        ]

    def along(at, upward, downward):
        @pl.when((at <= level) & has_up)
        def _():
            upward()

        @pl.when((at >= level) & has_down)
        def _():
            downward()

    def starts(slot, step, from_input=False):
        for copy in attention_copies(slot, step, from_input):
            copy.start()

    def sends(slot, step):
        for copy in attention_copies(slot, step):
            copy.wait_send()

    along(level, lambda: starts(me, 0, True), lambda: starts(me, 1, True))
    starts(me, 2, True)
    for copy in loads:
        copy.wait()
    stores = [pltpu.make_async_copy(buf, dst.at[me], own_sem.at[i]) for i, (_, buf, dst) in enumerate(pieces)]
    for copy in stores:
        copy.start()

    def part(kind, layer, last, other_x, piece):
        first, count = THIRDS[piece]
        return pieces[kind][2].at[
            layer * 2 + (side ^ last), group ^ other_x, pl.ds(first, count)
        ]

    def sent(kind, layer, last, other_x, piece, step, dp_mask, seq_mask):
        region = part(kind, layer, last, other_x, piece)
        return remote(
            region, region, hop_send.at[kind, layer, step], hop_recv.at[kind, layer, step],
            partner(dp_mask, seq_mask),
        )

    steps = {
        1: (0, 0, 0, 0, 2),
        2: (0, 0, 0, 1, 0),
        3: (0, 1, 0, 1, 0),
        4: (0, 0, 1, 1, 0),
        5: (0, 0, 1, 0, 2),
        6: (1, 0, 1, 0, 2),
    }

    def give(kind, layer, step):
        last, other_x, piece, dp_mask, seq_mask = steps[step]
        return sent(kind, layer, last, other_x, piece, step, dp_mask, seq_mask)

    def take(kind, layer, step):
        last, other_x, piece, dp_mask, seq_mask = steps[step]
        return sent(
            kind, layer, last ^ dp_mask, other_x ^ (seq_mask // 2), piece, step, dp_mask, seq_mask
        )

    def climb(kind, layer, upward):
        region = pieces[kind][2].at[layer * 2 + side, group]
        return remote(
            region, region, hop_send.at[kind, layer, 0 if upward else 7],
            hop_recv.at[kind, layer, 0], above if upward else below,
        )

    def pass_on(kind, layer):
        along(
            layer, lambda: climb(kind, layer, True).start(), lambda: climb(kind, layer, False).start()
        )

    def spread(kind, index):
        layer = arrival(index)

        @pl.when(index > 0)
        def _():
            climb(kind, layer, True).wait_recv()
            pass_on(kind, layer)
            give(kind, layer, 1).start()
            give(kind, layer, 5).start()

        give(kind, layer, 2).start()
        give(kind, layer, 4).start()

    def relay(kind, index):
        layer = arrival(index)

        @pl.when(index > 0)
        def _():
            take(kind, layer, 1).wait_recv()

        give(kind, layer, 3).start()
        take(kind, layer, 4).wait_recv()
        give(kind, layer, 6).start()

    def settle(kind, layer):
        take(kind, layer, 2).wait_recv()
        take(kind, layer, 3).wait_recv()
        take(kind, layer, 6).wait_recv()

        @pl.when(layer != level)
        def _():
            take(kind, layer, 5).wait_recv()

    def drained(kind, layer):
        @pl.when(layer != level)
        def _():
            give(kind, layer, 1).wait_send()
            give(kind, layer, 5).wait_send()

        for step in (2, 3, 4, 6):
            give(kind, layer, step).wait_send()
        along(
            layer,
            lambda: climb(kind, layer, True).wait_send(),
            lambda: climb(kind, layer, False).wait_send(),
        )

    def over(action, kind, position):
        def body(index, carry):
            action(kind, position * quarter + index)
            return carry

        lax.fori_loop(0, quarter, body, 0)

    for copy in stores:
        copy.wait()

    def receive(index, carry):
        at = arrival(index)
        slot = at * 2 + side
        for copy in attention_copies(slot, 0):
            copy.wait_recv()
        along(at, lambda: starts(slot, 0), lambda: starts(slot, 1))
        starts(slot, 2)
        return carry

    lax.fori_loop(1, layers, receive, 0)
    for kind in range(3):
        pass_on(kind, level)

    def receive_side(index, carry):
        for copy in attention_copies(arrival(index) * 2 + (side ^ 1), 2):
            copy.wait_recv()
        return carry

    lax.fori_loop(0, layers, receive_side, 0)
    for position in range(4):
        over(spread, 0, position)
    over(spread, 1, 0)

    own_x.wait()
    to_pair.wait_recv()

    @pl.when(group == 1)
    def _():
        to_far.wait_recv()
        far_pair.start()
        far_pair.wait_recv()

    def halves(index, carry):
        here = pl.ds(pl.multiple_of(index * QB, QB), QB)

        @pl.when((group == 0) & (index < 2 * rows // QB))
        def _():
            x_both[here, :] = x_both[pl.ds(pl.multiple_of(index * QB + 2 * rows, QB), QB), :]

        high, low = split(x_both[here, :])
        x_high[here, :] = high
        x_low[here, :] = low
        high, low = split(jnp.transpose(x_both[here, :]))
        xt_high[:, here] = high
        xt_low[:, here] = low
        return carry

    lax.fori_loop(0, 4 * rows // QB, halves, 0)
    own_w.wait()
    own_s.wait()
    count = 1 << bits
    shard = width // count
    for index in range(3):
        for slot in range(count):
            high, low = split(w_all[index, slot])
            w_high[index, pl.ds(slot * shard, shard), :] = high
            w_low[index, pl.ds(slot * shard, shard), :] = low
    bias = jnp.zeros((8, width), F32)
    blank = jnp.zeros((8, width - 128), F32)
    for slot in range(count):
        row = jnp.concatenate([s_all[slot, :8, :], blank], axis=1)
        bias = bias + (pltpu.roll(row, shard * slot, 1) if slot else row)
    bias = jnp.where(role == 0, bias[:2, :half], bias[:2, half:])

    def project(index, here):
        high, low = x_high[here, :], x_low[here, :]
        return (
            dot(high, w_high[index]) + dot(high, w_low[index]) + dot(low, w_high[index])
        )


    def keys_values(index, carry):
        here = pl.ds(pl.multiple_of(index * QB, QB), QB)
        @pl.when(index >= 4)
        def _():
            over(relay, 0, index - 4)

        k_both[here, :] = project(1, here)
        v_both[here, :] = project(2, here) + bias[1:2]
        return carry

    lax.fori_loop(0, 8, keys_values, 0)

    def queries(index, carry):
        here = pl.ds(pl.multiple_of(index * QB, QB), QB)
        @pl.when((index == 0) | (index == 2))
        def _():
            over(spread, 1, 1 + index // 2)

        q_all[here, :] = project(0, pl.ds(pl.multiple_of(index * QB + 2 * rows, QB), QB)) + bias[:1]
        return carry

    lax.fori_loop(0, 4, queries, 0)

    for pair in range(half // 128):
        lanes = pl.ds(pair * 128, 128)
        for head in range(2):
            _, hh, ll = packs(q_all[:, lanes] * 0.125, head)
            q4[head, :, :128] = hh
            q4[head, :, 128:] = ll
            for start, key4, value2 in ((0, k4p, v2p), (2 * rows, k4s, v2s)):
                hl, _, _ = packs(k_both[pl.ds(start, 2 * rows), lanes], head)
                key4[head, :, :128] = hl
                key4[head, :, 128:] = hl
                value2[head] = packs(v_both[pl.ds(start, 2 * rows), lanes], head)[0]

        def attend(block, carry):
            if pair == 0:
                @pl.when(block == 0)
                def _():
                    over(spread, 1, 3)

                @pl.when(block > 0)
                def _():
                    over(spread, 2, block - 1)

                over(relay, 1, block)
            if pair == 1:
                @pl.when(block == 1)
                def _():
                    over(spread, 2, 3)

                @pl.when(block > 0)
                def _():
                    over(relay, 2, block - 1)
            if pair == 2:
                @pl.when(block == 2)
                def _():
                    over(relay, 2, 3)

            here = pl.ds(pl.multiple_of(block * QB, QB), QB)
            seen = self_mask(lens_ref, block, 0)
            results = []
            for head in range(2):
                query = q4[head, here, :]
                far = dot_nt(query, k4p[head])
                near = jnp.where(seen, dot_nt(query, k4s[head, here, :]), MASKED)
                top = jnp.maximum(
                    jnp.max(far, axis=1, keepdims=True), jnp.max(near, axis=1, keepdims=True)
                )
                far = jnp.exp(far - top)
                near = jnp.exp(near - top)
                total = jnp.sum(far, axis=1, keepdims=True) + jnp.sum(near, axis=1, keepdims=True)
                far_h, far_l = split(far)
                near_h, near_l = split(near)
                out = dot(far_h, v2p[head]) + dot(far_l, v2p[head])
                value = v2s[head, here, :]
                out = out + dot(near_h, value) + dot(near_l, value)
                out = (out + pltpu.roll(out, HD, 1)) / total
                lse = top + jnp.log(total)
                lse_all[2 * pair + head, :, here] = jnp.transpose(
                    jnp.broadcast_to(lse, (QB, 128))
                )[:8]
                results.append(out)
            o_all[here, lanes] = jnp.where(lane_ids((QB, 128)) < HD, results[0], results[1])
            return carry

        lax.fori_loop(0, 4, attend, 0)

    def last(index, carry):
        for kind in range(3):
            settle(kind, index)
        return carry

    lax.fori_loop(0, layers, last, 0)
    part_count = count // 2
    swap = remote(
        out_all.at[pl.ds((1 - role) * part_count, part_count)], out_other, pair_sem.at[0],
        pair_sem.at[1], partner(0, 1),
    )
    swap.start()

    def ended(index, carry):
        for kind in range(3):
            drained(kind, index)
        return carry

    lax.fori_loop(0, layers, ended, 0)
    def passed(index, carry):
        slot = index * 2 + side
        along(index, lambda: sends(slot, 0), lambda: sends(slot, 1))
        sends(slot, 2)
        return carry

    lax.fori_loop(0, layers, passed, 0)
    to_pair.wait_send()

    @pl.when(group == 0)
    def _():
        to_far.wait_send()

    @pl.when(group == 1)
    def _():
        far_pair.wait_send()

    swap.wait()


def run_forward(lens, weights, small, tokens, out_piece, up_piece, down_piece):
    bits = dp_bits()
    count = 1 << bits
    layers = count // 2
    anywhere = pl.BlockSpec(memory_space=pl.ANY)
    vmem = pl.BlockSpec(memory_space=pltpu.VMEM)
    three, shard, half = weights.shape
    rows, width = tokens.shape
    heads = half // HD
    shape = lambda *dims: jax.ShapeDtypeStruct(dims, F32)
    whole = lambda piece: shape(count, *piece.shape)
    return pl.pallas_call(
        functools.partial(forward_kernel, bits),
        in_specs=[pl.BlockSpec(memory_space=pltpu.SMEM)] + [anywhere] * 6,
        out_specs=[vmem] * 10 + [anywhere] * 4,
        out_shape=[
            jax.ShapeDtypeStruct((three, width, half), BF),
            jax.ShapeDtypeStruct((three, width, half), BF),
            shape(count, *small.shape),
            jax.ShapeDtypeStruct((width, 4 * rows), BF),
            jax.ShapeDtypeStruct((width, 4 * rows), BF),
            shape(4 * rows, half),
            shape(4 * rows, half),
            shape(2 * rows, half),
            shape(2 * rows, half),
            shape(heads, 8, 2 * rows),
            whole(out_piece),
            whole(up_piece),
            whole(down_piece),
            shape(count // 2, *out_piece.shape),
        ],
        scratch_shapes=[
            pltpu.VMEM((three, count, shard, half), F32),
            pltpu.VMEM((4 * rows, width), F32),
            pltpu.VMEM((4 * rows, width), BF),
            pltpu.VMEM((4 * rows, width), BF),
            pltpu.VMEM((2, 2 * rows, 256), BF),
            pltpu.VMEM((2, 2 * rows, 256), BF),
            pltpu.VMEM((2, 2 * rows, 256), BF),
            pltpu.VMEM((2, 2 * rows, 128), BF),
            pltpu.VMEM((2, 2 * rows, 128), BF),
            pltpu.VMEM(out_piece.shape, F32),
            pltpu.VMEM(up_piece.shape, F32),
            pltpu.VMEM(down_piece.shape, F32),
            pltpu.SemaphoreType.DMA((2, count, 3)),
            pltpu.SemaphoreType.DMA((2, count)),
            pltpu.SemaphoreType.DMA((3,)),
            pltpu.SemaphoreType.DMA((3,)),
            pltpu.SemaphoreType.DMA((6,)),
            pltpu.SemaphoreType.DMA((3, layers, 8)),
            pltpu.SemaphoreType.DMA((3, layers, 7)),
            pltpu.SemaphoreType.DMA((2,)),
        ],
        compiler_params=pltpu.CompilerParams(
            collective_id=1, has_side_effects=True, vmem_limit_bytes=60 << 20
        ),
        name="gather_weights_and_attend",
    )(lens, weights, small, tokens, out_piece, up_piece, down_piece)


def backward_kernel(lens_ref, q_ref, kp_ref, vp_ref, ks_ref, vs_ref, o_ref, g_ref, lse_ref,
                    dq_ref, dkp_ref, dvp_ref, dks_ref, dvs_ref,
                    q4, k4p, k4s, v4p, v4s, g4, q2, g2, k2tp, k2ts, delta):
    rows = q_ref.shape[0]
    prod = jnp.transpose(o_ref[...] * g_ref[...])
    for head in range(2):
        hl, hh, ll = packs(q_ref[...] * 0.125, head)
        q2[head] = hl
        q4[head, :, :128] = hh
        q4[head, :, 128:] = ll
        hl, hh, ll = packs(g_ref[...], head)
        g2[head] = hl
        g4[head, :, :128] = hh
        g4[head, :, 128:] = ll
        for src, dst in ((kp_ref, k4p), (ks_ref, k4s), (vp_ref, v4p), (vs_ref, v4s)):
            hl, _, _ = packs(src[...], head)
            dst[head, :, :128] = hl
            dst[head, :, 128:] = hl
        for src, dst in ((kp_ref, k2tp), (ks_ref, k2ts)):
            flipped = jnp.transpose(src[...])[head * HD : head * HD + HD]
            high, low = high_low(flipped)
            dst[head, :HD] = high.astype(BF)
            dst[head, HD:] = low.astype(BF)
        delta[head] = jnp.broadcast_to(
            jnp.sum(prod[head * HD : head * HD + HD], axis=0, keepdims=True), (8, rows)
        )
    dkp_ref[...] = jnp.zeros_like(dkp_ref)
    dvp_ref[...] = jnp.zeros_like(dvp_ref)

    def step(block, carry):
        here = pl.ds(pl.multiple_of(block * QB, QB), QB)
        seen = self_mask(lens_ref, block, 1)
        keep = {}
        for head in range(2):
            query = q4[head, here, :]
            grad = g4[head, here, :]
            lse = lse_ref[head, :1, here]
            low = delta[head, :1, here]
            far = jnp.exp(dot_nt(k4p[head], query) - lse)
            near = jnp.exp(jnp.where(seen, dot_nt(k4s[head, here, :], query), MASKED) - lse)
            far_g = far * (dot_nt(v4p[head], grad) - low)
            near_g = near * (dot_nt(v4s[head, here, :], grad) - low)
            grad2 = g2[head, here, :]
            query2 = q2[head, here, :]
            ph, p_l = split(far)
            dvp = dot(ph, grad2) + dot(p_l, grad2)
            ph, p_l = split(near)
            dvs = dot(ph, grad2) + dot(p_l, grad2)
            sh, sl = split(far_g)
            dkp = dot(sh, query2) + dot(sl, query2)
            dq = dot(k2tp[head], sh) + dot(k2tp[head], sl)
            sh, sl = split(near_g)
            dks = dot(sh, query2) + dot(sl, query2)
            side = k2ts[head, :, here]
            dq = dq + dot(side, sh) + dot(side, sl)
            dq = dq[:HD] + dq[HD:]
            keep[head] = (
                dq,
                dkp + pltpu.roll(dkp, HD, 1),
                dvp + pltpu.roll(dvp, HD, 1),
                dks + pltpu.roll(dks, HD, 1),
                dvs + pltpu.roll(dvs, HD, 1),
            )
        left = lane_ids((QB, 128)) < HD
        far_left = lane_ids(dkp_ref.shape) < HD
        dq_ref[here, :] = jnp.transpose(
            jnp.concatenate([keep[0][0], keep[1][0]], axis=0)
        ) * 0.125
        dkp_ref[...] += jnp.where(far_left, keep[0][1], keep[1][1])
        dvp_ref[...] += jnp.where(far_left, keep[0][2], keep[1][2])
        dks_ref[here, :] = jnp.where(left, keep[0][3], keep[1][3])
        dvs_ref[here, :] = jnp.where(left, keep[0][4], keep[1][4])
        return carry

    lax.fori_loop(0, rows // QB, step, 0)


def attend_backward(lens, q, k_both, v_both, out, grad, lse):
    rows, width = q.shape
    heads = width // HD
    near = pl.BlockSpec((rows, 128), lambda j, lens: (0, j))
    group = pl.BlockSpec((rows, 128), lambda j, lens: (1, j))
    flops = heads * 2 * rows * (rows + QB) * (256 * 5)
    shape = jax.ShapeDtypeStruct((rows, width), F32)
    return pl.pallas_call(
        backward_kernel,
        grid_spec=pltpu.PrefetchScalarGridSpec(
            num_scalar_prefetch=1,
            grid=(heads // 2,),
            in_specs=[
                near, near, near, group, group, near, near,
                pl.BlockSpec((2, 8, rows), lambda j, lens: (j, 0, 0)),
            ],
            out_specs=[near] * 5,
            scratch_shapes=[
                pltpu.VMEM((2, rows, 256), BF),
                pltpu.VMEM((2, rows, 256), BF),
                pltpu.VMEM((2, rows, 256), BF),
                pltpu.VMEM((2, rows, 256), BF),
                pltpu.VMEM((2, rows, 256), BF),
                pltpu.VMEM((2, rows, 256), BF),
                pltpu.VMEM((2, rows, 128), BF),
                pltpu.VMEM((2, rows, 128), BF),
                pltpu.VMEM((2, 128, rows), BF),
                pltpu.VMEM((2, 128, rows), BF),
                pltpu.VMEM((2, 8, rows), F32),
            ],
        ),
        out_shape=[shape] * 5,
        compiler_params=pltpu.CompilerParams(vmem_limit_bytes=56 << 20),
        cost_estimate=pl.CostEstimate(
            flops=flops, bytes_accessed=12 * rows * width * 4, transcendentals=heads * rows * rows
        ),
        name="attention_backward",
    )(lens, q, k_both, v_both, k_both, v_both, out, grad, lse)


TRANSFERS = {
    (0, 2): [("first", 0, 3), ("send", 0, 1)],
    (0, 4): [("first", 0, 2), ("send", 0, 0)],
    (1, 0): [("down", 1, 0), ("second", 0, 3)],
    (1, 1): [("first", 0, 1)],
    (1, 2): [("second", 0, 2)],
    (1, 3): [("first", 0, 0), ("send", 1, 3), ("send", 1, 2), ("send", 1, 1), ("send", 1, 0)],
    (1, 4): [("down", 2, 0), ("second", 0, 1)],
    (2, 0): [("second", 0, 0), ("qkv", 0, 3)],
    (2, 1): [("qkv", 0, 2), ("down", 3, 0)],
    (2, 2): [("first", 1, 3), ("first", 1, 2), ("qkv", 0, 1)],
    (2, 3): [("first", 1, 1), ("first", 1, 0), ("qkv", 0, 0)],
}


def backward_all_kernel(
    bits, lens_ref, lse_ref, xt_high, xt_low, w_high, w_low, small_ref,
    q_hbm, k_hbm, v_hbm, o_hbm, g_hbm, first_hbm, up_hbm, out_hbm, down_hbm,
    grad_in, up_mine, up_other, out_mine, out_other, down_mine, down_other, qkv_mine, qkv_other, small_out,
    down_far, down_near, down_sum,
    q_in, k_in, v_in, o_in, g_in, q4, g4, k2p, k2s, v2p, v2s, q2, g2, k2tp, k2ts, delta,
    d_q, d_k, d_v, d_kv, d_q2, on_prompt, on_own, prompt_in, far_in,
    up_a, up_b, up_ra, up_rax, up_rb, up_rby, up_s, up_rz,
    out_a, out_b, out_ra, out_rax, out_rb, out_rby, out_s, out_rz,
    qkv_g, qkv_in, qkv_x, sm, sm_in, sm_x, sm_pair,
    load_sem, acc_sem, xy_send, xy_recv, z_send, z_recv, end_send, end_recv,
    q_send, q_recv, qx_send, qx_recv, s_send, s_recv, sx_send, sx_recv, t_send, t_recv, d_send, d_recv,
):
    me = lax.axis_index("dp")
    seq = lax.axis_index("seq")
    group, role = seq // 2, seq % 2
    masks = hop_masks(bits)
    count = 1 << bits
    layers = count // 2
    zbits = bits - 1
    width, both_rows = xt_high.shape
    half = w_high.shape[2]
    rows = both_rows // 2
    own = rows // 2
    shard = width // count
    pairs = half // 128
    kinds = (
        (up_hbm, up_a, up_b, up_ra, up_rax, up_rb, up_rby, up_s, up_rz, up_mine, up_other),
        (out_hbm, out_a, out_b, out_ra, out_rax, out_rb, out_rby, out_s, out_rz, out_mine, out_other),
    )

    def stage(pair):
        lanes = pl.ds(pair * 128, 128)
        copies = []
        for index, (src, dst) in enumerate(
            ((q_hbm, q_in), (k_hbm, k_in), (v_hbm, v_in), (o_hbm, o_in), (g_hbm, g_in))
        ):
            copies.append(pltpu.make_async_copy(src.at[:, lanes], dst, load_sem.at[index]))
        return copies

    for copy in stage(0):
        copy.start()
    first_copy = pltpu.make_async_copy(first_hbm, on_own.at[pl.ds(0, own)], load_sem.at[5])
    first_copy.start()
    kept = {}
    for kind in range(2):
        grads, acc_a, acc_b = kinds[kind][:3]
        for layer in reversed(range(layers)):
            slot = me ^ (layer * 2)
            for index, copy in enumerate(
                (
                    (grads.at[slot, :, pl.ds(0, 2)], acc_a.at[layer]),
                    (grads.at[slot, group, pl.ds(2, 1)], acc_b.at[layer, 0]),
                    (grads.at[slot ^ 1, group, pl.ds(2, 1)], acc_b.at[layer, 1]),
                )
            ):
                kept[kind, layer, index] = pltpu.make_async_copy(
                    *copy, acc_sem.at[kind, layer, index]
                )
                kept[kind, layer, index].start()
    greet(bits)
    started = []

    def go(make, *which):
        make(*which).start()
        started.append((make, which))

    def xy(kind, layer, step):
        grads, acc_a, acc_b, ra, rax, rb, rby = kinds[kind][:7]
        slot = me ^ (layer * 2)
        src, dst, target = (
            (grads.at[slot ^ 1, :, pl.ds(0, 2)], ra.at[layer], partner(1, 0)),
            (grads.at[slot, group ^ 1, pl.ds(2, 1)], rb.at[layer, 0], partner(0, 2)),
            (grads.at[slot ^ 1, group ^ 1, pl.ds(2, 1)], rb.at[layer, 1], partner(0, 2)),
            (acc_a.at[layer, group ^ 1], rax.at[layer], partner(0, 2)),
            (acc_b.at[layer, 1], rby.at[layer], partner(1, 0)),
        )[step]
        return remote(
            src, dst, xy_send.at[kind, layer, step], xy_recv.at[kind, layer, step], target
        )

    def send(kind, layer):
        for step in range(3):
            go(xy, kind, layer, step)

    def first(kind, layer):
        _, acc_a, acc_b, ra, _, rb = kinds[kind][:6]
        for index in range(3):
            kept[kind, layer, index].wait()
        for step in range(3):
            xy(kind, layer, step).wait_recv()
        acc_a[layer] += ra[layer]
        acc_b[layer] += rb[layer]
        go(xy, kind, layer, 3)
        go(xy, kind, layer, 4)

    def climb(kind, layer, hop):
        index = layer ^ (1 << hop)
        total, landing = kinds[kind][7], kinds[kind][8]
        place = (1 << hop) + index
        return remote(
            total.at[layer], landing.at[place], z_send.at[kind, layer], z_recv.at[kind, place],
            partner(2 << hop, 0),
        )

    def second(kind, layer):
        _, acc_a, acc_b, _, rax, _, rby, total, landing = kinds[kind][:9]
        xy(kind, layer, 3).wait_recv()
        xy(kind, layer, 4).wait_recv()
        total[layer, pl.ds(0, 2)] = acc_a[layer, group] + rax[layer]
        total[layer, pl.ds(2, 1)] = acc_b[layer, 0] + rby[layer]
        top = layer.bit_length() - 1
        for hop in reversed(range(top + 1, zbits)):
            climb(kind, layer | (1 << hop), hop).wait_recv()
            total[layer] += landing[(1 << hop) + layer]
        if layer:
            go(climb, kind, layer, top)

    def cross(kind):
        total, mine = kinds[kind][7], kinds[kind][9]
        return remote(
            total.at[0], mine.at[group], end_send.at[kind, 0], end_recv.at[kind, 0], partner(0, 2)
        )

    def cross_in(kind):
        total, mine = kinds[kind][7], kinds[kind][9]
        return remote(
            total.at[0], mine.at[group ^ 1], end_send.at[kind, 0], end_recv.at[kind, 0], partner(0, 2)
        )

    def hand(kind):
        mine, other = kinds[kind][9:]
        return remote(mine, other, end_send.at[kind, 1], end_recv.at[kind, 1], partner(0, 1))

    def block(pair, relative):
        return qkv_g.at[pair, :, me ^ slot_mask(bits, relative)]

    def step_down(pair, relative, hop):
        index = relative ^ (1 << hop)
        place = (1 << hop) + index
        return remote(
            block(pair, relative), qkv_in.at[pair, place], q_send.at[pair, relative],
            q_recv.at[pair, place], partner(masks[hop], 0),
        )

    def leave(pair, relative, hop):
        go(step_down, pair, relative, hop)

    def qkv_begin(pair):
        for relative in reversed(range(count // 2, count)):
            leave(pair, relative, bits - 1)

    def qkv(pair, relative):
        here = block(pair, relative)
        top = relative.bit_length() - 1
        for hop in reversed(range(top + 1, bits)):
            step_down(pair, relative | (1 << hop), hop).wait_recv()
            here[...] += qkv_in[pair, (1 << hop) + relative]
        if relative:
            leave(pair, relative, top)

    def qkv_cross(pair):
        return remote(
            block(pair, 0), qkv_x.at[pair], qx_send.at[pair, 0], qx_recv.at[pair, 0], partner(0, 2)
        )

    def qkv_hand(pair):
        return remote(
            qkv_mine.at[pair], qkv_other.at[pair], qx_send.at[pair, 1], qx_recv.at[pair, 1],
            partner(0, 1),
        )

    def qkv_finish(pair):
        qkv_cross(pair).wait_recv()
        qkv_mine[pair] = block(pair, 0)[...] + qkv_x[pair]
        go(qkv_hand, pair)

    far_z, near_z = (me >> 2) & 1, (me >> 1) & 1
    down_own = pltpu.make_async_copy(down_hbm.at[far_z], down_sum, load_sem.at[6])

    def down_step(step, landing):
        src, dst, target = (
            (down_hbm.at[far_z ^ 1], down_far, partner(4, 0)),
            (down_sum.at[near_z ^ 1], down_near, partner(2, 0)),
            (down_mine.at[group ^ landing], down_mine.at[group ^ landing], partner(0, 2)),
            (down_mine, down_other, partner(0, 1)),
        )[step]
        return remote(src, dst, d_send.at[step], d_recv.at[step], target)

    def down(step, _):
        if step == 0:
            down_own.start()
        elif step == 1:
            down_own.wait()
            down_step(0, 0).wait_recv()
            down_sum[...] += down_far[...]
        elif step == 2:
            down_step(1, 0).wait_recv()
            down_mine[group] = down_sum[near_z] + down_near[...]
        else:
            down_step(2, 1).wait_recv()
        go(down_step, step, 0)

    actions = {"send": send, "first": first, "second": second, "qkv": qkv, "down": down}

    def run(events):
        for name, kind, index in events:
            actions[name](kind, index)

    def prepare(pair):
        prod = jnp.transpose(o_in[...] * g_in[...])
        for head in range(2):
            hl, hh, ll = packs(q_in[...] * 0.125, head)
            q2[head] = hl
            q4[head, :, :128] = hh
            q4[head, :, 128:] = ll
            hl, hh, ll = packs(g_in[...], head)
            g2[head] = hl
            g4[head, :, :128] = hh
            g4[head, :, 128:] = ll
            for src, start, dst in (
                (k_in, 0, k2p), (k_in, rows, k2s), (v_in, 0, v2p), (v_in, rows, v2s),
            ):
                dst[head] = packs(src[pl.ds(start, rows), :], head)[0]
            for start, dst in ((0, k2tp), (rows, k2ts)):
                flipped = jnp.transpose(k_in[pl.ds(start, rows), :])[head * HD : head * HD + HD]
                high, low = high_low(flipped)
                dst[head, :HD] = high.astype(BF)
                dst[head, HD:] = low.astype(BF)
            delta[head] = jnp.broadcast_to(
                jnp.sum(prod[head * HD : head * HD + HD], axis=0, keepdims=True), (8, rows)
            )

    def twice(value):
        return jnp.concatenate([value, value], axis=1)

    def attend(pair):
        d_k[pl.ds(0, rows), :] = jnp.zeros((rows, 128), F32)
        d_v[pl.ds(0, rows), :] = jnp.zeros((rows, 128), F32)

        def body(step, carry):
            for position in range(4):
                events = TRANSFERS.get((pair, position))
                if events:
                    @pl.when(step == position)
                    def _():
                        run(events)

            here = pl.ds(pl.multiple_of(step * QB, QB), QB)
            there = pl.ds(pl.multiple_of(step * QB + rows, QB), QB)
            seen = self_mask(lens_ref, step, 1)
            keep = {}
            for head in range(2):
                query = q4[head, here, :]
                grad = g4[head, here, :]
                lse = lse_ref[2 * pair + head, :1, here]
                low = delta[head, :1, here]
                far = jnp.exp(dot_nt(twice(k2p[head]), query) - lse)
                near = jnp.exp(
                    jnp.where(seen, dot_nt(twice(k2s[head, here, :]), query), MASKED) - lse
                )
                far_g = far * (dot_nt(twice(v2p[head]), grad) - low)
                near_g = near * (dot_nt(twice(v2s[head, here, :]), grad) - low)
                grad2 = g2[head, here, :]
                query2 = q2[head, here, :]
                ph, p_l = split(far)
                dvp = dot(ph, grad2) + dot(p_l, grad2)
                ph, p_l = split(near)
                dvs = dot(ph, grad2) + dot(p_l, grad2)
                sh, sl = split(far_g)
                dkp = dot(sh, query2) + dot(sl, query2)
                dq = dot(k2tp[head], sh) + dot(k2tp[head], sl)
                sh, sl = split(near_g)
                dks = dot(sh, query2) + dot(sl, query2)
                side = k2ts[head, :, here]
                dq = dq + dot(side, sh) + dot(side, sl)
                keep[head] = (
                    dq[:HD] + dq[HD:],
                    dkp + pltpu.roll(dkp, HD, 1),
                    dvp + pltpu.roll(dvp, HD, 1),
                    dks + pltpu.roll(dks, HD, 1),
                    dvs + pltpu.roll(dvs, HD, 1),
                )
            left = lane_ids((QB, 128)) < HD
            far_left = lane_ids((rows, 128)) < HD
            d_q[here, :] = jnp.transpose(
                jnp.concatenate([keep[0][0], keep[1][0]], axis=0)
            ) * 0.125
            d_k[pl.ds(0, rows), :] += jnp.where(far_left, keep[0][1], keep[1][1])
            d_v[pl.ds(0, rows), :] += jnp.where(far_left, keep[0][2], keep[1][2])
            d_k[there, :] = jnp.where(left, keep[0][3], keep[1][3])
            d_v[there, :] = jnp.where(left, keep[0][4], keep[1][4])
            return carry

        lax.fori_loop(0, 4, body, 0)

    def divide():
        def body(index, carry):
            here = pl.ds(pl.multiple_of(index * QB, QB), QB)
            high, low = split(d_k[here, :])
            d_kv[here, 0:128] = high
            d_kv[here, 256:384] = low
            high, low = split(d_v[here, :])
            d_kv[here, 128:256] = high
            d_kv[here, 384:512] = low

            @pl.when(index < 4)
            def _():
                high, low = split(d_q[here, :])
                d_q2[here, 0:128] = high
                d_q2[here, 128:256] = low

            return carry

        lax.fori_loop(0, 8, body, 0)

    def to_prompt(pair):
        lanes = pl.ds(pair * 128, 128)
        high_w = jnp.concatenate([w_high[1, :, lanes], w_high[2, :, lanes]], axis=1)
        low_w = jnp.concatenate([w_low[1, :, lanes], w_low[2, :, lanes]], axis=1)

        def body(index, carry):
            here = pl.ds(pl.multiple_of(index * QB, QB), QB)
            high, low = d_kv[here, 0:256], d_kv[here, 256:512]
            result = dot_nt(high, high_w) + dot_nt(high, low_w) + dot_nt(low, high_w)
            on_prompt[here, :] = result if pair == 0 else on_prompt[here, :] + result
            return carry

        lax.fori_loop(0, 4, body, 0)

    def to_own(pair):
        lanes = pl.ds(pair * 128, 128)
        order = (1, 2, 0)
        high_w = jnp.concatenate([w_high[i, :, lanes] for i in order], axis=1)
        low_w = jnp.concatenate([w_low[i, :, lanes] for i in order], axis=1)

        def body(index, carry):
            here = pl.ds(pl.multiple_of(index * QB, QB), QB)
            there = pl.ds(pl.multiple_of(index * QB + rows, QB), QB)
            high = jnp.concatenate([d_kv[there, 0:256], d_q2[here, 0:128]], axis=1)
            low = jnp.concatenate([d_kv[there, 256:512], d_q2[here, 128:256]], axis=1)
            result = dot_nt(high, high_w) + dot_nt(high, low_w) + dot_nt(low, high_w)
            on_own[here, :] += result
            return carry

        lax.fori_loop(0, 4, body, 0)

    def weight_grads(pair):
        each = count // 2
        size = each * shard

        def body(index, carry):
            here = pl.ds(pl.multiple_of(index * size, size), size)
            high, low = xt_high[here, :], xt_low[here, :]
            first_kv = dot(high, d_kv[...])
            kv = first_kv[:, :256] + first_kv[:, 256:] + dot(low, d_kv[:, 0:256])
            high, low = high[:, rows:], low[:, rows:]
            first_q = dot(high, d_q2[...])
            query = first_q[:, :128] + first_q[:, 128:] + dot(low, d_q2[:, 0:128])
            for slot in range(each):
                part = slice(slot * shard, slot * shard + shard)
                qkv_g[pair, 0, index * each + slot] = query[part]
                qkv_g[pair, 1, index * each + slot] = kv[part, :128]
                qkv_g[pair, 2, index * each + slot] = kv[part, 128:]
            return carry

        lax.fori_loop(0, 2, body, 0)

    sums_q, sums_v = [], []
    down(0, 0)
    send(0, 3)
    send(0, 2)
    on_own[pl.ds(own, own), :] = jnp.zeros((own, width), F32)
    for pair in range(pairs):
        for copy in stage(pair):
            copy.wait()
        prepare(pair)
        if pair + 1 < pairs:
            for copy in stage(pair + 1):
                copy.start()
        attend(pair)
        run(TRANSFERS.get((pair, 4), []))
        divide()
        sums_q.append(jnp.sum(d_q[...], axis=0, keepdims=True))
        sums_v.append(jnp.sum(d_v[...], axis=0, keepdims=True))
        if pair == 0:
            first_copy.wait()
        if pair + 1 < pairs:
            weight_grads(pair)
            qkv_begin(pair)
            to_prompt(pair)
            to_own(pair)

    def swap(src, dst, index):
        return remote(src, dst, t_send.at[index], t_recv.at[index], partner(0, 1))

    last = pairs - 1
    to_prompt(last)
    prompt_swap = swap(on_prompt.at[pl.ds(own, own)], prompt_in, 0)
    go(lambda: prompt_swap)
    go(qkv_cross, 0)
    go(cross, 0)
    weight_grads(last)
    qkv_begin(last)
    prompt_swap.wait_recv()
    on_prompt[pl.ds(0, own), :] += prompt_in[...]
    far = remote(on_prompt.at[pl.ds(0, own)], far_in, t_send.at[1], t_recv.at[1], partner(0, 2))

    @pl.when(group == 1)
    def _():
        far.start()

    qkv(1, 3)
    qkv(1, 2)
    to_own(last)
    own_swap = swap(on_own.at[pl.ds(own, own)], grad_in, 2)
    go(lambda: own_swap)

    bias_q = jnp.concatenate(sums_q, axis=1)
    bias_v = jnp.concatenate(sums_v, axis=1)
    bias = jnp.concatenate([bias_q, bias_v, jnp.zeros((6, half), F32)], axis=0)
    nothing = jnp.zeros((8, half), F32)
    bias = jnp.where(
        role == 0,
        jnp.concatenate([bias, nothing], axis=1),
        jnp.concatenate([nothing, bias], axis=1),
    )
    inside = lane_ids((8, 128)) < shard
    for slot in range(count):
        turned = pltpu.roll(bias, (width - shard * slot) % width, 1) if slot else bias
        sm[slot] = small_ref[slot]
        sm[slot, pl.ds(0, 8), :] += jnp.where(inside, turned[:, :128], 0.0)

    def small_step(relative, hop):
        index = relative ^ (1 << hop)
        place = (1 << hop) + index
        return remote(
            sm.at[me ^ slot_mask(bits, relative)], sm_in.at[place], s_send.at[relative],
            s_recv.at[place], partner(masks[hop], 0),
        )

    for relative in reversed(range(count // 2, count)):
        go(small_step, relative, bits - 1)
    second(1, 3)
    second(1, 2)
    qkv(1, 1)
    qkv(last, 3)
    qkv(last, 2)
    qkv(1, 0)
    go(qkv_cross, 1)
    second(1, 1)
    second(1, 0)
    go(cross, 1)
    qkv_finish(0)
    for relative in reversed(range(count // 2)):
        top = relative.bit_length() - 1
        slot = me ^ slot_mask(bits, relative)
        for hop in reversed(range(top + 1, bits)):
            small_step(relative | (1 << hop), hop).wait_recv()
            sm[slot] += sm_in[(1 << hop) + relative]
        if relative:
            go(small_step, relative, top)
    small_x = remote(sm.at[me], sm_x, sx_send.at[0], sx_recv.at[0], partner(0, 2))
    go(lambda: small_x)
    for kind in range(2):
        kinds[kind][9][group] = kinds[kind][7][0]
        cross_in(kind).wait_recv()
        go(hand, kind)
    qkv_finish(1)
    small_x.wait_recv()
    small_out[...] = sm[me] + sm_x[...]
    small_pair = remote(small_out, sm_pair, sx_send.at[1], sx_recv.at[1], partner(0, 1))
    go(lambda: small_pair)
    qkv(last, 1)
    qkv(last, 0)
    go(qkv_cross, last)
    own_swap.wait_recv()
    grad_in[...] += on_own[pl.ds(0, own), :]
    qkv_finish(last)

    @pl.when(group == 0)
    def _():
        far.wait_recv()
        grad_in[...] += on_prompt[pl.ds(0, own), :] + far_in[...]

    small_pair.wait_recv()
    for kind in range(2):
        hand(kind).wait_recv()
    down_step(3, 0).wait_recv()
    for pair in range(pairs):
        qkv_hand(pair).wait_recv()
    for make, which in started:
        make(*which).wait_send()
    small_out[...] += sm_pair[...]

    @pl.when(group == 1)
    def _():
        far.wait_send()


def run_backward(lens, lse, xt_high, xt_low, w_high, w_low, small, q, k, v, o, g, first_grad,
                 up_grads, out_grads, down_grads):
    bits = dp_bits()
    count = 1 << bits
    layers = count // 2
    anywhere = pl.BlockSpec(memory_space=pl.ANY)
    vmem = pl.BlockSpec(memory_space=pltpu.VMEM)
    width, both_rows = xt_high.shape
    rows, half = q.shape
    own = rows // 2
    pairs = half // 128
    shard = width // count
    shape = lambda *dims: jax.ShapeDtypeStruct(dims, F32)
    space = lambda *dims: pltpu.VMEM(dims, F32)
    short = lambda *dims: pltpu.VMEM(dims, BF)
    dma = lambda *dims: pltpu.SemaphoreType.DMA(dims)

    def buffers(unit):
        return [
            space(layers, 2, 2, *unit),
            space(layers, 2, 1, *unit),
            space(layers, 2, 2, *unit),
            space(layers, 2, *unit),
            space(layers, 2, 1, *unit),
            space(layers, 1, *unit),
            space(layers, 3, *unit),
            space(layers, 3, *unit),
        ]

    up_unit, out_unit = up_grads.shape[3:], out_grads.shape[3:]
    tiny = small.shape[1:]
    return pl.pallas_call(
        functools.partial(backward_all_kernel, bits),
        in_specs=[pl.BlockSpec(memory_space=pltpu.SMEM)] + [vmem] * 6 + [anywhere] * 9,
        out_specs=[vmem] * 10,
        out_shape=[
            shape(own, width),
            shape(2, 3, *up_unit),
            shape(2, 3, *up_unit),
            shape(2, 3, *out_unit),
            shape(2, 3, *out_unit),
            shape(2, *down_grads.shape[2:]),
            shape(2, *down_grads.shape[2:]),
            shape(pairs, 3, shard, 128),
            shape(pairs, 3, shard, 128),
            shape(*tiny),
        ],
        scratch_shapes=[
            space(*down_grads.shape[1:]),
            space(*down_grads.shape[2:]),
            space(*down_grads.shape[1:]),
            space(rows, 128),
            space(both_rows, 128),
            space(both_rows, 128),
            space(rows, 128),
            space(rows, 128),
            short(2, rows, 256),
            short(2, rows, 256),
            short(2, rows, 128),
            short(2, rows, 128),
            short(2, rows, 128),
            short(2, rows, 128),
            short(2, rows, 128),
            short(2, rows, 128),
            short(2, 128, rows),
            short(2, 128, rows),
            space(2, 8, rows),
            space(rows, 128),
            space(both_rows, 128),
            space(both_rows, 128),
            short(both_rows, 512),
            short(rows, 256),
            space(rows, width),
            space(rows, width),
            space(own, width),
            space(own, width),
        ]
        + buffers(up_unit)
        + buffers(out_unit)
        + [
            space(pairs, 3, count, shard, 128),
            space(pairs, count, 3, shard, 128),
            space(pairs, 3, shard, 128),
            space(count, *tiny),
            space(count, *tiny),
            space(*tiny),
            space(*tiny),
            dma(7),
            dma(2, layers, 3),
            dma(2, layers, 5),
            dma(2, layers, 5),
            dma(2, layers),
            dma(2, layers),
            dma(2, 2),
            dma(2, 2),
            dma(pairs, count),
            dma(pairs, count),
            dma(pairs, 2),
            dma(pairs, 2),
            dma(count),
            dma(count),
            dma(2),
            dma(2),
            dma(3),
            dma(3),
            dma(4),
            dma(4),
        ],
        compiler_params=pltpu.CompilerParams(
            collective_id=3, has_side_effects=True, vmem_limit_bytes=67043328
        ),
        name="attention_backward_and_scatter",
    )(lens, lse, xt_high, xt_low, w_high, w_low, small, q, k, v, o, g, first_grad, up_grads, out_grads,
      down_grads)


def norm_forward(resid, gain, shift):
    center = resid - jnp.mean(resid, axis=-1, keepdims=True)
    inverse = lax.rsqrt(jnp.mean(center * center, axis=-1, keepdims=True) + EPSILON)
    normed = center * inverse
    return normed * gain + shift, normed, inverse


def norm_backward(grad_out, normed, inverse, gain):
    grad_normed = grad_out * gain
    first_term = jnp.mean(grad_normed, axis=-1, keepdims=True)
    second_term = jnp.mean(grad_normed * normed, axis=-1, keepdims=True)
    grad_resid = inverse * (grad_normed - first_term - normed * second_term)
    return grad_resid, jnp.sum(grad_out * normed, axis=0), jnp.sum(grad_out, axis=0)


def on_device(
    hidden_in,
    teacher,
    lengths,
    qkv_weight,
    qkv_bias,
    out_weight,
    out_bias,
    ln_gain,
    ln_shift,
    ffn_in,
    ffn_in_bias,
    ffn_out,
):
    _, rows, width = hidden_in.shape
    dp_count = lax.axis_size("dp")
    dp_index = lax.axis_index("dp")
    seq_index = lax.axis_index("seq")
    group, role = seq_index // 2, seq_index % 2
    total_tokens = dp_count * rows * SEQ
    shard = qkv_weight.shape[1]
    half = width // 2
    ffn = ffn_in.shape[1]
    ffn_shard = ffn // dp_count
    ffn_half = ffn_shard // 2

    x_own = hidden_in.reshape(rows, width)
    target = teacher.reshape(rows, width)
    lens = lengths.reshape(CONT)

    length_sum = jnp.sum(lens).astype(F32)
    lanes = lambda value: jnp.pad(value, ((0, 0), (0, 128 - value.shape[1])))
    up_rows = -(-ffn_shard // 128)
    up_bias = jnp.pad(ffn_in_bias, (0, up_rows * 128 - ffn_shard)).reshape(up_rows, 128)
    small_rows = -(-(9 + up_rows) // 8) * 8
    small = jnp.concatenate(
        [
            lanes(qkv_bias),
            lanes(out_bias),
            lanes(ln_gain),
            lanes(ln_shift),
            up_bias,
            jnp.full((small_rows - 8 - up_rows, 128), length_sum, F32),
        ]
    )
    local_lens = jnp.where(role == 0, lens, jnp.roll(lens, CONT // 2))
    local_lens = jnp.where(group == 0, 0, local_lens)
    out_half = shard // 2
    up_piece = pick(ffn_in.reshape(shard, dp_count, 2, ffn_half), role, 2)
    out_piece = pick(out_weight.reshape(2, out_half, width), role, 0)
    down_piece = pick(ffn_out.reshape(2, ffn_half, width), role, 0)
    (w_high, w_low, small, xt_high, xt_low, k_both, v_both, queries, attended, lse,
     out_blocks, w_up, w_down, out_other) = run_forward(
        local_lens,
        lax.dynamic_slice_in_dim(qkv_weight, role * half, half, 2),
        small,
        x_own,
        out_piece.reshape(2, 3, out_half // 6, width),
        up_piece.reshape(2, 3, shard // 6, ffn // 2),
        down_piece.reshape(2, 3, ffn_half // 6, width),
    )
    w_up = w_up.reshape(width, ffn // 2)
    w_down = w_down.reshape(ffn // 2, width)
    out_mine = pick(out_blocks.reshape(2, dp_count // 2, out_half, width), role, 0)
    out_other = out_other.reshape(dp_count // 2, out_half, width)
    w_out = ordered(role, out_mine[:, None], out_other[:, None], 1).reshape(half, width)
    vectors = small[:, :8, :shard].transpose(1, 0, 2).reshape(4, 2, width)
    b_out, gains, shifts = vectors[1], vectors[2], vectors[3]
    b_up = small[:, 8 : 8 + up_rows].reshape(dp_count, up_rows * 128)[:, :ffn_shard]
    b_up = pick(b_up.reshape(dp_count, 2, ffn_half), role, 1).reshape(ffn // 2)
    count = float(dp_count * PROMPT) + jnp.sum(small[:, small_rows - 1, 0])

    def reduce_pair(partial):
        return partial[:rows] + swap_pair(partial[rows:])

    def both_halves(own):
        return jnp.concatenate([own, swap_pair(own)], axis=0)

    first_resid = x_own + reduce_pair(mm(attended, w_out)) + b_out[0]
    first_norm, first_hat, first_inv = norm_forward(first_resid, gains[0], shifts[0])
    norm_group = both_halves(first_norm)
    pre_act = mm(norm_group, w_up) + b_up
    normal_cdf = 0.5 * (1.0 + lax.erf(pre_act * INV_ROOT_TWO))
    activated = pre_act * normal_cdf
    slope = normal_cdf + pre_act * jnp.exp(-0.5 * pre_act * pre_act) * INV_ROOT_TAU
    second_resid = first_norm + reduce_pair(mm(activated, w_down)) + b_out[1]
    final, second_hat, second_inv = norm_forward(second_resid, gains[1], shifts[1])

    slot = seq_index * rows + jnp.arange(rows, dtype=jnp.int32) - PROMPT
    own_len = jnp.sum(
        jnp.where((slot // CLEN)[None] == jnp.arange(CONT, dtype=jnp.int32)[:, None], lens[:, None], 0),
        axis=0,
    )
    valid = ((slot < 0) | (slot % CLEN < own_len)).astype(F32)
    difference = (final - target) * valid[:, None]
    squares = jnp.sum(difference * difference)
    grad_final = difference * (total_tokens / count)
    grad_second, grad_gain_two, grad_shift_two = norm_backward(
        grad_final, second_hat, second_inv, gains[1]
    )
    grad_bias_down = jnp.sum(grad_second, axis=0)
    second_group = both_halves(grad_second)
    grad_w_down = mm_tn(activated, second_group)
    ybit = dp_index & 1
    early = dp_count <= 8
    if early:
        down = grad_w_down.reshape(dp_count // 2, 2, 2, 2, ffn_half // 4, width)
        down_a, down_b = down[:, :, :, 0], down[:, :, :, 1]
        send_a, send_b = pick(down_a, ybit ^ 1, 1), pick(down_b, group ^ 1, 2)
        keep_a, keep_b = pick(down_a, ybit, 1), pick(down_b, group, 2)
        second_group, send_a, send_b = lax.optimization_barrier((second_group, send_a, send_b))
        come_a, come_b = swap_dp(send_a, 0), swap_group(send_b)
    grad_pre = mm_nt(second_group, w_down) * slope
    grad_b_up = jnp.sum(grad_pre, axis=0)
    grad_w_up = mm_tn(norm_group, grad_pre)
    if early:
        grad_w_up, come_a, come_b = lax.optimization_barrier((grad_w_up, come_a, come_b))
        down_a, down_b = keep_a + come_a, keep_b + come_b
        send_a, send_b = pick(down_a, group ^ 1, 1), pick(down_b, ybit ^ 1, 1)
        keep_a, keep_b = pick(down_a, group, 1), pick(down_b, ybit, 1)
        grad_pre, send_a, send_b = lax.optimization_barrier((grad_pre, send_a, send_b))
        come_a, come_b = swap_group(send_a), swap_dp(send_b, 0)
    if not early:
        share_down = scatter_rows(grad_w_down)
    grad_first_norm = grad_second + reduce_pair(mm_nt(grad_pre, w_up))
    grad_first, grad_gain_one, grad_shift_one = norm_backward(
        grad_first_norm, first_hat, first_inv, gains[0]
    )
    grad_bias_out = jnp.sum(grad_first, axis=0)
    first_group = both_halves(grad_first)
    grad_attended = mm_nt(first_group, w_out)
    if early:
        grad_attended, come_a, come_b = lax.optimization_barrier((grad_attended, come_a, come_b))
        half_down = jnp.stack([keep_a + come_a, keep_b + come_b], axis=1)
        half_down = half_down.reshape(2, dp_count // 4, 2, ffn_half // 4, width)
    grad_w_out = mm_tn(attended, first_group)
    mine = grad_w_out.reshape(dp_count // 2, 2, out_half, width)
    received = swap_pair(pick(mine, 1 - role, 1))
    mine = ordered(role, pick(mine, role, 1), received, 0)
    up = jnp.zeros((dp_count, 2, ffn_half), F32)
    up = lax.dynamic_update_slice(up, grad_b_up.reshape(dp_count, 1, ffn_half), (0, role, 0))
    up = jnp.pad(up.reshape(dp_count, ffn_shard), ((0, 0), (0, up_rows * 128 - ffn_shard)))

    def small_block(bias_q, bias_v):
        vectors = jnp.stack(
            [
                bias_q,
                bias_v,
                grad_bias_out,
                grad_bias_down,
                grad_gain_one,
                grad_gain_two,
                grad_shift_one,
                grad_shift_two,
            ]
        )
        vectors = vectors.reshape(8, dp_count, shard).transpose(1, 0, 2)
        return jnp.concatenate(
            [
                jnp.pad(vectors, ((0, 0), (0, 0), (0, 128 - shard))),
                up.reshape(dp_count, up_rows, 128),
                jnp.full((dp_count, small_rows - 8 - up_rows, 128), squares, F32),
            ],
            axis=1,
        )

    def join(share, axis):
        return ordered(role, share, swap_pair(share), axis)

    if early:
        (grad_input, up_mine, up_other, out_mine, out_other, down_mine, down_other,
         qkv_mine, qkv_other, small) = run_backward(
            local_lens, lse, xt_high, xt_low, w_high, w_low,
            small_block(jnp.zeros((width,), F32), jnp.zeros((width,), F32)),
            queries, k_both, v_both, attended, grad_attended, grad_first,
            grad_w_up.reshape(dp_count, 2, 3, shard // 6, ffn // 2),
            mine.reshape(dp_count, 2, 3, out_half // 6, width),
            half_down,
        )
        lay = lambda value: value.transpose(1, 2, 0, 3).reshape(3, shard, half)
        out_qkv = ordered(role, lay(qkv_mine), lay(qkv_other), 2)
        out_out = ordered(
            role, out_mine.reshape(out_half, width), out_other.reshape(out_half, width), 0
        )
        lay = lambda value: value.reshape(shard, dp_count, 1, ffn_half)
        out_up = ordered(role, lay(up_mine), lay(up_other), 2).reshape(shard, ffn)
        out_down = ordered(
            role, down_mine.reshape(ffn_half, width), down_other.reshape(ffn_half, width), 0
        )
    else:
        share_up = scatter_rows(grad_w_up)
        d_q, d_kp, d_vp, d_ks, d_vs = attend_backward(
            local_lens, queries, k_both, v_both, attended, grad_attended, lse
        )
        weights = w_high.astype(F32) + w_low.astype(F32)
        w_q, w_k, w_v = weights[0], weights[1], weights[2]
        x_t = xt_high.astype(F32) + xt_low.astype(F32)
        on_prompt = reduce_pair(mm_nt(d_kp, w_k) + mm_nt(d_vp, w_v))
        from_cont = lax.ppermute(on_prompt, "seq", [(2, 0), (3, 1)])
        grad_w_k = mm(x_t, jnp.concatenate([d_kp, d_ks], axis=0))
        grad_w_v = mm(x_t, jnp.concatenate([d_vp, d_vs], axis=0))
        grad_w_q = mm(x_t[:, 2 * rows :], d_q)
        on_own = reduce_pair(mm_nt(d_q, w_q) + mm_nt(d_ks, w_k) + mm_nt(d_vs, w_v))
        grad_input = grad_first + on_own + jnp.where(group == 0, on_prompt + from_cont, 0.0)

        def widen(value):
            return lax.dynamic_update_slice(jnp.zeros((width,), F32), value, (role * half,))

        share_qkv, share_out, small, other_qkv, other_out = scatter_all(
            jnp.stack([grad_w_q, grad_w_k, grad_w_v]).reshape(3, dp_count, shard, half),
            mine.reshape(dp_count, out_half, width),
            small_block(
                widen(jnp.sum(d_q, axis=0)),
                widen(jnp.sum(d_vp, axis=0) + jnp.sum(d_vs, axis=0)),
            ),
        )
        out_qkv = ordered(role, share_qkv, other_qkv, 2)
        out_out = ordered(role, share_out, other_out, 0)
        out_up = join(share_up.reshape(shard, dp_count, 1, ffn_half), 2).reshape(shard, ffn)
        out_down = join(share_down.reshape(ffn_half, width), 0)
    pairs = small[:8, :shard].reshape(4, 2, shard)
    out_b_up = small[8 : 8 + up_rows].reshape(up_rows * 128)[:ffn_shard]
    loss = small[small_rows - 1, 0] / (count * width)
    return (
        final[None],
        grad_input[None],
        out_qkv,
        pairs[0],
        out_out,
        pairs[1],
        pairs[2],
        pairs[3],
        out_up,
        out_b_up,
        out_down,
        loss,
    )


def solution(mesh):
    return jax.shard_map(
        on_device,
        mesh=mesh,
        in_specs=(
            P("dp", "seq", None),
            P("dp", "seq", None),
            P("dp", None),
            P(None, "dp", None),
            P(None, "dp"),
            P("dp", None),
            P(None, "dp"),
            P(None, "dp"),
            P(None, "dp"),
            P("dp", None),
            P("dp"),
            P("dp", None),
        ),
        out_specs=(
            P("dp", "seq", None),
            P("dp", "seq", None),
            P(None, "dp", None),
            P(None, "dp"),
            P("dp", None),
            P(None, "dp"),
            P(None, "dp"),
            P(None, "dp"),
            P("dp", None),
            P("dp"),
            P("dp", None),
            P(),
        ),
        check_vma=False,
    )
```

```python
import functools

import jax
import jax.numpy as jnp
from jax import lax
from jax.experimental import pallas as pl
from jax.experimental.pallas import tpu as pltpu
from jax.sharding import PartitionSpec as P

HD = 64
PROMPT = 1024
CONT = 8
CLEN = 128
SEQ = 4
QB = 256

HIGH = lax.Precision.HIGH
EPSILON = 1e-05
MASKED = -1e30
INV_ROOT_TWO = 0.7071067811865476
INV_ROOT_TAU = 0.3989422804014327
BF = jnp.bfloat16
F32 = jnp.float32


def mm(left, right):
    return lax.dot_general(
        left, right, (((1,), (0,)), ((), ())), precision=HIGH, preferred_element_type=F32
    )


def mm_nt(left, right):
    return lax.dot_general(
        left, right, (((1,), (1,)), ((), ())), precision=HIGH, preferred_element_type=F32
    )


def mm_tn(left, right):
    return lax.dot_general(
        left, right, (((0,), (0,)), ((), ())), precision=HIGH, preferred_element_type=F32
    )


def swap_pair(value):
    return lax.ppermute(value, "seq", [(i, i ^ 1) for i in range(SEQ)])


def swap_group(value):
    return lax.ppermute(value, "seq", [(i, i ^ 2) for i in range(SEQ)])


def swap_dp(value, bit):
    count = lax.axis_size("dp")
    return lax.ppermute(value, "dp", [(i, i ^ (1 << bit)) for i in range(count)])


def ordered(bit, own, other, axis):
    first = jnp.where(bit == 0, own, other)
    second = jnp.where(bit == 0, other, own)
    return jnp.concatenate([first, second], axis=axis)


def pick(value, index, axis):
    return lax.dynamic_index_in_dim(value, index, axis, keepdims=False)


def dp_bits():
    return lax.axis_size("dp").bit_length() - 1


def gather_rows(piece, axis=0):
    return lax.all_gather(piece, "dp", axis=axis, tiled=True)


def scatter_rows(grads, axis=0):
    share = lax.psum_scatter(grads, "dp", scatter_dimension=axis, tiled=True)
    return share + swap_group(share)


def partner(dp_mask, seq_mask):
    return (lax.axis_index("dp") ^ dp_mask, lax.axis_index("seq") ^ seq_mask)


def remote(src, dst, send_sem, recv_sem, target):
    return pltpu.make_async_remote_copy(
        src_ref=src,
        dst_ref=dst,
        send_sem=send_sem,
        recv_sem=recv_sem,
        device_id=target,
        device_id_type=pl.DeviceIdType.MESH,
    )


def greet(bits):
    barrier = pltpu.get_barrier_semaphore()
    others = [partner(1 << bit, 0) for bit in range(bits)] + [partner(0, 1), partner(0, 2)]
    for other in others:
        pl.semaphore_signal(
            barrier, inc=1, device_id=other, device_id_type=pl.DeviceIdType.MESH
        )
    pl.semaphore_wait(barrier, len(others))


def greet_line(has_up, has_down, above, below):
    barrier = pltpu.get_barrier_semaphore()

    def hello(other):
        pl.semaphore_signal(
            barrier, inc=1, device_id=other, device_id_type=pl.DeviceIdType.MESH
        )

    for other in (partner(1, 0), partner(0, 1), partner(0, 2)):
        hello(other)
    for there, other in ((has_up, above), (has_down, below)):
        @pl.when(there)
        def _(other=other):
            hello(other)
    ends = jnp.where(has_up, 1, 0) + jnp.where(has_down, 1, 0)
    pl.semaphore_wait(barrier, 3 + ends)


def line_arrival(level, layers, index):
    both_sides = jnp.minimum(level, layers - 1 - level)
    paired = index <= 2 * both_sides
    distance = jnp.where(paired, (index + 1) // 2, index - both_sides)
    upward = jnp.where(paired, index % 2 == 0, level < layers - 1 - level)
    return jnp.where(upward, level + distance, level - distance)


def hop_masks(bits):
    return [1 << bit for bit in range(1, bits)] + [1]


def slot_mask(bits, relative):
    masks = hop_masks(bits)
    return sum(masks[p] for p in range(bits) if relative >> p & 1)


def scatter_kernel(bits, *refs):
    kinds = 3
    grads, refs = refs[:kinds], refs[kinds:]
    mine, refs = refs[:kinds], refs[kinds:]
    other, refs = refs[: kinds - 1], refs[kinds - 1 :]
    acc, refs = refs[:kinds], refs[kinds:]
    hop_in, refs = refs[:kinds], refs[kinds:]
    x_in, refs = refs[:kinds], refs[kinds:]
    pair_in, send_sem, recv_sem, x_send, x_recv, load_sem, store_sem = refs
    me = lax.axis_index("dp")
    masks = hop_masks(bits)
    count = 1 << bits

    def source(kind, relative):
        slot = me ^ slot_mask(bits, relative)
        return grads[kind].at[:, slot] if kind == 0 else grads[kind].at[slot]

    def hop_copy(kind, relative, hop, from_input):
        index = relative ^ (1 << hop)
        src = source(kind, relative) if from_input else acc[kind].at[relative]
        place = (1 << hop) + index
        return remote(
            src, hop_in[kind].at[place], send_sem.at[kind, relative], recv_sem.at[kind, place],
            partner(masks[hop], 0),
        )

    loads = {}
    for relative in reversed(range(count // 2)):
        for kind in range(kinds):
            copy = pltpu.make_async_copy(
                source(kind, relative), acc[kind].at[relative], load_sem.at[kind, relative]
            )
            copy.start()
            loads[kind, relative] = copy
    greet(bits)
    started = []
    last = bits - 1
    for relative in reversed(range(count // 2, count)):
        for kind in range(kinds):
            copy = hop_copy(kind, relative, last, True)
            copy.start()
            started.append(copy)
    for relative in reversed(range(count // 2)):
        for kind in range(kinds):
            loads[kind, relative].wait()
        lowest = relative.bit_length() - 1
        for hop in reversed(range(max(lowest + 1, 0), bits)):
            for kind in range(kinds):
                hop_copy(kind, relative | (1 << hop), hop, hop == last).wait_recv()
                acc[kind][relative] += hop_in[kind][(1 << hop) + relative]
        if relative:
            for kind in range(kinds):
                copy = hop_copy(kind, relative, lowest, False)
                copy.start()
                started.append(copy)
    crossing = []
    for kind in range(kinds):
        copy = remote(acc[kind].at[0], x_in[kind], x_send.at[kind], x_recv.at[kind], partner(0, 2))
        copy.start()
        crossing.append(copy)
    for kind in range(kinds):
        crossing[kind].wait_recv()
        mine[kind][...] = acc[kind][0] + x_in[kind][...]
    handing = []
    for kind in range(kinds - 1):
        copy = remote(
            mine[kind], other[kind], x_send.at[kinds + kind], x_recv.at[kinds + kind], partner(0, 1)
        )
        copy.start()
        handing.append(copy)
    copy = remote(
        mine[kinds - 1], pair_in, x_send.at[2 * kinds - 1], x_recv.at[2 * kinds - 1], partner(0, 1)
    )
    copy.start()
    handing.append(copy)
    for copy in handing:
        copy.wait()
    mine[kinds - 1][...] += pair_in[...]
    for copy in started + crossing:
        copy.wait_send()


def scatter_all(qkv, out, small):
    bits = dp_bits()
    count = 1 << bits
    any_spec = pl.BlockSpec(memory_space=pl.ANY)
    vmem = pl.BlockSpec(memory_space=pltpu.VMEM)
    shapes = [(qkv.shape[0],) + qkv.shape[2:], out.shape[1:], small.shape[1:]]
    like = [jax.ShapeDtypeStruct(shape, F32) for shape in shapes]
    return pl.pallas_call(
        functools.partial(scatter_kernel, bits),
        in_specs=[any_spec] * 3,
        out_specs=[vmem] * 5,
        out_shape=like + like[:2],
        scratch_shapes=[pltpu.VMEM((count // 2,) + shape, F32) for shape in shapes]
        + [pltpu.VMEM((count,) + shape, F32) for shape in shapes]
        + [pltpu.VMEM(shape, F32) for shape in shapes]
        + [
            pltpu.VMEM(shapes[2], F32),
            pltpu.SemaphoreType.DMA((3, count)),
            pltpu.SemaphoreType.DMA((3, count)),
            pltpu.SemaphoreType.DMA((6,)),
            pltpu.SemaphoreType.DMA((6,)),
            pltpu.SemaphoreType.DMA((3, count // 2)),
            pltpu.SemaphoreType.DMA((1,)),
        ],
        compiler_params=pltpu.CompilerParams(
            collective_id=2, has_side_effects=True, vmem_limit_bytes=40 << 20
        ),
        cost_estimate=pl.CostEstimate(
            flops=0, bytes_accessed=(qkv.size + out.size) * 4 * 12, transcendentals=0
        ),
        name="scatter_attention_grads",
    )(qkv, out, small)


def lane_ids(shape):
    return lax.broadcasted_iota(jnp.int32, shape, 1)


def high_low(value):
    high = value.astype(BF).astype(F32)
    return high, value - high


def packs(value, head):
    high, low = high_low(value)
    left = lane_ids(value.shape) < HD
    high_r = pltpu.roll(high, HD, 1)
    low_r = pltpu.roll(low, HD, 1)
    if head == 0:
        return (
            jnp.where(left, high, low_r).astype(BF),
            jnp.where(left, high, high_r).astype(BF),
            jnp.where(left, low, low_r).astype(BF),
        )
    return (
        jnp.where(left, high_r, low).astype(BF),
        jnp.where(left, high_r, high).astype(BF),
        jnp.where(left, low_r, low).astype(BF),
    )


def dot(left, right):
    return lax.dot_general(left, right, (((1,), (0,)), ((), ())), preferred_element_type=F32)


def dot_nt(left, right):
    return lax.dot_general(left, right, (((1,), (1,)), ((), ())), preferred_element_type=F32)


def split(value):
    high = value.astype(BF)
    return high, (value - high.astype(F32)).astype(BF)


def self_mask(lens_ref, block, query_axis):
    key_axis = 1 - query_axis
    query = lax.broadcasted_iota(jnp.int32, (QB, QB), query_axis)
    key = lax.broadcasted_iota(jnp.int32, (QB, QB), key_axis)
    per = QB // CLEN
    seen = jnp.zeros((QB, QB), jnp.bool_)
    for piece in range(per):
        low = piece * CLEN
        limit = low + lens_ref[block * per + piece]
        inside = (query >= low) & (query < low + CLEN) & (key >= low) & (key < limit)
        seen = seen | inside
    return seen & (key <= query)


THIRDS = ((0, 1), (1, 2))


def forward_kernel(bits, lens_ref, w_ref, s_ref, x_ref, out_ref, up_ref, down_ref,
                   w_high, w_low, s_all, xt_high, xt_low, k_both, v_both, q_all, o_all, lse_all,
                   out_all, up_all, down_all, out_other,
                   w_all, x_both, x_high, x_low, q4, k4p, k4s, v2p, v2s,
                   out_buf, up_buf, down_buf,
                   send_sem, recv_sem, x_send, x_recv, own_sem, hop_send, hop_recv, pair_sem):
    me = lax.axis_index("dp")
    seq = lax.axis_index("seq")
    group, role = seq // 2, seq % 2
    rows, width = x_ref.shape
    half = w_ref.shape[2]
    layers = 1 << (bits - 1)
    quarter = layers // 4
    level, side = me // 2, me % 2
    has_up, has_down = level < layers - 1, level > 0
    above, below = (me + 2, seq), (me - 2, seq)
    greet_line(has_up, has_down, above, below)
    arrival = functools.partial(line_arrival, level, layers)

    pieces = ((out_ref, out_buf, out_all), (up_ref, up_buf, up_all), (down_ref, down_buf, down_all))
    loads = [pltpu.make_async_copy(src, buf, own_sem.at[i]) for i, (src, buf, _) in enumerate(pieces)]
    own_w = pltpu.make_async_copy(w_ref, w_all.at[:, me], own_sem.at[3])
    own_s = pltpu.make_async_copy(s_ref, s_all.at[me], own_sem.at[4])
    own_x = pltpu.make_async_copy(x_ref, x_both.at[pl.ds(2 * rows, rows)], own_sem.at[5])
    for copy in loads + [own_w, own_s, own_x]:
        copy.start()
    to_pair = remote(
        x_ref, x_both.at[pl.ds(3 * rows, rows)], x_send.at[0], x_recv.at[0], partner(0, 1)
    )
    to_far = remote(x_ref, x_both.at[pl.ds(0, rows)], x_send.at[1], x_recv.at[1], partner(0, 2))
    far_pair = remote(
        x_both.at[pl.ds(0, rows)], x_both.at[pl.ds(rows, rows)], x_send.at[2], x_recv.at[2],
        partner(0, 1),
    )
    to_pair.start()

    @pl.when(group == 0)
    def _():
        to_far.start()

    def attention_copies(slot, step, from_input=False):
        target = (above, below, partner(1, 0))[step]
        regions = (w_all.at[:, slot], s_all.at[slot])
        return [
            remote(
                (w_ref, s_ref)[kind] if from_input else region, region,
                send_sem.at[kind, slot, step], recv_sem.at[kind, slot], target,
            )
            for kind, region in enumerate(regions)
        ]

    def along(at, upward, downward):
        @pl.when((at <= level) & has_up)
        def _():
            upward()

        @pl.when((at >= level) & has_down)
        def _():
            downward()

    def starts(slot, step, from_input=False):
        for copy in attention_copies(slot, step, from_input):
            copy.start()

    def sends(slot, step):
        for copy in attention_copies(slot, step):
            copy.wait_send()

    along(level, lambda: starts(me, 0, True), lambda: starts(me, 1, True))
    starts(me, 2, True)
    for copy in loads:
        copy.wait()
    stores = [pltpu.make_async_copy(buf, dst.at[me], own_sem.at[i]) for i, (_, buf, dst) in enumerate(pieces)]
    for copy in stores:
        copy.start()

    def part(kind, layer, last, other_x, piece):
        first, count = THIRDS[piece]
        return pieces[kind][2].at[
            layer * 2 + (side ^ last), group ^ other_x, pl.ds(first, count)
        ]

    def sent(kind, layer, last, other_x, piece, step, dp_mask, seq_mask):
        region = part(kind, layer, last, other_x, piece)
        return remote(
            region, region, hop_send.at[kind, layer, step], hop_recv.at[kind, layer, step],
            partner(dp_mask, seq_mask),
        )

    steps = {
        1: (0, 0, 0, 0, 2),
        2: (0, 0, 0, 1, 0),
        3: (0, 1, 0, 1, 0),
        4: (0, 0, 1, 1, 0),
        5: (0, 0, 1, 0, 2),
        6: (1, 0, 1, 0, 2),
    }

    def give(kind, layer, step):
        last, other_x, piece, dp_mask, seq_mask = steps[step]
        return sent(kind, layer, last, other_x, piece, step, dp_mask, seq_mask)

    def take(kind, layer, step):
        last, other_x, piece, dp_mask, seq_mask = steps[step]
        return sent(
            kind, layer, last ^ dp_mask, other_x ^ (seq_mask // 2), piece, step, dp_mask, seq_mask
        )

    def climb(kind, layer, upward):
        region = pieces[kind][2].at[layer * 2 + side, group]
        return remote(
            region, region, hop_send.at[kind, layer, 0 if upward else 7],
            hop_recv.at[kind, layer, 0], above if upward else below,
        )

    def pass_on(kind, layer):
        along(
            layer, lambda: climb(kind, layer, True).start(), lambda: climb(kind, layer, False).start()
        )

    def spread(kind, index):
        layer = arrival(index)

        @pl.when(index > 0)
        def _():
            climb(kind, layer, True).wait_recv()
            pass_on(kind, layer)
            give(kind, layer, 1).start()
            give(kind, layer, 5).start()

        give(kind, layer, 2).start()
        give(kind, layer, 4).start()

    def relay(kind, index):
        layer = arrival(index)

        @pl.when(index > 0)
        def _():
            take(kind, layer, 1).wait_recv()

        give(kind, layer, 3).start()
        take(kind, layer, 4).wait_recv()
        give(kind, layer, 6).start()

    def settle(kind, layer):
        take(kind, layer, 2).wait_recv()
        take(kind, layer, 3).wait_recv()
        take(kind, layer, 6).wait_recv()

        @pl.when(layer != level)
        def _():
            take(kind, layer, 5).wait_recv()

    def drained(kind, layer):
        @pl.when(layer != level)
        def _():
            give(kind, layer, 1).wait_send()
            give(kind, layer, 5).wait_send()

        for step in (2, 3, 4, 6):
            give(kind, layer, step).wait_send()
        along(
            layer,
            lambda: climb(kind, layer, True).wait_send(),
            lambda: climb(kind, layer, False).wait_send(),
        )

    def over(action, kind, position):
        def body(index, carry):
            action(kind, position * quarter + index)
            return carry

        lax.fori_loop(0, quarter, body, 0)

    for copy in stores:
        copy.wait()

    def receive(index, carry):
        at = arrival(index)
        slot = at * 2 + side
        for copy in attention_copies(slot, 0):
            copy.wait_recv()
        along(at, lambda: starts(slot, 0), lambda: starts(slot, 1))
        starts(slot, 2)
        return carry

    lax.fori_loop(1, layers, receive, 0)
    for kind in range(3):
        pass_on(kind, level)

    def receive_side(index, carry):
        for copy in attention_copies(arrival(index) * 2 + (side ^ 1), 2):
            copy.wait_recv()
        return carry

    lax.fori_loop(0, layers, receive_side, 0)
    for position in range(4):
        over(spread, 0, position)
    over(spread, 1, 0)

    own_x.wait()
    to_pair.wait_recv()

    @pl.when(group == 1)
    def _():
        to_far.wait_recv()
        far_pair.start()
        far_pair.wait_recv()

    def halves(index, carry):
        here = pl.ds(pl.multiple_of(index * QB, QB), QB)

        @pl.when((group == 0) & (index < 2 * rows // QB))
        def _():
            x_both[here, :] = x_both[pl.ds(pl.multiple_of(index * QB + 2 * rows, QB), QB), :]

        high, low = split(x_both[here, :])
        x_high[here, :] = high
        x_low[here, :] = low
        high, low = split(jnp.transpose(x_both[here, :]))
        xt_high[:, here] = high
        xt_low[:, here] = low
        return carry

    lax.fori_loop(0, 4 * rows // QB, halves, 0)
    own_w.wait()
    own_s.wait()
    count = 1 << bits
    shard = width // count
    for index in range(3):
        for slot in range(count):
            high, low = split(w_all[index, slot])
            w_high[index, pl.ds(slot * shard, shard), :] = high
            w_low[index, pl.ds(slot * shard, shard), :] = low
    bias = jnp.zeros((8, width), F32)
    blank = jnp.zeros((8, width - 128), F32)
    for slot in range(count):
        row = jnp.concatenate([s_all[slot, :8, :], blank], axis=1)
        bias = bias + (pltpu.roll(row, shard * slot, 1) if slot else row)
    bias = jnp.where(role == 0, bias[:2, :half], bias[:2, half:])

    def project(index, here):
        high, low = x_high[here, :], x_low[here, :]
        return (
            dot(high, w_high[index]) + dot(high, w_low[index]) + dot(low, w_high[index])
        )


    def keys_values(index, carry):
        here = pl.ds(pl.multiple_of(index * QB, QB), QB)
        @pl.when(index >= 4)
        def _():
            over(relay, 0, index - 4)

        k_both[here, :] = project(1, here)
        v_both[here, :] = project(2, here) + bias[1:2]
        return carry

    lax.fori_loop(0, 8, keys_values, 0)

    def queries(index, carry):
        here = pl.ds(pl.multiple_of(index * QB, QB), QB)
        @pl.when((index == 0) | (index == 2))
        def _():
            over(spread, 1, 1 + index // 2)

        q_all[here, :] = project(0, pl.ds(pl.multiple_of(index * QB + 2 * rows, QB), QB)) + bias[:1]
        return carry

    lax.fori_loop(0, 4, queries, 0)

    for pair in range(half // 128):
        lanes = pl.ds(pair * 128, 128)
        for head in range(2):
            _, hh, ll = packs(q_all[:, lanes] * 0.125, head)
            q4[head, :, :128] = hh
            q4[head, :, 128:] = ll
            for start, key4, value2 in ((0, k4p, v2p), (2 * rows, k4s, v2s)):
                hl, _, _ = packs(k_both[pl.ds(start, 2 * rows), lanes], head)
                key4[head, :, :128] = hl
                key4[head, :, 128:] = hl
                value2[head] = packs(v_both[pl.ds(start, 2 * rows), lanes], head)[0]

        def attend(block, carry):
            if pair == 0:
                @pl.when(block == 0)
                def _():
                    over(spread, 1, 3)

                @pl.when(block > 0)
                def _():
                    over(spread, 2, block - 1)

                over(relay, 1, block)
            if pair == 1:
                @pl.when(block == 1)
                def _():
                    over(spread, 2, 3)

                @pl.when(block > 0)
                def _():
                    over(relay, 2, block - 1)
            if pair == 2:
                @pl.when(block == 2)
                def _():
                    over(relay, 2, 3)

            here = pl.ds(pl.multiple_of(block * QB, QB), QB)
            seen = self_mask(lens_ref, block, 0)
            results = []
            for head in range(2):
                query = q4[head, here, :]
                far = dot_nt(query, k4p[head])
                near = jnp.where(seen, dot_nt(query, k4s[head, here, :]), MASKED)
                top = jnp.maximum(
                    jnp.max(far, axis=1, keepdims=True), jnp.max(near, axis=1, keepdims=True)
                )
                far = jnp.exp(far - top)
                near = jnp.exp(near - top)
                total = jnp.sum(far, axis=1, keepdims=True) + jnp.sum(near, axis=1, keepdims=True)
                far_h, far_l = split(far)
                near_h, near_l = split(near)
                out = dot(far_h, v2p[head]) + dot(far_l, v2p[head])
                value = v2s[head, here, :]
                out = out + dot(near_h, value) + dot(near_l, value)
                out = (out + pltpu.roll(out, HD, 1)) / total
                lse = top + jnp.log(total)
                lse_all[2 * pair + head, :, here] = jnp.transpose(
                    jnp.broadcast_to(lse, (QB, 128))
                )[:8]
                results.append(out)
            o_all[here, lanes] = jnp.where(lane_ids((QB, 128)) < HD, results[0], results[1])
            return carry

        lax.fori_loop(0, 4, attend, 0)

    def last(index, carry):
        for kind in range(3):
            settle(kind, index)
        return carry

    lax.fori_loop(0, layers, last, 0)
    part_count = count // 2
    swap = remote(
        out_all.at[pl.ds((1 - role) * part_count, part_count)], out_other, pair_sem.at[0],
        pair_sem.at[1], partner(0, 1),
    )
    swap.start()

    def ended(index, carry):
        for kind in range(3):
            drained(kind, index)
        return carry

    lax.fori_loop(0, layers, ended, 0)
    def passed(index, carry):
        slot = index * 2 + side
        along(index, lambda: sends(slot, 0), lambda: sends(slot, 1))
        sends(slot, 2)
        return carry

    lax.fori_loop(0, layers, passed, 0)
    to_pair.wait_send()

    @pl.when(group == 0)
    def _():
        to_far.wait_send()

    @pl.when(group == 1)
    def _():
        far_pair.wait_send()

    swap.wait()


def run_forward(lens, weights, small, tokens, out_piece, up_piece, down_piece):
    bits = dp_bits()
    count = 1 << bits
    layers = count // 2
    anywhere = pl.BlockSpec(memory_space=pl.ANY)
    vmem = pl.BlockSpec(memory_space=pltpu.VMEM)
    three, shard, half = weights.shape
    rows, width = tokens.shape
    heads = half // HD
    shape = lambda *dims: jax.ShapeDtypeStruct(dims, F32)
    whole = lambda piece: shape(count, *piece.shape)
    return pl.pallas_call(
        functools.partial(forward_kernel, bits),
        in_specs=[pl.BlockSpec(memory_space=pltpu.SMEM)] + [anywhere] * 6,
        out_specs=[vmem] * 10 + [anywhere] * 4,
        out_shape=[
            jax.ShapeDtypeStruct((three, width, half), BF),
            jax.ShapeDtypeStruct((three, width, half), BF),
            shape(count, *small.shape),
            jax.ShapeDtypeStruct((width, 4 * rows), BF),
            jax.ShapeDtypeStruct((width, 4 * rows), BF),
            shape(4 * rows, half),
            shape(4 * rows, half),
            shape(2 * rows, half),
            shape(2 * rows, half),
            shape(heads, 8, 2 * rows),
            whole(out_piece),
            whole(up_piece),
            whole(down_piece),
            shape(count // 2, *out_piece.shape),
        ],
        scratch_shapes=[
            pltpu.VMEM((three, count, shard, half), F32),
            pltpu.VMEM((4 * rows, width), F32),
            pltpu.VMEM((4 * rows, width), BF),
            pltpu.VMEM((4 * rows, width), BF),
            pltpu.VMEM((2, 2 * rows, 256), BF),
            pltpu.VMEM((2, 2 * rows, 256), BF),
            pltpu.VMEM((2, 2 * rows, 256), BF),
            pltpu.VMEM((2, 2 * rows, 128), BF),
            pltpu.VMEM((2, 2 * rows, 128), BF),
            pltpu.VMEM(out_piece.shape, F32),
            pltpu.VMEM(up_piece.shape, F32),
            pltpu.VMEM(down_piece.shape, F32),
            pltpu.SemaphoreType.DMA((2, count, 3)),
            pltpu.SemaphoreType.DMA((2, count)),
            pltpu.SemaphoreType.DMA((3,)),
            pltpu.SemaphoreType.DMA((3,)),
            pltpu.SemaphoreType.DMA((6,)),
            pltpu.SemaphoreType.DMA((3, layers, 8)),
            pltpu.SemaphoreType.DMA((3, layers, 7)),
            pltpu.SemaphoreType.DMA((2,)),
        ],
        compiler_params=pltpu.CompilerParams(
            collective_id=1, has_side_effects=True, vmem_limit_bytes=60 << 20
        ),
        name="gather_weights_and_attend",
    )(lens, weights, small, tokens, out_piece, up_piece, down_piece)


def backward_kernel(lens_ref, q_ref, kp_ref, vp_ref, ks_ref, vs_ref, o_ref, g_ref, lse_ref,
                    dq_ref, dkp_ref, dvp_ref, dks_ref, dvs_ref,
                    q4, k4p, k4s, v4p, v4s, g4, q2, g2, k2tp, k2ts, delta):
    rows = q_ref.shape[0]
    prod = jnp.transpose(o_ref[...] * g_ref[...])
    for head in range(2):
        hl, hh, ll = packs(q_ref[...] * 0.125, head)
        q2[head] = hl
        q4[head, :, :128] = hh
        q4[head, :, 128:] = ll
        hl, hh, ll = packs(g_ref[...], head)
        g2[head] = hl
        g4[head, :, :128] = hh
        g4[head, :, 128:] = ll
        for src, dst in ((kp_ref, k4p), (ks_ref, k4s), (vp_ref, v4p), (vs_ref, v4s)):
            hl, _, _ = packs(src[...], head)
            dst[head, :, :128] = hl
            dst[head, :, 128:] = hl
        for src, dst in ((kp_ref, k2tp), (ks_ref, k2ts)):
            flipped = jnp.transpose(src[...])[head * HD : head * HD + HD]
            high, low = high_low(flipped)
            dst[head, :HD] = high.astype(BF)
            dst[head, HD:] = low.astype(BF)
        delta[head] = jnp.broadcast_to(
            jnp.sum(prod[head * HD : head * HD + HD], axis=0, keepdims=True), (8, rows)
        )
    dkp_ref[...] = jnp.zeros_like(dkp_ref)
    dvp_ref[...] = jnp.zeros_like(dvp_ref)

    def step(block, carry):
        here = pl.ds(pl.multiple_of(block * QB, QB), QB)
        seen = self_mask(lens_ref, block, 1)
        keep = {}
        for head in range(2):
            query = q4[head, here, :]
            grad = g4[head, here, :]
            lse = lse_ref[head, :1, here]
            low = delta[head, :1, here]
            far = jnp.exp(dot_nt(k4p[head], query) - lse)
            near = jnp.exp(jnp.where(seen, dot_nt(k4s[head, here, :], query), MASKED) - lse)
            far_g = far * (dot_nt(v4p[head], grad) - low)
            near_g = near * (dot_nt(v4s[head, here, :], grad) - low)
            grad2 = g2[head, here, :]
            query2 = q2[head, here, :]
            ph, p_l = split(far)
            dvp = dot(ph, grad2) + dot(p_l, grad2)
            ph, p_l = split(near)
            dvs = dot(ph, grad2) + dot(p_l, grad2)
            sh, sl = split(far_g)
            dkp = dot(sh, query2) + dot(sl, query2)
            dq = dot(k2tp[head], sh) + dot(k2tp[head], sl)
            sh, sl = split(near_g)
            dks = dot(sh, query2) + dot(sl, query2)
            side = k2ts[head, :, here]
            dq = dq + dot(side, sh) + dot(side, sl)
            dq = dq[:HD] + dq[HD:]
            keep[head] = (
                dq,
                dkp + pltpu.roll(dkp, HD, 1),
                dvp + pltpu.roll(dvp, HD, 1),
                dks + pltpu.roll(dks, HD, 1),
                dvs + pltpu.roll(dvs, HD, 1),
            )
        left = lane_ids((QB, 128)) < HD
        far_left = lane_ids(dkp_ref.shape) < HD
        dq_ref[here, :] = jnp.transpose(
            jnp.concatenate([keep[0][0], keep[1][0]], axis=0)
        ) * 0.125
        dkp_ref[...] += jnp.where(far_left, keep[0][1], keep[1][1])
        dvp_ref[...] += jnp.where(far_left, keep[0][2], keep[1][2])
        dks_ref[here, :] = jnp.where(left, keep[0][3], keep[1][3])
        dvs_ref[here, :] = jnp.where(left, keep[0][4], keep[1][4])
        return carry

    lax.fori_loop(0, rows // QB, step, 0)


def attend_backward(lens, q, k_both, v_both, out, grad, lse):
    rows, width = q.shape
    heads = width // HD
    near = pl.BlockSpec((rows, 128), lambda j, lens: (0, j))
    group = pl.BlockSpec((rows, 128), lambda j, lens: (1, j))
    flops = heads * 2 * rows * (rows + QB) * (256 * 5)
    shape = jax.ShapeDtypeStruct((rows, width), F32)
    return pl.pallas_call(
        backward_kernel,
        grid_spec=pltpu.PrefetchScalarGridSpec(
            num_scalar_prefetch=1,
            grid=(heads // 2,),
            in_specs=[
                near, near, near, group, group, near, near,
                pl.BlockSpec((2, 8, rows), lambda j, lens: (j, 0, 0)),
            ],
            out_specs=[near] * 5,
            scratch_shapes=[
                pltpu.VMEM((2, rows, 256), BF),
                pltpu.VMEM((2, rows, 256), BF),
                pltpu.VMEM((2, rows, 256), BF),
                pltpu.VMEM((2, rows, 256), BF),
                pltpu.VMEM((2, rows, 256), BF),
                pltpu.VMEM((2, rows, 256), BF),
                pltpu.VMEM((2, rows, 128), BF),
                pltpu.VMEM((2, rows, 128), BF),
                pltpu.VMEM((2, 128, rows), BF),
                pltpu.VMEM((2, 128, rows), BF),
                pltpu.VMEM((2, 8, rows), F32),
            ],
        ),
        out_shape=[shape] * 5,
        compiler_params=pltpu.CompilerParams(vmem_limit_bytes=56 << 20),
        cost_estimate=pl.CostEstimate(
            flops=flops, bytes_accessed=12 * rows * width * 4, transcendentals=heads * rows * rows
        ),
        name="attention_backward",
    )(lens, q, k_both, v_both, k_both, v_both, out, grad, lse)


TRANSFERS = {
    (0, 2): [("first", 0, 3), ("send", 0, 1)],
    (0, 3): [("down on", 0, 3)],
    (0, 4): [("first", 0, 2), ("send", 0, 0), ("down on", 0, 2)],
    (1, 0): [("second", 0, 3)],
    (1, 1): [("first", 0, 1), ("down on", 0, 1)],
    (1, 2): [("second", 0, 2), ("on", 0, 3)],
    (1, 3): [("first", 0, 0), ("send", 1, 3), ("send", 1, 2), ("send", 1, 1), ("send", 1, 0)],
    (1, 4): [("second", 0, 1), ("on", 0, 2), ("down on", 0, 0)],
    (2, 0): [("qkv", 0, 3), ("qkv", 0, 2)],
    (2, 1): [("second", 0, 0), ("on", 0, 1), ("qkv", 0, 1)],
    (2, 2): [("qkv on", 0, 3), ("qkv", 0, 0), ("down on", 0, -1), ("first", 1, 3)],
    (2, 3): [("on", 0, 0), ("qkv on", 0, 2), ("first", 1, 2), ("first", 1, 1), ("first", 1, 0)],
    (2, 4): [("qkv on", 0, 1)],
}


def backward_all_kernel(
    bits, lens_ref, lse_ref, xt_high, xt_low, w_high, w_low, small_ref,
    q_hbm, k_hbm, v_hbm, o_hbm, g_hbm, first_hbm, up_hbm, out_hbm, down_hbm,
    grad_in, up_mine, up_other, out_mine, out_other, down_mine, down_other, qkv_mine, qkv_other, small_out,
    down_in, down_sum,
    q_in, k_in, v_in, o_in, g_in, q4, g4, k2p, k2s, v2p, v2s, q2, g2, k2tp, k2ts, delta,
    d_q, d_k, d_v, d_kv, d_q2, on_prompt, on_own, prompt_in, far_in,
    up_a, up_b, up_ra, up_rax, up_rb, up_rby, up_s, up_rz,
    out_a, out_b, out_ra, out_rax, out_rb, out_rby, out_s, out_rz,
    qkv_g, qkv_in, qkv_x, sm, sm_in, sm_x, sm_pair,
    load_sem, acc_sem, xy_send, xy_recv, z_send, z_recv, end_send, end_recv,
    q_send, q_recv, qx_send, qx_recv, s_send, s_recv, sx_send, sx_recv, t_send, t_recv, d_load, d_send, d_recv, dz_send, dz_recv,
):
    me = lax.axis_index("dp")
    seq = lax.axis_index("seq")
    group, role = seq // 2, seq % 2
    count = 1 << bits
    layers = count // 2
    level, side = me // 2, me % 2
    has_up, has_down = level < layers - 1, level > 0
    above, below = (me + 2, seq), (me - 2, seq)
    arrival = functools.partial(line_arrival, level, layers)
    width, both_rows = xt_high.shape
    half = w_high.shape[2]
    rows = both_rows // 2
    own = rows // 2
    shard = width // count
    pairs = half // 128
    kinds = (
        (up_hbm, up_a, up_b, up_ra, up_rax, up_rb, up_rby, up_s, up_rz, up_mine, up_other),
        (out_hbm, out_a, out_b, out_ra, out_rax, out_rb, out_rby, out_s, out_rz, out_mine, out_other),
    )

    def stage(pair):
        lanes = pl.ds(pair * 128, 128)
        copies = []
        for index, (src, dst) in enumerate(
            ((q_hbm, q_in), (k_hbm, k_in), (v_hbm, v_in), (o_hbm, o_in), (g_hbm, g_in))
        ):
            copies.append(pltpu.make_async_copy(src.at[:, lanes], dst, load_sem.at[index]))
        return copies

    for copy in stage(0):
        copy.start()
    first_copy = pltpu.make_async_copy(first_hbm, on_own.at[pl.ds(0, own)], load_sem.at[5])
    first_copy.start()
    kept = {}
    for kind in range(2):
        grads, acc_a, acc_b = kinds[kind][:3]
        for layer in reversed(range(layers)):
            slot = arrival(layer) * 2 + side
            for index, copy in enumerate(
                (
                    (grads.at[slot, :, pl.ds(0, 1)], acc_a.at[layer]),
                    (grads.at[slot, group, pl.ds(1, 2)], acc_b.at[layer, 0]),
                    (grads.at[slot + 1 - 2 * side, group, pl.ds(1, 2)], acc_b.at[layer, 1]),
                )
            ):
                kept[kind, layer, index] = pltpu.make_async_copy(
                    *copy, acc_sem.at[kind, layer, index]
                )
                kept[kind, layer, index].start()
    greet_line(has_up, has_down, above, below)
    started = []
    ended = []

    def go(make, *which):
        make(*which).start()
        started.append((make, which))

    def xy(kind, layer, step):
        grads, acc_a, acc_b, ra, rax, rb, rby = kinds[kind][:7]
        slot = arrival(layer) * 2 + side
        src, dst, target = (
            (grads.at[slot + 1 - 2 * side, :, pl.ds(0, 1)], ra.at[layer], partner(1, 0)),
            (grads.at[slot, group ^ 1, pl.ds(1, 2)], rb.at[layer, 0], partner(0, 2)),
            (grads.at[slot + 1 - 2 * side, group ^ 1, pl.ds(1, 2)], rb.at[layer, 1], partner(0, 2)),
            (acc_a.at[layer, group ^ 1], rax.at[layer], partner(0, 2)),
            (acc_b.at[layer, 1], rby.at[layer], partner(1, 0)),
        )[step]
        return remote(
            src, dst, xy_send.at[kind, layer, step], xy_recv.at[kind, layer, step], target
        )

    def send(kind, layer):
        for step in range(3):
            go(xy, kind, layer, step)

    def first(kind, layer):
        _, acc_a, acc_b, ra, _, rb = kinds[kind][:6]
        for index in range(3):
            kept[kind, layer, index].wait()
        for step in range(3):
            xy(kind, layer, step).wait_recv()
        acc_a[layer] += ra[layer]
        acc_b[layer] += rb[layer]
        go(xy, kind, layer, 3)
        go(xy, kind, layer, 4)

    def incoming(at):
        return ((at > level) & has_down) | ((at < level) & has_up)

    def line_in(layer, add):
        at = arrival(layer)
        if layer == 0:
            @pl.when(has_down)
            def _():
                add(at)

            @pl.when(has_up)
            def _():
                add(layers)
        else:
            @pl.when(incoming(at))
            def _():
                add(at)

    def line_out(layer, make, late):
        if layer:
            at = arrival(layer)
            now = incoming(at) if late else jnp.logical_not(incoming(at))

            @pl.when((at > level) & now)
            def _():
                make(at, above).start()

            @pl.when((at < level) & now)
            def _():
                make(jnp.where(at == level - 1, layers, at), below).start()

            if late:
                def act():
                    at = arrival(layer)

                    @pl.when(at > level)
                    def _():
                        make(at, above).wait_send()

                    @pl.when(at < level)
                    def _():
                        make(jnp.where(at == level - 1, layers, at), below).wait_send()

                ended.append(act)

    def climb(kind, layer, place, target):
        return remote(
            kinds[kind][7].at[layer], kinds[kind][8].at[place], z_send.at[kind, layer],
            z_recv.at[kind, place], target,
        )

    def second(kind, layer):
        _, acc_a, acc_b, _, rax, _, rby, total, landing = kinds[kind][:9]
        xy(kind, layer, 3).wait_recv()
        xy(kind, layer, 4).wait_recv()
        total[layer, pl.ds(0, 1)] = acc_a[layer, group] + rax[layer]
        total[layer, pl.ds(1, 2)] = acc_b[layer, 0] + rby[layer]

        line_out(layer, functools.partial(climb, kind, layer), False)

    def onward(kind, layer):
        total, landing = kinds[kind][7:9]

        def add(place):
            climb(kind, layer, place, above).wait_recv()
            total[layer] += landing[place]

        line_in(layer, add)
        line_out(layer, functools.partial(climb, kind, layer), True)

    def cross(kind):
        total, mine = kinds[kind][7], kinds[kind][9]
        return remote(
            total.at[0], mine.at[group], end_send.at[kind, 0], end_recv.at[kind, 0], partner(0, 2)
        )

    def cross_in(kind):
        total, mine = kinds[kind][7], kinds[kind][9]
        return remote(
            total.at[0], mine.at[group ^ 1], end_send.at[kind, 0], end_recv.at[kind, 0], partner(0, 2)
        )

    def hand(kind):
        mine, other = kinds[kind][9:]
        return remote(mine, other, end_send.at[kind, 1], end_recv.at[kind, 1], partner(0, 1))

    def tracks(pair):
        found = [
            (lambda slot: qkv_g.at[pair, :, slot], qkv_in.at[pair], q_send.at[pair], q_recv.at[pair])
        ]
        if pair == pairs - 1:
            found.append((lambda slot: sm.at[slot], sm_in, s_send, s_recv))
        return found

    def to_side(pair, which, layer):
        block, landing, send_sem, recv_sem = tracks(pair)[which]
        slot = arrival(layer) * 2 + 1 - side
        return remote(
            block(slot), landing.at[layer], send_sem.at[layer], recv_sem.at[layer], partner(1, 0)
        )

    def qkv_climb(pair, which, layer, place, target):
        block, landing, send_sem, recv_sem = tracks(pair)[which]
        return remote(
            block(arrival(layer) * 2 + side), landing.at[layers + place],
            send_sem.at[layers + layer], recv_sem.at[layers + place], target,
        )

    def qkv_begin(pair):
        for layer in reversed(range(layers)):
            for which in range(len(tracks(pair))):
                go(to_side, pair, which, layer)

    def qkv(pair, layer):
        for which, track in enumerate(tracks(pair)):
            here = track[0](arrival(layer) * 2 + side)
            to_side(pair, which, layer).wait_recv()
            here[...] += track[1][layer]
            line_out(layer, functools.partial(qkv_climb, pair, which, layer), False)

    def qkv_on(pair, layer):
        for which, track in enumerate(tracks(pair)):
            here = track[0](arrival(layer) * 2 + side)

            def add(place):
                qkv_climb(pair, which, layer, place, above).wait_recv()
                here[...] += track[1][layers + place]

            line_in(layer, add)
            line_out(layer, functools.partial(qkv_climb, pair, which, layer), True)

    def qkv_cross(pair):
        return remote(
            qkv_g.at[pair, :, me], qkv_x.at[pair], qx_send.at[pair, 0], qx_recv.at[pair, 0], partner(0, 2)
        )

    def qkv_hand(pair):
        return remote(
            qkv_mine.at[pair], qkv_other.at[pair], qx_send.at[pair, 1], qx_recv.at[pair, 1],
            partner(0, 1),
        )

    def qkv_finish(pair):
        qkv_cross(pair).wait_recv()
        qkv_mine[pair] = qkv_g[pair, :, me] + qkv_x[pair]
        go(qkv_hand, pair)

    down_loads = [
        pltpu.make_async_copy(down_hbm.at[arrival(layer)], down_sum.at[layer], d_load.at[layer])
        for layer in range(layers)
    ]

    def down_climb(layer, place, target):
        return remote(
            down_sum.at[layer], down_in.at[place], dz_send.at[layer], dz_recv.at[place], target
        )

    def down_cross(landing):
        region = down_mine.at[group ^ landing]
        return remote(region, region, d_send.at[0], d_recv.at[0], partner(0, 2))

    def down_hand():
        return remote(down_mine, down_other, d_send.at[1], d_recv.at[1], partner(0, 1))

    def down_begin(layer):
        down_loads[layer].wait()
        line_out(layer, functools.partial(down_climb, layer), False)

    def down_on(_, layer):
        if layer < 0:
            down_cross(1).wait_recv()
            go(down_hand)
            return

        def add(place):
            down_climb(layer, place, above).wait_recv()
            down_sum[layer] += down_in[place]

        line_in(layer, add)
        line_out(layer, functools.partial(down_climb, layer), True)
        if layer == 0:
            down_mine[group] = down_sum[0]
            go(down_cross, 0)

    actions = {
        "send": send,
        "first": first,
        "second": second,
        "on": onward,
        "qkv": qkv,
        "qkv on": qkv_on,
        "down on": down_on,
    }

    def run(events):
        for name, kind, index in events:
            actions[name](kind, index)

    def prepare(pair):
        prod = jnp.transpose(o_in[...] * g_in[...])
        for head in range(2):
            hl, hh, ll = packs(q_in[...] * 0.125, head)
            q2[head] = hl
            q4[head, :, :128] = hh
            q4[head, :, 128:] = ll
            hl, hh, ll = packs(g_in[...], head)
            g2[head] = hl
            g4[head, :, :128] = hh
            g4[head, :, 128:] = ll
            for src, start, dst in (
                (k_in, 0, k2p), (k_in, rows, k2s), (v_in, 0, v2p), (v_in, rows, v2s),
            ):
                dst[head] = packs(src[pl.ds(start, rows), :], head)[0]
            for start, dst in ((0, k2tp), (rows, k2ts)):
                flipped = jnp.transpose(k_in[pl.ds(start, rows), :])[head * HD : head * HD + HD]
                high, low = high_low(flipped)
                dst[head, :HD] = high.astype(BF)
                dst[head, HD:] = low.astype(BF)
            delta[head] = jnp.broadcast_to(
                jnp.sum(prod[head * HD : head * HD + HD], axis=0, keepdims=True), (8, rows)
            )

    def twice(value):
        return jnp.concatenate([value, value], axis=1)

    def attend(pair):
        d_k[pl.ds(0, rows), :] = jnp.zeros((rows, 128), F32)
        d_v[pl.ds(0, rows), :] = jnp.zeros((rows, 128), F32)

        def body(step, carry):
            for position in range(4):
                events = TRANSFERS.get((pair, position))
                if events:
                    @pl.when(step == position)
                    def _():
                        run(events)

            here = pl.ds(pl.multiple_of(step * QB, QB), QB)
            there = pl.ds(pl.multiple_of(step * QB + rows, QB), QB)
            seen = self_mask(lens_ref, step, 1)
            keep = {}
            for head in range(2):
                query = q4[head, here, :]
                grad = g4[head, here, :]
                lse = lse_ref[2 * pair + head, :1, here]
                low = delta[head, :1, here]
                far = jnp.exp(dot_nt(twice(k2p[head]), query) - lse)
                near = jnp.exp(
                    jnp.where(seen, dot_nt(twice(k2s[head, here, :]), query), MASKED) - lse
                )
                far_g = far * (dot_nt(twice(v2p[head]), grad) - low)
                near_g = near * (dot_nt(twice(v2s[head, here, :]), grad) - low)
                grad2 = g2[head, here, :]
                query2 = q2[head, here, :]
                ph, p_l = split(far)
                dvp = dot(ph, grad2) + dot(p_l, grad2)
                ph, p_l = split(near)
                dvs = dot(ph, grad2) + dot(p_l, grad2)
                sh, sl = split(far_g)
                dkp = dot(sh, query2) + dot(sl, query2)
                dq = dot(k2tp[head], sh) + dot(k2tp[head], sl)
                sh, sl = split(near_g)
                dks = dot(sh, query2) + dot(sl, query2)
                side = k2ts[head, :, here]
                dq = dq + dot(side, sh) + dot(side, sl)
                keep[head] = (
                    dq[:HD] + dq[HD:],
                    dkp + pltpu.roll(dkp, HD, 1),
                    dvp + pltpu.roll(dvp, HD, 1),
                    dks + pltpu.roll(dks, HD, 1),
                    dvs + pltpu.roll(dvs, HD, 1),
                )
            left = lane_ids((QB, 128)) < HD
            far_left = lane_ids((rows, 128)) < HD
            d_q[here, :] = jnp.transpose(
                jnp.concatenate([keep[0][0], keep[1][0]], axis=0)
            ) * 0.125
            d_k[pl.ds(0, rows), :] += jnp.where(far_left, keep[0][1], keep[1][1])
            d_v[pl.ds(0, rows), :] += jnp.where(far_left, keep[0][2], keep[1][2])
            d_k[there, :] = jnp.where(left, keep[0][3], keep[1][3])
            d_v[there, :] = jnp.where(left, keep[0][4], keep[1][4])
            return carry

        lax.fori_loop(0, 4, body, 0)

    def divide():
        def body(index, carry):
            here = pl.ds(pl.multiple_of(index * QB, QB), QB)
            high, low = split(d_k[here, :])
            d_kv[here, 0:128] = high
            d_kv[here, 256:384] = low
            high, low = split(d_v[here, :])
            d_kv[here, 128:256] = high
            d_kv[here, 384:512] = low

            @pl.when(index < 4)
            def _():
                high, low = split(d_q[here, :])
                d_q2[here, 0:128] = high
                d_q2[here, 128:256] = low

            return carry

        lax.fori_loop(0, 8, body, 0)

    def to_prompt(pair):
        lanes = pl.ds(pair * 128, 128)
        high_w = jnp.concatenate([w_high[1, :, lanes], w_high[2, :, lanes]], axis=1)
        low_w = jnp.concatenate([w_low[1, :, lanes], w_low[2, :, lanes]], axis=1)

        def body(index, carry):
            here = pl.ds(pl.multiple_of(index * QB, QB), QB)
            high, low = d_kv[here, 0:256], d_kv[here, 256:512]
            result = dot_nt(high, high_w) + dot_nt(high, low_w) + dot_nt(low, high_w)
            on_prompt[here, :] = result if pair == 0 else on_prompt[here, :] + result
            return carry

        lax.fori_loop(0, 4, body, 0)

    def to_own(pair):
        lanes = pl.ds(pair * 128, 128)
        order = (1, 2, 0)
        high_w = jnp.concatenate([w_high[i, :, lanes] for i in order], axis=1)
        low_w = jnp.concatenate([w_low[i, :, lanes] for i in order], axis=1)

        def body(index, carry):
            here = pl.ds(pl.multiple_of(index * QB, QB), QB)
            there = pl.ds(pl.multiple_of(index * QB + rows, QB), QB)
            high = jnp.concatenate([d_kv[there, 0:256], d_q2[here, 0:128]], axis=1)
            low = jnp.concatenate([d_kv[there, 256:512], d_q2[here, 128:256]], axis=1)
            result = dot_nt(high, high_w) + dot_nt(high, low_w) + dot_nt(low, high_w)
            on_own[here, :] += result
            return carry

        lax.fori_loop(0, 4, body, 0)

    def weight_grads(pair):
        each = count // 2
        size = each * shard

        def body(index, carry):
            here = pl.ds(pl.multiple_of(index * size, size), size)
            high, low = xt_high[here, :], xt_low[here, :]
            first_kv = dot(high, d_kv[...])
            kv = first_kv[:, :256] + first_kv[:, 256:] + dot(low, d_kv[:, 0:256])
            high, low = high[:, rows:], low[:, rows:]
            first_q = dot(high, d_q2[...])
            query = first_q[:, :128] + first_q[:, 128:] + dot(low, d_q2[:, 0:128])
            for slot in range(each):
                part = slice(slot * shard, slot * shard + shard)
                qkv_g[pair, 0, index * each + slot] = query[part]
                qkv_g[pair, 1, index * each + slot] = kv[part, :128]
                qkv_g[pair, 2, index * each + slot] = kv[part, 128:]
            return carry

        lax.fori_loop(0, 2, body, 0)

    sums_q, sums_v = [], []
    for copy in reversed(down_loads):
        copy.start()
    send(0, 3)
    send(0, 2)
    for layer in reversed(range(layers)):
        down_begin(layer)
    on_own[pl.ds(own, own), :] = jnp.zeros((own, width), F32)
    for pair in range(pairs):
        for copy in stage(pair):
            copy.wait()
        prepare(pair)
        if pair + 1 < pairs:
            for copy in stage(pair + 1):
                copy.start()
        attend(pair)
        run(TRANSFERS.get((pair, 4), []))
        divide()
        sums_q.append(jnp.sum(d_q[...], axis=0, keepdims=True))
        sums_v.append(jnp.sum(d_v[...], axis=0, keepdims=True))
        if pair == 0:
            first_copy.wait()
        if pair + 1 < pairs:
            weight_grads(pair)
            qkv_begin(pair)
            to_prompt(pair)
            to_own(pair)

    def swap(src, dst, index):
        return remote(src, dst, t_send.at[index], t_recv.at[index], partner(0, 1))

    last = pairs - 1
    to_prompt(last)
    prompt_swap = swap(on_prompt.at[pl.ds(own, own)], prompt_in, 0)
    go(lambda: prompt_swap)
    qkv_on(0, 0)
    go(qkv_cross, 0)
    go(cross, 0)
    weight_grads(last)
    bias_q = jnp.concatenate(sums_q, axis=1)
    bias_v = jnp.concatenate(sums_v, axis=1)
    bias = jnp.concatenate([bias_q, bias_v, jnp.zeros((6, half), F32)], axis=0)
    nothing = jnp.zeros((8, half), F32)
    bias = jnp.where(
        role == 0,
        jnp.concatenate([bias, nothing], axis=1),
        jnp.concatenate([nothing, bias], axis=1),
    )
    inside = lane_ids((8, 128)) < shard
    for slot in range(count):
        turned = pltpu.roll(bias, (width - shard * slot) % width, 1) if slot else bias
        sm[slot] = small_ref[slot]
        sm[slot, pl.ds(0, 8), :] += jnp.where(inside, turned[:, :128], 0.0)

    qkv_begin(last)
    prompt_swap.wait_recv()
    on_prompt[pl.ds(0, own), :] += prompt_in[...]
    far = remote(on_prompt.at[pl.ds(0, own)], far_in, t_send.at[1], t_recv.at[1], partner(0, 2))

    @pl.when(group == 1)
    def _():
        far.start()

    for layer in reversed(range(layers)):
        qkv(1, layer)
    to_own(last)
    own_swap = swap(on_own.at[pl.ds(own, own)], grad_in, 2)
    go(lambda: own_swap)

    for layer in reversed(range(layers)):
        second(1, layer)
    qkv_on(1, 3)
    qkv(last, 3)
    onward(1, 3)
    qkv_on(1, 2)
    qkv(last, 2)
    onward(1, 2)
    qkv_on(1, 1)
    qkv(last, 1)
    onward(1, 1)
    qkv(last, 0)
    qkv_on(last, 3)
    qkv_on(1, 0)
    go(qkv_cross, 1)
    onward(1, 0)
    go(cross, 1)
    qkv_on(last, 2)
    qkv_finish(0)
    for kind in range(2):
        kinds[kind][9][group] = kinds[kind][7][0]
        cross_in(kind).wait_recv()
        go(hand, kind)
    qkv_finish(1)
    qkv_on(last, 1)
    qkv_on(last, 0)
    go(qkv_cross, last)
    small_x = remote(sm.at[me], sm_x, sx_send.at[0], sx_recv.at[0], partner(0, 2))
    go(lambda: small_x)
    own_swap.wait_recv()
    grad_in[...] += on_own[pl.ds(0, own), :]
    qkv_finish(last)
    small_x.wait_recv()
    small_out[...] = sm[me] + sm_x[...]
    small_pair = remote(small_out, sm_pair, sx_send.at[1], sx_recv.at[1], partner(0, 1))
    go(lambda: small_pair)

    @pl.when(group == 0)
    def _():
        far.wait_recv()
        grad_in[...] += on_prompt[pl.ds(0, own), :] + far_in[...]

    small_pair.wait_recv()
    for kind in range(2):
        hand(kind).wait_recv()
    down_hand().wait_recv()
    for pair in range(pairs):
        qkv_hand(pair).wait_recv()
    for make, which in started:
        make(*which).wait_send()
    for act in ended:
        act()
    small_out[...] += sm_pair[...]

    @pl.when(group == 1)
    def _():
        far.wait_send()


def run_backward(lens, lse, xt_high, xt_low, w_high, w_low, small, q, k, v, o, g, first_grad,
                 up_grads, out_grads, down_grads):
    bits = dp_bits()
    count = 1 << bits
    layers = count // 2
    anywhere = pl.BlockSpec(memory_space=pl.ANY)
    vmem = pl.BlockSpec(memory_space=pltpu.VMEM)
    width, both_rows = xt_high.shape
    rows, half = q.shape
    own = rows // 2
    pairs = half // 128
    shard = width // count
    shape = lambda *dims: jax.ShapeDtypeStruct(dims, F32)
    space = lambda *dims: pltpu.VMEM(dims, F32)
    short = lambda *dims: pltpu.VMEM(dims, BF)
    dma = lambda *dims: pltpu.SemaphoreType.DMA(dims)

    def buffers(unit):
        return [
            space(layers, 2, 1, *unit),
            space(layers, 2, 2, *unit),
            space(layers, 2, 1, *unit),
            space(layers, 1, *unit),
            space(layers, 2, 2, *unit),
            space(layers, 2, *unit),
            space(layers, 3, *unit),
            space(layers + 1, 3, *unit),
        ]

    up_unit, out_unit = up_grads.shape[3:], out_grads.shape[3:]
    tiny = small.shape[1:]
    return pl.pallas_call(
        functools.partial(backward_all_kernel, bits),
        in_specs=[pl.BlockSpec(memory_space=pltpu.SMEM)] + [vmem] * 6 + [anywhere] * 9,
        out_specs=[vmem] + [vmem, anywhere] * 4 + [vmem],
        out_shape=[
            shape(own, width),
            shape(2, 3, *up_unit),
            shape(2, 3, *up_unit),
            shape(2, 3, *out_unit),
            shape(2, 3, *out_unit),
            shape(2, *down_grads.shape[1:]),
            shape(2, *down_grads.shape[1:]),
            shape(pairs, 3, shard, 128),
            shape(pairs, 3, shard, 128),
            shape(*tiny),
        ],
        scratch_shapes=[
            space(layers + 1, *down_grads.shape[1:]),
            space(*down_grads.shape),
            space(rows, 128),
            space(both_rows, 128),
            space(both_rows, 128),
            space(rows, 128),
            space(rows, 128),
            short(2, rows, 256),
            short(2, rows, 256),
            short(2, rows, 128),
            short(2, rows, 128),
            short(2, rows, 128),
            short(2, rows, 128),
            short(2, rows, 128),
            short(2, rows, 128),
            short(2, 128, rows),
            short(2, 128, rows),
            space(2, 8, rows),
            space(rows, 128),
            space(both_rows, 128),
            space(both_rows, 128),
            short(both_rows, 512),
            short(rows, 256),
            space(rows, width),
            space(rows, width),
            space(own, width),
            space(own, width),
        ]
        + buffers(up_unit)
        + buffers(out_unit)
        + [
            space(pairs, 3, count, shard, 128),
            space(pairs, count + 1, 3, shard, 128),
            space(pairs, 3, shard, 128),
            space(count, *tiny),
            space(count + 1, *tiny),
            space(*tiny),
            space(*tiny),
            dma(6),
            dma(2, layers, 3),
            dma(2, layers, 5),
            dma(2, layers, 5),
            dma(2, layers),
            dma(2, layers + 1),
            dma(2, 2),
            dma(2, 2),
            dma(pairs, count),
            dma(pairs, count + 1),
            dma(pairs, 2),
            dma(pairs, 2),
            dma(count),
            dma(count + 1),
            dma(2),
            dma(2),
            dma(3),
            dma(3),
            dma(layers),
            dma(2),
            dma(2),
            dma(layers),
            dma(layers + 1),
        ],
        compiler_params=pltpu.CompilerParams(
            collective_id=3, has_side_effects=True, vmem_limit_bytes=67043328
        ),
        name="attention_backward_and_scatter",
    )(lens, lse, xt_high, xt_low, w_high, w_low, small, q, k, v, o, g, first_grad, up_grads, out_grads,
      down_grads)


def norm_forward(resid, gain, shift):
    center = resid - jnp.mean(resid, axis=-1, keepdims=True)
    inverse = lax.rsqrt(jnp.mean(center * center, axis=-1, keepdims=True) + EPSILON)
    normed = center * inverse
    return normed * gain + shift, normed, inverse


def norm_backward(grad_out, normed, inverse, gain):
    grad_normed = grad_out * gain
    first_term = jnp.mean(grad_normed, axis=-1, keepdims=True)
    second_term = jnp.mean(grad_normed * normed, axis=-1, keepdims=True)
    grad_resid = inverse * (grad_normed - first_term - normed * second_term)
    return grad_resid, jnp.sum(grad_out * normed, axis=0), jnp.sum(grad_out, axis=0)


def on_device(
    hidden_in,
    teacher,
    lengths,
    qkv_weight,
    qkv_bias,
    out_weight,
    out_bias,
    ln_gain,
    ln_shift,
    ffn_in,
    ffn_in_bias,
    ffn_out,
):
    _, rows, width = hidden_in.shape
    dp_count = lax.axis_size("dp")
    dp_index = lax.axis_index("dp")
    seq_index = lax.axis_index("seq")
    group, role = seq_index // 2, seq_index % 2
    total_tokens = dp_count * rows * SEQ
    shard = qkv_weight.shape[1]
    half = width // 2
    ffn = ffn_in.shape[1]
    ffn_shard = ffn // dp_count
    ffn_half = ffn_shard // 2

    x_own = hidden_in.reshape(rows, width)
    target = teacher.reshape(rows, width)
    lens = lengths.reshape(CONT)

    length_sum = jnp.sum(lens).astype(F32)
    lanes = lambda value: jnp.pad(value, ((0, 0), (0, 128 - value.shape[1])))
    up_rows = -(-ffn_shard // 128)
    up_bias = jnp.pad(ffn_in_bias, (0, up_rows * 128 - ffn_shard)).reshape(up_rows, 128)
    small_rows = -(-(9 + up_rows) // 8) * 8
    small = jnp.concatenate(
        [
            lanes(qkv_bias),
            lanes(out_bias),
            lanes(ln_gain),
            lanes(ln_shift),
            up_bias,
            jnp.full((small_rows - 8 - up_rows, 128), length_sum, F32),
        ]
    )
    local_lens = jnp.where(role == 0, lens, jnp.roll(lens, CONT // 2))
    local_lens = jnp.where(group == 0, 0, local_lens)
    out_half = shard // 2
    up_piece = pick(ffn_in.reshape(shard, dp_count, 2, ffn_half), role, 2)
    out_piece = pick(out_weight.reshape(2, out_half, width), role, 0)
    down_piece = pick(ffn_out.reshape(2, ffn_half, width), role, 0)
    (w_high, w_low, small, xt_high, xt_low, k_both, v_both, queries, attended, lse,
     out_blocks, w_up, w_down, out_other) = run_forward(
        local_lens,
        lax.dynamic_slice_in_dim(qkv_weight, role * half, half, 2),
        small,
        x_own,
        out_piece.reshape(2, 3, out_half // 6, width),
        up_piece.reshape(2, 3, shard // 6, ffn // 2),
        down_piece.reshape(2, 3, ffn_half // 6, width),
    )
    w_up = w_up.reshape(width, ffn // 2)
    w_down = w_down.reshape(ffn // 2, width)
    out_mine = pick(out_blocks.reshape(2, dp_count // 2, out_half, width), role, 0)
    out_other = out_other.reshape(dp_count // 2, out_half, width)
    w_out = ordered(role, out_mine[:, None], out_other[:, None], 1).reshape(half, width)
    vectors = small[:, :8, :shard].transpose(1, 0, 2).reshape(4, 2, width)
    b_out, gains, shifts = vectors[1], vectors[2], vectors[3]
    b_up = small[:, 8 : 8 + up_rows].reshape(dp_count, up_rows * 128)[:, :ffn_shard]
    b_up = pick(b_up.reshape(dp_count, 2, ffn_half), role, 1).reshape(ffn // 2)
    count = float(dp_count * PROMPT) + jnp.sum(small[:, small_rows - 1, 0])

    def reduce_pair(partial):
        return partial[:rows] + swap_pair(partial[rows:])

    def both_halves(own):
        return jnp.concatenate([own, swap_pair(own)], axis=0)

    first_resid = x_own + reduce_pair(mm(attended, w_out)) + b_out[0]
    first_norm, first_hat, first_inv = norm_forward(first_resid, gains[0], shifts[0])
    norm_group = both_halves(first_norm)
    pre_act = mm(norm_group, w_up) + b_up
    normal_cdf = 0.5 * (1.0 + lax.erf(pre_act * INV_ROOT_TWO))
    activated = pre_act * normal_cdf
    slope = normal_cdf + pre_act * jnp.exp(-0.5 * pre_act * pre_act) * INV_ROOT_TAU
    second_resid = first_norm + reduce_pair(mm(activated, w_down)) + b_out[1]
    final, second_hat, second_inv = norm_forward(second_resid, gains[1], shifts[1])

    slot = seq_index * rows + jnp.arange(rows, dtype=jnp.int32) - PROMPT
    own_len = jnp.sum(
        jnp.where((slot // CLEN)[None] == jnp.arange(CONT, dtype=jnp.int32)[:, None], lens[:, None], 0),
        axis=0,
    )
    valid = ((slot < 0) | (slot % CLEN < own_len)).astype(F32)
    difference = (final - target) * valid[:, None]
    squares = jnp.sum(difference * difference)
    grad_final = difference * (total_tokens / count)
    grad_second, grad_gain_two, grad_shift_two = norm_backward(
        grad_final, second_hat, second_inv, gains[1]
    )
    grad_bias_down = jnp.sum(grad_second, axis=0)
    second_group = both_halves(grad_second)
    grad_w_down = mm_tn(activated, second_group)
    ybit = dp_index & 1
    early = dp_count <= 8
    if early:
        down = grad_w_down.reshape(dp_count // 2, 2, 2, 2, ffn_half // 4, width)
        down_a, down_b = down[:, :, :, 0], down[:, :, :, 1]
        send_a, send_b = pick(down_a, ybit ^ 1, 1), pick(down_b, group ^ 1, 2)
        keep_a, keep_b = pick(down_a, ybit, 1), pick(down_b, group, 2)
        second_group, send_a, send_b = lax.optimization_barrier((second_group, send_a, send_b))
        come_a, come_b = swap_dp(send_a, 0), swap_group(send_b)
    grad_pre = mm_nt(second_group, w_down) * slope
    grad_b_up = jnp.sum(grad_pre, axis=0)
    grad_w_up = mm_tn(norm_group, grad_pre)
    if early:
        grad_w_up, come_a, come_b = lax.optimization_barrier((grad_w_up, come_a, come_b))
        down_a, down_b = keep_a + come_a, keep_b + come_b
        send_a, send_b = pick(down_a, group ^ 1, 1), pick(down_b, ybit ^ 1, 1)
        keep_a, keep_b = pick(down_a, group, 1), pick(down_b, ybit, 1)
        grad_pre, send_a, send_b = lax.optimization_barrier((grad_pre, send_a, send_b))
        come_a, come_b = swap_group(send_a), swap_dp(send_b, 0)
    if not early:
        share_down = scatter_rows(grad_w_down)
    grad_first_norm = grad_second + reduce_pair(mm_nt(grad_pre, w_up))
    grad_first, grad_gain_one, grad_shift_one = norm_backward(
        grad_first_norm, first_hat, first_inv, gains[0]
    )
    grad_bias_out = jnp.sum(grad_first, axis=0)
    first_group = both_halves(grad_first)
    grad_attended = mm_nt(first_group, w_out)
    if early:
        grad_attended, come_a, come_b = lax.optimization_barrier((grad_attended, come_a, come_b))
        half_down = jnp.stack([keep_a + come_a, keep_b + come_b], axis=1)
    grad_w_out = mm_tn(attended, first_group)
    mine = grad_w_out.reshape(dp_count // 2, 2, out_half, width)
    received = swap_pair(pick(mine, 1 - role, 1))
    mine = ordered(role, pick(mine, role, 1), received, 0)
    up = jnp.zeros((dp_count, 2, ffn_half), F32)
    up = lax.dynamic_update_slice(up, grad_b_up.reshape(dp_count, 1, ffn_half), (0, role, 0))
    up = jnp.pad(up.reshape(dp_count, ffn_shard), ((0, 0), (0, up_rows * 128 - ffn_shard)))

    def small_block(bias_q, bias_v):
        vectors = jnp.stack(
            [
                bias_q,
                bias_v,
                grad_bias_out,
                grad_bias_down,
                grad_gain_one,
                grad_gain_two,
                grad_shift_one,
                grad_shift_two,
            ]
        )
        vectors = vectors.reshape(8, dp_count, shard).transpose(1, 0, 2)
        return jnp.concatenate(
            [
                jnp.pad(vectors, ((0, 0), (0, 0), (0, 128 - shard))),
                up.reshape(dp_count, up_rows, 128),
                jnp.full((dp_count, small_rows - 8 - up_rows, 128), squares, F32),
            ],
            axis=1,
        )

    def join(share, axis):
        return ordered(role, share, swap_pair(share), axis)

    if early:
        (grad_input, up_mine, up_other, out_mine, out_other, down_mine, down_other,
         qkv_mine, qkv_other, small) = run_backward(
            local_lens, lse, xt_high, xt_low, w_high, w_low,
            small_block(jnp.zeros((width,), F32), jnp.zeros((width,), F32)),
            queries, k_both, v_both, attended, grad_attended, grad_first,
            grad_w_up.reshape(dp_count, 2, 3, shard // 6, ffn // 2),
            mine.reshape(dp_count, 2, 3, out_half // 6, width),
            half_down,
        )
        lay = lambda value: value.transpose(1, 2, 0, 3).reshape(3, shard, half)
        out_qkv = ordered(role, lay(qkv_mine), lay(qkv_other), 2)
        out_out = ordered(
            role, out_mine.reshape(out_half, width), out_other.reshape(out_half, width), 0
        )
        lay = lambda value: value.reshape(shard, dp_count, 1, ffn_half)
        out_up = ordered(role, lay(up_mine), lay(up_other), 2).reshape(shard, ffn)
        out_down = ordered(
            role, down_mine.reshape(ffn_half, width), down_other.reshape(ffn_half, width), 0
        )
    else:
        share_up = scatter_rows(grad_w_up)
        d_q, d_kp, d_vp, d_ks, d_vs = attend_backward(
            local_lens, queries, k_both, v_both, attended, grad_attended, lse
        )
        weights = w_high.astype(F32) + w_low.astype(F32)
        w_q, w_k, w_v = weights[0], weights[1], weights[2]
        x_t = xt_high.astype(F32) + xt_low.astype(F32)
        on_prompt = reduce_pair(mm_nt(d_kp, w_k) + mm_nt(d_vp, w_v))
        from_cont = lax.ppermute(on_prompt, "seq", [(2, 0), (3, 1)])
        grad_w_k = mm(x_t, jnp.concatenate([d_kp, d_ks], axis=0))
        grad_w_v = mm(x_t, jnp.concatenate([d_vp, d_vs], axis=0))
        grad_w_q = mm(x_t[:, 2 * rows :], d_q)
        on_own = reduce_pair(mm_nt(d_q, w_q) + mm_nt(d_ks, w_k) + mm_nt(d_vs, w_v))
        grad_input = grad_first + on_own + jnp.where(group == 0, on_prompt + from_cont, 0.0)

        def widen(value):
            return lax.dynamic_update_slice(jnp.zeros((width,), F32), value, (role * half,))

        share_qkv, share_out, small, other_qkv, other_out = scatter_all(
            jnp.stack([grad_w_q, grad_w_k, grad_w_v]).reshape(3, dp_count, shard, half),
            mine.reshape(dp_count, out_half, width),
            small_block(
                widen(jnp.sum(d_q, axis=0)),
                widen(jnp.sum(d_vp, axis=0) + jnp.sum(d_vs, axis=0)),
            ),
        )
        out_qkv = ordered(role, share_qkv, other_qkv, 2)
        out_out = ordered(role, share_out, other_out, 0)
        out_up = join(share_up.reshape(shard, dp_count, 1, ffn_half), 2).reshape(shard, ffn)
        out_down = join(share_down.reshape(ffn_half, width), 0)
    pairs = small[:8, :shard].reshape(4, 2, shard)
    out_b_up = small[8 : 8 + up_rows].reshape(up_rows * 128)[:ffn_shard]
    loss = small[small_rows - 1, 0] / (count * width)
    return (
        final[None],
        grad_input[None],
        out_qkv,
        pairs[0],
        out_out,
        pairs[1],
        pairs[2],
        pairs[3],
        out_up,
        out_b_up,
        out_down,
        loss,
    )


def solution(mesh):
    return jax.shard_map(
        on_device,
        mesh=mesh,
        in_specs=(
            P("dp", "seq", None),
            P("dp", "seq", None),
            P("dp", None),
            P(None, "dp", None),
            P(None, "dp"),
            P("dp", None),
            P(None, "dp"),
            P(None, "dp"),
            P(None, "dp"),
            P("dp", None),
            P("dp"),
            P("dp", None),
        ),
        out_specs=(
            P("dp", "seq", None),
            P("dp", "seq", None),
            P(None, "dp", None),
            P(None, "dp"),
            P("dp", None),
            P(None, "dp"),
            P(None, "dp"),
            P(None, "dp"),
            P("dp", None),
            P("dp"),
            P("dp", None),
            P(),
        ),
        check_vma=False,
    )
```

```python
import functools

import jax
import jax.numpy as jnp
from jax import lax
from jax.experimental import pallas as pl
from jax.experimental.pallas import tpu as pltpu
from jax.sharding import PartitionSpec as P

HD = 64
PROMPT = 1024
CONT = 8
CLEN = 128
SEQ = 4
QB = 256

HIGH = lax.Precision.HIGH
EPSILON = 1e-05
MASKED = -1e30
INV_ROOT_TWO = 0.7071067811865476
INV_ROOT_TAU = 0.3989422804014327
BF = jnp.bfloat16
F32 = jnp.float32


def mm(left, right):
    return lax.dot_general(
        left, right, (((1,), (0,)), ((), ())), precision=HIGH, preferred_element_type=F32
    )


def mm_nt(left, right):
    return lax.dot_general(
        left, right, (((1,), (1,)), ((), ())), precision=HIGH, preferred_element_type=F32
    )


def mm_tn(left, right):
    return lax.dot_general(
        left, right, (((0,), (0,)), ((), ())), precision=HIGH, preferred_element_type=F32
    )


def swap_pair(value):
    return lax.ppermute(value, "seq", [(i, i ^ 1) for i in range(SEQ)])


def swap_group(value):
    return lax.ppermute(value, "seq", [(i, i ^ 2) for i in range(SEQ)])


def swap_dp(value, bit):
    count = lax.axis_size("dp")
    return lax.ppermute(value, "dp", [(i, i ^ (1 << bit)) for i in range(count)])


def ordered(bit, own, other, axis):
    first = jnp.where(bit == 0, own, other)
    second = jnp.where(bit == 0, other, own)
    return jnp.concatenate([first, second], axis=axis)


def pick(value, index, axis):
    return lax.dynamic_index_in_dim(value, index, axis, keepdims=False)


def dp_bits():
    return lax.axis_size("dp").bit_length() - 1


def gather_rows(piece, axis=0):
    return lax.all_gather(piece, "dp", axis=axis, tiled=True)


def scatter_rows(grads, axis=0):
    share = lax.psum_scatter(grads, "dp", scatter_dimension=axis, tiled=True)
    return share + swap_group(share)


def partner(dp_mask, seq_mask):
    return (lax.axis_index("dp") ^ dp_mask, lax.axis_index("seq") ^ seq_mask)


def remote(src, dst, send_sem, recv_sem, target):
    return pltpu.make_async_remote_copy(
        src_ref=src,
        dst_ref=dst,
        send_sem=send_sem,
        recv_sem=recv_sem,
        device_id=target,
        device_id_type=pl.DeviceIdType.MESH,
    )


def greet(bits):
    barrier = pltpu.get_barrier_semaphore()
    others = [partner(1 << bit, 0) for bit in range(bits)] + [partner(0, 1), partner(0, 2)]
    for other in others:
        pl.semaphore_signal(
            barrier, inc=1, device_id=other, device_id_type=pl.DeviceIdType.MESH
        )
    pl.semaphore_wait(barrier, len(others))


def greet_line(has_up, has_down, above, below):
    barrier = pltpu.get_barrier_semaphore()

    def hello(other):
        pl.semaphore_signal(
            barrier, inc=1, device_id=other, device_id_type=pl.DeviceIdType.MESH
        )

    for other in (partner(1, 0), partner(0, 1), partner(0, 2)):
        hello(other)
    for there, other in ((has_up, above), (has_down, below)):
        @pl.when(there)
        def _(other=other):
            hello(other)
    ends = jnp.where(has_up, 1, 0) + jnp.where(has_down, 1, 0)
    pl.semaphore_wait(barrier, 3 + ends)


def line_arrival(level, layers, index):
    both_sides = jnp.minimum(level, layers - 1 - level)
    paired = index <= 2 * both_sides
    distance = jnp.where(paired, (index + 1) // 2, index - both_sides)
    upward = jnp.where(paired, index % 2 == 0, level < layers - 1 - level)
    return jnp.where(upward, level + distance, level - distance)


def hop_masks(bits):
    return [1 << bit for bit in range(1, bits)] + [1]


def slot_mask(bits, relative):
    masks = hop_masks(bits)
    return sum(masks[p] for p in range(bits) if relative >> p & 1)


def scatter_kernel(bits, *refs):
    kinds = 3
    grads, refs = refs[:kinds], refs[kinds:]
    mine, refs = refs[:kinds], refs[kinds:]
    other, refs = refs[: kinds - 1], refs[kinds - 1 :]
    acc, refs = refs[:kinds], refs[kinds:]
    hop_in, refs = refs[:kinds], refs[kinds:]
    x_in, refs = refs[:kinds], refs[kinds:]
    pair_in, send_sem, recv_sem, x_send, x_recv, load_sem, store_sem = refs
    me = lax.axis_index("dp")
    masks = hop_masks(bits)
    count = 1 << bits

    def source(kind, relative):
        slot = me ^ slot_mask(bits, relative)
        return grads[kind].at[:, slot] if kind == 0 else grads[kind].at[slot]

    def hop_copy(kind, relative, hop, from_input):
        index = relative ^ (1 << hop)
        src = source(kind, relative) if from_input else acc[kind].at[relative]
        place = (1 << hop) + index
        return remote(
            src, hop_in[kind].at[place], send_sem.at[kind, relative], recv_sem.at[kind, place],
            partner(masks[hop], 0),
        )

    loads = {}
    for relative in reversed(range(count // 2)):
        for kind in range(kinds):
            copy = pltpu.make_async_copy(
                source(kind, relative), acc[kind].at[relative], load_sem.at[kind, relative]
            )
            copy.start()
            loads[kind, relative] = copy
    greet(bits)
    started = []
    last = bits - 1
    for relative in reversed(range(count // 2, count)):
        for kind in range(kinds):
            copy = hop_copy(kind, relative, last, True)
            copy.start()
            started.append(copy)
    for relative in reversed(range(count // 2)):
        for kind in range(kinds):
            loads[kind, relative].wait()
        lowest = relative.bit_length() - 1
        for hop in reversed(range(max(lowest + 1, 0), bits)):
            for kind in range(kinds):
                hop_copy(kind, relative | (1 << hop), hop, hop == last).wait_recv()
                acc[kind][relative] += hop_in[kind][(1 << hop) + relative]
        if relative:
            for kind in range(kinds):
                copy = hop_copy(kind, relative, lowest, False)
                copy.start()
                started.append(copy)
    crossing = []
    for kind in range(kinds):
        copy = remote(acc[kind].at[0], x_in[kind], x_send.at[kind], x_recv.at[kind], partner(0, 2))
        copy.start()
        crossing.append(copy)
    for kind in range(kinds):
        crossing[kind].wait_recv()
        mine[kind][...] = acc[kind][0] + x_in[kind][...]
    handing = []
    for kind in range(kinds - 1):
        copy = remote(
            mine[kind], other[kind], x_send.at[kinds + kind], x_recv.at[kinds + kind], partner(0, 1)
        )
        copy.start()
        handing.append(copy)
    copy = remote(
        mine[kinds - 1], pair_in, x_send.at[2 * kinds - 1], x_recv.at[2 * kinds - 1], partner(0, 1)
    )
    copy.start()
    handing.append(copy)
    for copy in handing:
        copy.wait()
    mine[kinds - 1][...] += pair_in[...]
    for copy in started + crossing:
        copy.wait_send()


def scatter_all(qkv, out, small):
    bits = dp_bits()
    count = 1 << bits
    any_spec = pl.BlockSpec(memory_space=pl.ANY)
    vmem = pl.BlockSpec(memory_space=pltpu.VMEM)
    shapes = [(qkv.shape[0],) + qkv.shape[2:], out.shape[1:], small.shape[1:]]
    like = [jax.ShapeDtypeStruct(shape, F32) for shape in shapes]
    return pl.pallas_call(
        functools.partial(scatter_kernel, bits),
        in_specs=[any_spec] * 3,
        out_specs=[vmem] * 5,
        out_shape=like + like[:2],
        scratch_shapes=[pltpu.VMEM((count // 2,) + shape, F32) for shape in shapes]
        + [pltpu.VMEM((count,) + shape, F32) for shape in shapes]
        + [pltpu.VMEM(shape, F32) for shape in shapes]
        + [
            pltpu.VMEM(shapes[2], F32),
            pltpu.SemaphoreType.DMA((3, count)),
            pltpu.SemaphoreType.DMA((3, count)),
            pltpu.SemaphoreType.DMA((6,)),
            pltpu.SemaphoreType.DMA((6,)),
            pltpu.SemaphoreType.DMA((3, count // 2)),
            pltpu.SemaphoreType.DMA((1,)),
        ],
        compiler_params=pltpu.CompilerParams(
            collective_id=2, has_side_effects=True, vmem_limit_bytes=40 << 20
        ),
        cost_estimate=pl.CostEstimate(
            flops=0, bytes_accessed=(qkv.size + out.size) * 4 * 12, transcendentals=0
        ),
        name="scatter_attention_grads",
    )(qkv, out, small)


def lane_ids(shape):
    return lax.broadcasted_iota(jnp.int32, shape, 1)


def high_low(value):
    high = value.astype(BF).astype(F32)
    return high, value - high


def packs(value, head):
    high, low = high_low(value)
    left = lane_ids(value.shape) < HD
    high_r = pltpu.roll(high, HD, 1)
    low_r = pltpu.roll(low, HD, 1)
    if head == 0:
        return (
            jnp.where(left, high, low_r).astype(BF),
            jnp.where(left, high, high_r).astype(BF),
            jnp.where(left, low, low_r).astype(BF),
        )
    return (
        jnp.where(left, high_r, low).astype(BF),
        jnp.where(left, high_r, high).astype(BF),
        jnp.where(left, low_r, low).astype(BF),
    )


def dot(left, right):
    return lax.dot_general(left, right, (((1,), (0,)), ((), ())), preferred_element_type=F32)


def dot_nt(left, right):
    return lax.dot_general(left, right, (((1,), (1,)), ((), ())), preferred_element_type=F32)


def split(value):
    high = value.astype(BF)
    return high, (value - high.astype(F32)).astype(BF)


def self_mask(lens_ref, block, query_axis):
    key_axis = 1 - query_axis
    query = lax.broadcasted_iota(jnp.int32, (QB, QB), query_axis)
    key = lax.broadcasted_iota(jnp.int32, (QB, QB), key_axis)
    per = QB // CLEN
    seen = jnp.zeros((QB, QB), jnp.bool_)
    for piece in range(per):
        low = piece * CLEN
        limit = low + lens_ref[block * per + piece]
        inside = (query >= low) & (query < low + CLEN) & (key >= low) & (key < limit)
        seen = seen | inside
    return seen & (key <= query)


THIRDS = ((0, 1), (1, 2))


def forward_kernel(bits, lens_ref, w_ref, s_ref, x_ref, out_ref, up_ref, down_ref,
                   w_high, w_low, s_all, xt_high, xt_low, k_both, v_both, q_all, o_all, lse_all,
                   out_all, up_all, down_all, out_other,
                   w_all, x_both, x_high, x_low, q4, k4p, k4s, v2p, v2s,
                   out_buf, up_buf, down_buf,
                   send_sem, recv_sem, x_send, x_recv, own_sem, hop_send, hop_recv, pair_sem):
    me = lax.axis_index("dp")
    seq = lax.axis_index("seq")
    group, role = seq // 2, seq % 2
    rows, width = x_ref.shape
    half = w_ref.shape[2]
    layers = 1 << (bits - 1)
    quarter = layers // 4
    level, side = me // 2, me % 2
    has_up, has_down = level < layers - 1, level > 0
    above, below = (me + 2, seq), (me - 2, seq)
    greet_line(has_up, has_down, above, below)
    arrival = functools.partial(line_arrival, level, layers)

    pieces = ((out_ref, out_buf, out_all), (up_ref, up_buf, up_all), (down_ref, down_buf, down_all))
    loads = [pltpu.make_async_copy(src, buf, own_sem.at[i]) for i, (src, buf, _) in enumerate(pieces)]
    own_w = pltpu.make_async_copy(w_ref, w_all.at[:, me], own_sem.at[3])
    own_s = pltpu.make_async_copy(s_ref, s_all.at[me], own_sem.at[4])
    own_x = pltpu.make_async_copy(x_ref, x_both.at[pl.ds(2 * rows, rows)], own_sem.at[5])
    for copy in loads + [own_w, own_s, own_x]:
        copy.start()
    to_pair = remote(
        x_ref, x_both.at[pl.ds(3 * rows, rows)], x_send.at[0], x_recv.at[0], partner(0, 1)
    )
    to_far = remote(x_ref, x_both.at[pl.ds(0, rows)], x_send.at[1], x_recv.at[1], partner(0, 2))
    far_pair = remote(
        x_both.at[pl.ds(0, rows)], x_both.at[pl.ds(rows, rows)], x_send.at[2], x_recv.at[2],
        partner(0, 1),
    )
    to_pair.start()

    @pl.when(group == 0)
    def _():
        to_far.start()

    def attention_copies(slot, step, from_input=False):
        target = (above, below, partner(1, 0))[step]
        regions = (w_all.at[:, slot], s_all.at[slot])
        return [
            remote(
                (w_ref, s_ref)[kind] if from_input else region, region,
                send_sem.at[kind, slot, step], recv_sem.at[kind, slot], target,
            )
            for kind, region in enumerate(regions)
        ]

    def along(at, upward, downward):
        @pl.when((at <= level) & has_up)
        def _():
            upward()

        @pl.when((at >= level) & has_down)
        def _():
            downward()

    def starts(slot, step, from_input=False):
        for copy in attention_copies(slot, step, from_input):
            copy.start()

    def sends(slot, step):
        for copy in attention_copies(slot, step):
            copy.wait_send()

    along(level, lambda: starts(me, 0, True), lambda: starts(me, 1, True))
    starts(me, 2, True)
    for copy in loads:
        copy.wait()
    stores = [pltpu.make_async_copy(buf, dst.at[me], own_sem.at[i]) for i, (_, buf, dst) in enumerate(pieces)]
    for copy in stores:
        copy.start()

    def part(kind, layer, last, other_x, piece):
        first, count = THIRDS[piece]
        return pieces[kind][2].at[
            layer * 2 + (side ^ last), group ^ other_x, pl.ds(first, count)
        ]

    def sent(kind, layer, last, other_x, piece, step, dp_mask, seq_mask):
        region = part(kind, layer, last, other_x, piece)
        return remote(
            region, region, hop_send.at[kind, layer, step], hop_recv.at[kind, layer, step],
            partner(dp_mask, seq_mask),
        )

    steps = {
        1: (0, 0, 0, 0, 2),
        2: (0, 0, 0, 1, 0),
        3: (0, 1, 0, 1, 0),
        4: (0, 0, 1, 1, 0),
        5: (0, 0, 1, 0, 2),
        6: (1, 0, 1, 0, 2),
    }

    def give(kind, layer, step):
        last, other_x, piece, dp_mask, seq_mask = steps[step]
        return sent(kind, layer, last, other_x, piece, step, dp_mask, seq_mask)

    def take(kind, layer, step):
        last, other_x, piece, dp_mask, seq_mask = steps[step]
        return sent(
            kind, layer, last ^ dp_mask, other_x ^ (seq_mask // 2), piece, step, dp_mask, seq_mask
        )

    def climb(kind, layer, upward):
        region = pieces[kind][2].at[layer * 2 + side, group]
        return remote(
            region, region, hop_send.at[kind, layer, 0 if upward else 7],
            hop_recv.at[kind, layer, 0], above if upward else below,
        )

    def pass_on(kind, layer):
        along(
            layer, lambda: climb(kind, layer, True).start(), lambda: climb(kind, layer, False).start()
        )

    def spread(kind, index):
        layer = arrival(index)

        @pl.when(index > 0)
        def _():
            climb(kind, layer, True).wait_recv()
            pass_on(kind, layer)
            give(kind, layer, 1).start()
            give(kind, layer, 5).start()

        give(kind, layer, 4).start()
        give(kind, layer, 2).start()

    def relay(kind, index):
        layer = arrival(index)

        @pl.when(index > 0)
        def _():
            take(kind, layer, 1).wait_recv()

        give(kind, layer, 3).start()
        take(kind, layer, 4).wait_recv()
        give(kind, layer, 6).start()

    def settle(kind, layer):
        take(kind, layer, 2).wait_recv()
        take(kind, layer, 3).wait_recv()
        take(kind, layer, 6).wait_recv()

        @pl.when(layer != level)
        def _():
            take(kind, layer, 5).wait_recv()

    def drained(kind, layer):
        @pl.when(layer != level)
        def _():
            give(kind, layer, 1).wait_send()
            give(kind, layer, 5).wait_send()

        for step in (2, 3, 4, 6):
            give(kind, layer, step).wait_send()
        along(
            layer,
            lambda: climb(kind, layer, True).wait_send(),
            lambda: climb(kind, layer, False).wait_send(),
        )

    def over(action, kind, position):
        def body(index, carry):
            action(kind, position * quarter + index)
            return carry

        lax.fori_loop(0, quarter, body, 0)

    for copy in stores:
        copy.wait()

    def receive(index, carry):
        at = arrival(index)
        slot = at * 2 + side
        for copy in attention_copies(slot, 0):
            copy.wait_recv()
        along(at, lambda: starts(slot, 0), lambda: starts(slot, 1))
        starts(slot, 2)
        return carry

    lax.fori_loop(1, layers, receive, 0)
    for kind in range(3):
        pass_on(kind, level)

    def receive_side(index, carry):
        for copy in attention_copies(arrival(index) * 2 + (side ^ 1), 2):
            copy.wait_recv()
        return carry

    lax.fori_loop(0, layers, receive_side, 0)
    for position in range(4):
        over(spread, 0, position)
    over(spread, 1, 0)

    own_x.wait()
    to_pair.wait_recv()

    @pl.when(group == 1)
    def _():
        to_far.wait_recv()
        far_pair.start()
        far_pair.wait_recv()

    def halves(index, carry):
        here = pl.ds(pl.multiple_of(index * QB, QB), QB)

        @pl.when((group == 0) & (index < 2 * rows // QB))
        def _():
            x_both[here, :] = x_both[pl.ds(pl.multiple_of(index * QB + 2 * rows, QB), QB), :]

        high, low = split(x_both[here, :])
        x_high[here, :] = high
        x_low[here, :] = low
        high, low = split(jnp.transpose(x_both[here, :]))
        xt_high[:, here] = high
        xt_low[:, here] = low
        return carry

    lax.fori_loop(0, 4 * rows // QB, halves, 0)
    own_w.wait()
    own_s.wait()
    count = 1 << bits
    shard = width // count
    for index in range(3):
        for slot in range(count):
            high, low = split(w_all[index, slot])
            w_high[index, pl.ds(slot * shard, shard), :] = high
            w_low[index, pl.ds(slot * shard, shard), :] = low
    bias = jnp.zeros((8, width), F32)
    blank = jnp.zeros((8, width - 128), F32)
    for slot in range(count):
        row = jnp.concatenate([s_all[slot, :8, :], blank], axis=1)
        bias = bias + (pltpu.roll(row, shard * slot, 1) if slot else row)
    bias = jnp.where(role == 0, bias[:2, :half], bias[:2, half:])

    def project(index, here):
        high, low = x_high[here, :], x_low[here, :]
        return (
            dot(high, w_high[index]) + dot(high, w_low[index]) + dot(low, w_high[index])
        )


    def keys_values(index, carry):
        here = pl.ds(pl.multiple_of(index * QB, QB), QB)
        @pl.when(index >= 4)
        def _():
            over(relay, 0, index - 4)

        k_both[here, :] = project(1, here)
        v_both[here, :] = project(2, here) + bias[1:2]
        return carry

    lax.fori_loop(0, 8, keys_values, 0)

    def queries(index, carry):
        here = pl.ds(pl.multiple_of(index * QB, QB), QB)
        @pl.when((index == 0) | (index == 2))
        def _():
            over(spread, 1, 1 + index // 2)

        q_all[here, :] = project(0, pl.ds(pl.multiple_of(index * QB + 2 * rows, QB), QB)) + bias[:1]
        return carry

    lax.fori_loop(0, 4, queries, 0)

    for pair in range(half // 128):
        lanes = pl.ds(pair * 128, 128)
        for head in range(2):
            _, hh, ll = packs(q_all[:, lanes] * 0.125, head)
            q4[head, :, :128] = hh
            q4[head, :, 128:] = ll
            for start, key4, value2 in ((0, k4p, v2p), (2 * rows, k4s, v2s)):
                hl, _, _ = packs(k_both[pl.ds(start, 2 * rows), lanes], head)
                key4[head, :, :128] = hl
                key4[head, :, 128:] = hl
                value2[head] = packs(v_both[pl.ds(start, 2 * rows), lanes], head)[0]

        def attend(block, carry):
            if pair == 0:
                @pl.when(block == 0)
                def _():
                    over(spread, 1, 3)

                @pl.when(block > 0)
                def _():
                    over(spread, 2, block - 1)

                over(relay, 1, block)
            if pair == 1:
                @pl.when(block == 1)
                def _():
                    over(spread, 2, 3)

                @pl.when(block > 0)
                def _():
                    over(relay, 2, block - 1)
            if pair == 2:
                @pl.when(block == 2)
                def _():
                    over(relay, 2, 3)

            here = pl.ds(pl.multiple_of(block * QB, QB), QB)
            seen = self_mask(lens_ref, block, 0)
            results = []
            for head in range(2):
                query = q4[head, here, :]
                far = dot_nt(query, k4p[head])
                near = jnp.where(seen, dot_nt(query, k4s[head, here, :]), MASKED)
                top = jnp.maximum(
                    jnp.max(far, axis=1, keepdims=True), jnp.max(near, axis=1, keepdims=True)
                )
                far = jnp.exp(far - top)
                near = jnp.exp(near - top)
                total = jnp.sum(far, axis=1, keepdims=True) + jnp.sum(near, axis=1, keepdims=True)
                far_h, far_l = split(far)
                near_h, near_l = split(near)
                out = dot(far_h, v2p[head]) + dot(far_l, v2p[head])
                value = v2s[head, here, :]
                out = out + dot(near_h, value) + dot(near_l, value)
                out = (out + pltpu.roll(out, HD, 1)) / total
                lse = top + jnp.log(total)
                lse_all[2 * pair + head, :, here] = jnp.transpose(
                    jnp.broadcast_to(lse, (QB, 128))
                )[:8]
                results.append(out)
            o_all[here, lanes] = jnp.where(lane_ids((QB, 128)) < HD, results[0], results[1])
            return carry

        lax.fori_loop(0, 4, attend, 0)

    def last(index, carry):
        for kind in range(3):
            settle(kind, index)
        return carry

    lax.fori_loop(0, layers, last, 0)
    part_count = count // 2
    swap = remote(
        out_all.at[pl.ds((1 - role) * part_count, part_count)], out_other, pair_sem.at[0],
        pair_sem.at[1], partner(0, 1),
    )
    swap.start()

    def ended(index, carry):
        for kind in range(3):
            drained(kind, index)
        return carry

    lax.fori_loop(0, layers, ended, 0)
    def passed(index, carry):
        slot = index * 2 + side
        along(index, lambda: sends(slot, 0), lambda: sends(slot, 1))
        sends(slot, 2)
        return carry

    lax.fori_loop(0, layers, passed, 0)
    to_pair.wait_send()

    @pl.when(group == 0)
    def _():
        to_far.wait_send()

    @pl.when(group == 1)
    def _():
        far_pair.wait_send()

    swap.wait()


def run_forward(lens, weights, small, tokens, out_piece, up_piece, down_piece):
    bits = dp_bits()
    count = 1 << bits
    layers = count // 2
    anywhere = pl.BlockSpec(memory_space=pl.ANY)
    vmem = pl.BlockSpec(memory_space=pltpu.VMEM)
    three, shard, half = weights.shape
    rows, width = tokens.shape
    heads = half // HD
    shape = lambda *dims: jax.ShapeDtypeStruct(dims, F32)
    whole = lambda piece: shape(count, *piece.shape)
    return pl.pallas_call(
        functools.partial(forward_kernel, bits),
        in_specs=[pl.BlockSpec(memory_space=pltpu.SMEM)] + [anywhere] * 6,
        out_specs=[vmem] * 10 + [anywhere] * 4,
        out_shape=[
            jax.ShapeDtypeStruct((three, width, half), BF),
            jax.ShapeDtypeStruct((three, width, half), BF),
            shape(count, *small.shape),
            jax.ShapeDtypeStruct((width, 4 * rows), BF),
            jax.ShapeDtypeStruct((width, 4 * rows), BF),
            shape(4 * rows, half),
            shape(4 * rows, half),
            shape(2 * rows, half),
            shape(2 * rows, half),
            shape(heads, 8, 2 * rows),
            whole(out_piece),
            whole(up_piece),
            whole(down_piece),
            shape(count // 2, *out_piece.shape),
        ],
        scratch_shapes=[
            pltpu.VMEM((three, count, shard, half), F32),
            pltpu.VMEM((4 * rows, width), F32),
            pltpu.VMEM((4 * rows, width), BF),
            pltpu.VMEM((4 * rows, width), BF),
            pltpu.VMEM((2, 2 * rows, 256), BF),
            pltpu.VMEM((2, 2 * rows, 256), BF),
            pltpu.VMEM((2, 2 * rows, 256), BF),
            pltpu.VMEM((2, 2 * rows, 128), BF),
            pltpu.VMEM((2, 2 * rows, 128), BF),
            pltpu.VMEM(out_piece.shape, F32),
            pltpu.VMEM(up_piece.shape, F32),
            pltpu.VMEM(down_piece.shape, F32),
            pltpu.SemaphoreType.DMA((2, count, 3)),
            pltpu.SemaphoreType.DMA((2, count)),
            pltpu.SemaphoreType.DMA((3,)),
            pltpu.SemaphoreType.DMA((3,)),
            pltpu.SemaphoreType.DMA((6,)),
            pltpu.SemaphoreType.DMA((3, layers, 8)),
            pltpu.SemaphoreType.DMA((3, layers, 7)),
            pltpu.SemaphoreType.DMA((2,)),
        ],
        compiler_params=pltpu.CompilerParams(
            collective_id=1, has_side_effects=True, vmem_limit_bytes=60 << 20
        ),
        name="gather_weights_and_attend",
    )(lens, weights, small, tokens, out_piece, up_piece, down_piece)


def backward_kernel(lens_ref, q_ref, kp_ref, vp_ref, ks_ref, vs_ref, o_ref, g_ref, lse_ref,
                    dq_ref, dkp_ref, dvp_ref, dks_ref, dvs_ref,
                    q4, k4p, k4s, v4p, v4s, g4, q2, g2, k2tp, k2ts, delta):
    rows = q_ref.shape[0]
    prod = jnp.transpose(o_ref[...] * g_ref[...])
    for head in range(2):
        hl, hh, ll = packs(q_ref[...] * 0.125, head)
        q2[head] = hl
        q4[head, :, :128] = hh
        q4[head, :, 128:] = ll
        hl, hh, ll = packs(g_ref[...], head)
        g2[head] = hl
        g4[head, :, :128] = hh
        g4[head, :, 128:] = ll
        for src, dst in ((kp_ref, k4p), (ks_ref, k4s), (vp_ref, v4p), (vs_ref, v4s)):
            hl, _, _ = packs(src[...], head)
            dst[head, :, :128] = hl
            dst[head, :, 128:] = hl
        for src, dst in ((kp_ref, k2tp), (ks_ref, k2ts)):
            flipped = jnp.transpose(src[...])[head * HD : head * HD + HD]
            high, low = high_low(flipped)
            dst[head, :HD] = high.astype(BF)
            dst[head, HD:] = low.astype(BF)
        delta[head] = jnp.broadcast_to(
            jnp.sum(prod[head * HD : head * HD + HD], axis=0, keepdims=True), (8, rows)
        )
    dkp_ref[...] = jnp.zeros_like(dkp_ref)
    dvp_ref[...] = jnp.zeros_like(dvp_ref)

    def step(block, carry):
        here = pl.ds(pl.multiple_of(block * QB, QB), QB)
        seen = self_mask(lens_ref, block, 1)
        keep = {}
        for head in range(2):
            query = q4[head, here, :]
            grad = g4[head, here, :]
            lse = lse_ref[head, :1, here]
            low = delta[head, :1, here]
            far = jnp.exp(dot_nt(k4p[head], query) - lse)
            near = jnp.exp(jnp.where(seen, dot_nt(k4s[head, here, :], query), MASKED) - lse)
            far_g = far * (dot_nt(v4p[head], grad) - low)
            near_g = near * (dot_nt(v4s[head, here, :], grad) - low)
            grad2 = g2[head, here, :]
            query2 = q2[head, here, :]
            ph, p_l = split(far)
            dvp = dot(ph, grad2) + dot(p_l, grad2)
            ph, p_l = split(near)
            dvs = dot(ph, grad2) + dot(p_l, grad2)
            sh, sl = split(far_g)
            dkp = dot(sh, query2) + dot(sl, query2)
            dq = dot(k2tp[head], sh) + dot(k2tp[head], sl)
            sh, sl = split(near_g)
            dks = dot(sh, query2) + dot(sl, query2)
            side = k2ts[head, :, here]
            dq = dq + dot(side, sh) + dot(side, sl)
            dq = dq[:HD] + dq[HD:]
            keep[head] = (
                dq,
                dkp + pltpu.roll(dkp, HD, 1),
                dvp + pltpu.roll(dvp, HD, 1),
                dks + pltpu.roll(dks, HD, 1),
                dvs + pltpu.roll(dvs, HD, 1),
            )
        left = lane_ids((QB, 128)) < HD
        far_left = lane_ids(dkp_ref.shape) < HD
        dq_ref[here, :] = jnp.transpose(
            jnp.concatenate([keep[0][0], keep[1][0]], axis=0)
        ) * 0.125
        dkp_ref[...] += jnp.where(far_left, keep[0][1], keep[1][1])
        dvp_ref[...] += jnp.where(far_left, keep[0][2], keep[1][2])
        dks_ref[here, :] = jnp.where(left, keep[0][3], keep[1][3])
        dvs_ref[here, :] = jnp.where(left, keep[0][4], keep[1][4])
        return carry

    lax.fori_loop(0, rows // QB, step, 0)


def attend_backward(lens, q, k_both, v_both, out, grad, lse):
    rows, width = q.shape
    heads = width // HD
    near = pl.BlockSpec((rows, 128), lambda j, lens: (0, j))
    group = pl.BlockSpec((rows, 128), lambda j, lens: (1, j))
    flops = heads * 2 * rows * (rows + QB) * (256 * 5)
    shape = jax.ShapeDtypeStruct((rows, width), F32)
    return pl.pallas_call(
        backward_kernel,
        grid_spec=pltpu.PrefetchScalarGridSpec(
            num_scalar_prefetch=1,
            grid=(heads // 2,),
            in_specs=[
                near, near, near, group, group, near, near,
                pl.BlockSpec((2, 8, rows), lambda j, lens: (j, 0, 0)),
            ],
            out_specs=[near] * 5,
            scratch_shapes=[
                pltpu.VMEM((2, rows, 256), BF),
                pltpu.VMEM((2, rows, 256), BF),
                pltpu.VMEM((2, rows, 256), BF),
                pltpu.VMEM((2, rows, 256), BF),
                pltpu.VMEM((2, rows, 256), BF),
                pltpu.VMEM((2, rows, 256), BF),
                pltpu.VMEM((2, rows, 128), BF),
                pltpu.VMEM((2, rows, 128), BF),
                pltpu.VMEM((2, 128, rows), BF),
                pltpu.VMEM((2, 128, rows), BF),
                pltpu.VMEM((2, 8, rows), F32),
            ],
        ),
        out_shape=[shape] * 5,
        compiler_params=pltpu.CompilerParams(vmem_limit_bytes=56 << 20),
        cost_estimate=pl.CostEstimate(
            flops=flops, bytes_accessed=12 * rows * width * 4, transcendentals=heads * rows * rows
        ),
        name="attention_backward",
    )(lens, q, k_both, v_both, k_both, v_both, out, grad, lse)


TRANSFERS = {
    (0, 2): [("first", 0, 3), ("send", 0, 1)],
    (0, 3): [("down on", 0, 3)],
    (0, 4): [("first", 0, 2), ("send", 0, 0), ("down on", 0, 2)],
    (1, 0): [("second", 0, 3)],
    (1, 1): [("first", 0, 1), ("down on", 0, 1)],
    (1, 2): [("second", 0, 2), ("on", 0, 3)],
    (1, 3): [("first", 0, 0), ("send", 1, 3), ("send", 1, 2), ("send", 1, 1), ("send", 1, 0)],
    (1, 4): [("second", 0, 1), ("on", 0, 2), ("down on", 0, 0)],
    (2, 0): [("qkv", 0, 3), ("qkv", 0, 2)],
    (2, 1): [("second", 0, 0), ("on", 0, 1), ("qkv", 0, 1)],
    (2, 2): [("qkv on", 0, 3), ("qkv", 0, 0), ("down on", 0, -1), ("first", 1, 3)],
    (2, 3): [("on", 0, 0), ("qkv on", 0, 2), ("first", 1, 2), ("first", 1, 1), ("first", 1, 0)],
    (2, 4): [("qkv on", 0, 1)],
}


def backward_all_kernel(
    bits, lens_ref, lse_ref, xt_high, xt_low, w_high, w_low, small_ref,
    q_hbm, k_hbm, v_hbm, o_hbm, g_hbm, first_hbm, up_hbm, out_hbm, down_hbm,
    grad_in, up_mine, up_other, out_mine, out_other, down_mine, down_other, qkv_mine, qkv_other, small_out,
    down_in, down_sum,
    q_in, k_in, v_in, o_in, g_in, q4, g4, k2p, k2s, v2p, v2s, q2, g2, k2tp, k2ts, delta,
    d_q, d_k, d_v, d_kv, d_q2, on_prompt, on_own, prompt_in, far_in,
    up_a, up_b, up_ra, up_rax, up_rb, up_rby, up_s, up_rz,
    out_a, out_b, out_ra, out_rax, out_rb, out_rby, out_s, out_rz,
    qkv_g, qkv_in, qkv_x, sm, sm_in, sm_x, sm_pair,
    load_sem, acc_sem, xy_send, xy_recv, z_send, z_recv, end_send, end_recv,
    q_send, q_recv, qx_send, qx_recv, s_send, s_recv, sx_send, sx_recv, t_send, t_recv, d_load, d_send, d_recv, dz_send, dz_recv,
):
    me = lax.axis_index("dp")
    seq = lax.axis_index("seq")
    group, role = seq // 2, seq % 2
    count = 1 << bits
    layers = count // 2
    level, side = me // 2, me % 2
    has_up, has_down = level < layers - 1, level > 0
    above, below = (me + 2, seq), (me - 2, seq)
    arrival = functools.partial(line_arrival, level, layers)
    width, both_rows = xt_high.shape
    half = w_high.shape[2]
    rows = both_rows // 2
    own = rows // 2
    shard = width // count
    pairs = half // 128
    kinds = (
        (up_hbm, up_a, up_b, up_ra, up_rax, up_rb, up_rby, up_s, up_rz, up_mine, up_other),
        (out_hbm, out_a, out_b, out_ra, out_rax, out_rb, out_rby, out_s, out_rz, out_mine, out_other),
    )

    def stage(pair):
        lanes = pl.ds(pair * 128, 128)
        copies = []
        for index, (src, dst) in enumerate(
            ((q_hbm, q_in), (k_hbm, k_in), (v_hbm, v_in), (o_hbm, o_in), (g_hbm, g_in))
        ):
            copies.append(pltpu.make_async_copy(src.at[:, lanes], dst, load_sem.at[index]))
        return copies

    for copy in stage(0):
        copy.start()
    first_copy = pltpu.make_async_copy(first_hbm, on_own.at[pl.ds(0, own)], load_sem.at[5])
    first_copy.start()
    kept = {}
    for kind in range(2):
        grads, acc_a, acc_b = kinds[kind][:3]
        for layer in reversed(range(layers)):
            slot = arrival(layer) * 2 + side
            for index, copy in enumerate(
                (
                    (grads.at[slot, :, pl.ds(0, 1)], acc_a.at[layer]),
                    (grads.at[slot, group, pl.ds(1, 2)], acc_b.at[layer, 0]),
                    (grads.at[slot + 1 - 2 * side, group, pl.ds(1, 2)], acc_b.at[layer, 1]),
                )
            ):
                kept[kind, layer, index] = pltpu.make_async_copy(
                    *copy, acc_sem.at[kind, layer, index]
                )
                kept[kind, layer, index].start()
    greet_line(has_up, has_down, above, below)
    started = []
    ended = []

    def go(make, *which):
        make(*which).start()
        started.append((make, which))

    def xy(kind, layer, step):
        grads, acc_a, acc_b, ra, rax, rb, rby = kinds[kind][:7]
        slot = arrival(layer) * 2 + side
        src, dst, target = (
            (grads.at[slot + 1 - 2 * side, :, pl.ds(0, 1)], ra.at[layer], partner(1, 0)),
            (grads.at[slot, group ^ 1, pl.ds(1, 2)], rb.at[layer, 0], partner(0, 2)),
            (grads.at[slot + 1 - 2 * side, group ^ 1, pl.ds(1, 2)], rb.at[layer, 1], partner(0, 2)),
            (acc_a.at[layer, group ^ 1], rax.at[layer], partner(0, 2)),
            (acc_b.at[layer, 1], rby.at[layer], partner(1, 0)),
        )[step]
        return remote(
            src, dst, xy_send.at[kind, layer, step], xy_recv.at[kind, layer, step], target
        )

    def send(kind, layer):
        for step in range(3):
            go(xy, kind, layer, step)

    def first(kind, layer):
        _, acc_a, acc_b, ra, _, rb = kinds[kind][:6]
        for index in range(3):
            kept[kind, layer, index].wait()
        for step in range(3):
            xy(kind, layer, step).wait_recv()
        acc_a[layer] += ra[layer]
        acc_b[layer] += rb[layer]
        go(xy, kind, layer, 3)
        go(xy, kind, layer, 4)

    def incoming(at):
        return ((at > level) & has_down) | ((at < level) & has_up)

    def line_in(layer, add):
        at = arrival(layer)
        if layer == 0:
            @pl.when(has_down)
            def _():
                add(at)

            @pl.when(has_up)
            def _():
                add(layers)
        else:
            @pl.when(incoming(at))
            def _():
                add(at)

    def line_out(layer, make, late):
        if layer:
            at = arrival(layer)
            now = incoming(at) if late else jnp.logical_not(incoming(at))

            @pl.when((at > level) & now)
            def _():
                make(at, above).start()

            @pl.when((at < level) & now)
            def _():
                make(jnp.where(at == level - 1, layers, at), below).start()

            if late:
                def act():
                    at = arrival(layer)

                    @pl.when(at > level)
                    def _():
                        make(at, above).wait_send()

                    @pl.when(at < level)
                    def _():
                        make(jnp.where(at == level - 1, layers, at), below).wait_send()

                ended.append(act)

    def climb(kind, layer, place, target):
        return remote(
            kinds[kind][7].at[layer], kinds[kind][8].at[place], z_send.at[kind, layer],
            z_recv.at[kind, place], target,
        )

    def second(kind, layer):
        _, acc_a, acc_b, _, rax, _, rby, total, landing = kinds[kind][:9]
        xy(kind, layer, 3).wait_recv()
        xy(kind, layer, 4).wait_recv()
        total[layer, pl.ds(0, 1)] = acc_a[layer, group] + rax[layer]
        total[layer, pl.ds(1, 2)] = acc_b[layer, 0] + rby[layer]

        line_out(layer, functools.partial(climb, kind, layer), False)

    def onward(kind, layer):
        total, landing = kinds[kind][7:9]

        def add(place):
            climb(kind, layer, place, above).wait_recv()
            total[layer] += landing[place]

        line_in(layer, add)
        line_out(layer, functools.partial(climb, kind, layer), True)

    def cross(kind):
        total, mine = kinds[kind][7], kinds[kind][9]
        return remote(
            total.at[0], mine.at[group], end_send.at[kind, 0], end_recv.at[kind, 0], partner(0, 2)
        )

    def cross_in(kind):
        total, mine = kinds[kind][7], kinds[kind][9]
        return remote(
            total.at[0], mine.at[group ^ 1], end_send.at[kind, 0], end_recv.at[kind, 0], partner(0, 2)
        )

    def hand(kind):
        mine, other = kinds[kind][9:]
        return remote(mine, other, end_send.at[kind, 1], end_recv.at[kind, 1], partner(0, 1))

    def tracks(pair):
        found = [
            (lambda slot: qkv_g.at[pair, :, slot], qkv_in.at[pair], q_send.at[pair], q_recv.at[pair])
        ]
        if pair == pairs - 1:
            found.append((lambda slot: sm.at[slot], sm_in, s_send, s_recv))
        return found

    def to_side(pair, which, layer):
        block, landing, send_sem, recv_sem = tracks(pair)[which]
        slot = arrival(layer) * 2 + 1 - side
        return remote(
            block(slot), landing.at[layer], send_sem.at[layer], recv_sem.at[layer], partner(1, 0)
        )

    def qkv_climb(pair, which, layer, place, target):
        block, landing, send_sem, recv_sem = tracks(pair)[which]
        return remote(
            block(arrival(layer) * 2 + side), landing.at[layers + place],
            send_sem.at[layers + layer], recv_sem.at[layers + place], target,
        )

    def qkv_begin(pair):
        for layer in reversed(range(layers)):
            for which in range(len(tracks(pair))):
                go(to_side, pair, which, layer)

    def qkv(pair, layer):
        for which, track in enumerate(tracks(pair)):
            here = track[0](arrival(layer) * 2 + side)
            to_side(pair, which, layer).wait_recv()
            here[...] += track[1][layer]
            line_out(layer, functools.partial(qkv_climb, pair, which, layer), False)

    def qkv_on(pair, layer):
        for which, track in enumerate(tracks(pair)):
            here = track[0](arrival(layer) * 2 + side)

            def add(place):
                qkv_climb(pair, which, layer, place, above).wait_recv()
                here[...] += track[1][layers + place]

            line_in(layer, add)
            line_out(layer, functools.partial(qkv_climb, pair, which, layer), True)

    def qkv_cross(pair):
        return remote(
            qkv_g.at[pair, :, me], qkv_x.at[pair], qx_send.at[pair, 0], qx_recv.at[pair, 0], partner(0, 2)
        )

    def qkv_hand(pair):
        return remote(
            qkv_mine.at[pair], qkv_other.at[pair], qx_send.at[pair, 1], qx_recv.at[pair, 1],
            partner(0, 1),
        )

    def qkv_finish(pair):
        qkv_cross(pair).wait_recv()
        qkv_mine[pair] = qkv_g[pair, :, me] + qkv_x[pair]
        go(qkv_hand, pair)

    down_loads = [
        pltpu.make_async_copy(down_hbm.at[arrival(layer)], down_sum.at[layer], d_load.at[layer])
        for layer in range(layers)
    ]

    def down_climb(layer, place, target):
        return remote(
            down_sum.at[layer], down_in.at[place], dz_send.at[layer], dz_recv.at[place], target
        )

    def down_cross(landing):
        region = down_mine.at[group ^ landing]
        return remote(region, region, d_send.at[0], d_recv.at[0], partner(0, 2))

    def down_hand():
        return remote(down_mine, down_other, d_send.at[1], d_recv.at[1], partner(0, 1))

    def down_begin(layer):
        down_loads[layer].wait()
        line_out(layer, functools.partial(down_climb, layer), False)

    def down_on(_, layer):
        if layer < 0:
            down_cross(1).wait_recv()
            go(down_hand)
            return

        def add(place):
            down_climb(layer, place, above).wait_recv()
            down_sum[layer] += down_in[place]

        line_in(layer, add)
        line_out(layer, functools.partial(down_climb, layer), True)
        if layer == 0:
            down_mine[group] = down_sum[0]
            go(down_cross, 0)

    actions = {
        "send": send,
        "first": first,
        "second": second,
        "on": onward,
        "qkv": qkv,
        "qkv on": qkv_on,
        "down on": down_on,
    }

    def run(events):
        for name, kind, index in events:
            actions[name](kind, index)

    def prepare(pair):
        prod = jnp.transpose(o_in[...] * g_in[...])
        for head in range(2):
            hl, hh, ll = packs(q_in[...] * 0.125, head)
            q2[head] = hl
            q4[head, :, :128] = hh
            q4[head, :, 128:] = ll
            hl, hh, ll = packs(g_in[...], head)
            g2[head] = hl
            g4[head, :, :128] = hh
            g4[head, :, 128:] = ll
            for src, start, dst in (
                (k_in, 0, k2p), (k_in, rows, k2s), (v_in, 0, v2p), (v_in, rows, v2s),
            ):
                dst[head] = packs(src[pl.ds(start, rows), :], head)[0]
            for start, dst in ((0, k2tp), (rows, k2ts)):
                flipped = jnp.transpose(k_in[pl.ds(start, rows), :])[head * HD : head * HD + HD]
                high, low = high_low(flipped)
                dst[head, :HD] = high.astype(BF)
                dst[head, HD:] = low.astype(BF)
            delta[head] = jnp.broadcast_to(
                jnp.sum(prod[head * HD : head * HD + HD], axis=0, keepdims=True), (8, rows)
            )

    def twice(value):
        return jnp.concatenate([value, value], axis=1)

    def attend(pair):
        d_k[pl.ds(0, rows), :] = jnp.zeros((rows, 128), F32)
        d_v[pl.ds(0, rows), :] = jnp.zeros((rows, 128), F32)

        def body(step, carry):
            for position in range(4):
                events = TRANSFERS.get((pair, position))
                if events:
                    @pl.when(step == position)
                    def _():
                        run(events)

            here = pl.ds(pl.multiple_of(step * QB, QB), QB)
            there = pl.ds(pl.multiple_of(step * QB + rows, QB), QB)
            seen = self_mask(lens_ref, step, 1)
            keep = {}
            for head in range(2):
                query = q4[head, here, :]
                grad = g4[head, here, :]
                lse = lse_ref[2 * pair + head, :1, here]
                low = delta[head, :1, here]
                far = jnp.exp(dot_nt(twice(k2p[head]), query) - lse)
                near = jnp.exp(
                    jnp.where(seen, dot_nt(twice(k2s[head, here, :]), query), MASKED) - lse
                )
                far_g = far * (dot_nt(twice(v2p[head]), grad) - low)
                near_g = near * (dot_nt(twice(v2s[head, here, :]), grad) - low)
                grad2 = g2[head, here, :]
                query2 = q2[head, here, :]
                ph, p_l = split(far)
                dvp = dot(ph, grad2) + dot(p_l, grad2)
                ph, p_l = split(near)
                dvs = dot(ph, grad2) + dot(p_l, grad2)
                sh, sl = split(far_g)
                dkp = dot(sh, query2) + dot(sl, query2)
                dq = dot(k2tp[head], sh) + dot(k2tp[head], sl)
                sh, sl = split(near_g)
                dks = dot(sh, query2) + dot(sl, query2)
                side = k2ts[head, :, here]
                dq = dq + dot(side, sh) + dot(side, sl)
                keep[head] = (
                    dq[:HD] + dq[HD:],
                    dkp + pltpu.roll(dkp, HD, 1),
                    dvp + pltpu.roll(dvp, HD, 1),
                    dks + pltpu.roll(dks, HD, 1),
                    dvs + pltpu.roll(dvs, HD, 1),
                )
            left = lane_ids((QB, 128)) < HD
            far_left = lane_ids((rows, 128)) < HD
            d_q[here, :] = jnp.transpose(
                jnp.concatenate([keep[0][0], keep[1][0]], axis=0)
            ) * 0.125
            d_k[pl.ds(0, rows), :] += jnp.where(far_left, keep[0][1], keep[1][1])
            d_v[pl.ds(0, rows), :] += jnp.where(far_left, keep[0][2], keep[1][2])
            d_k[there, :] = jnp.where(left, keep[0][3], keep[1][3])
            d_v[there, :] = jnp.where(left, keep[0][4], keep[1][4])
            return carry

        lax.fori_loop(0, 4, body, 0)

    def divide():
        def body(index, carry):
            here = pl.ds(pl.multiple_of(index * QB, QB), QB)
            high, low = split(d_k[here, :])
            d_kv[here, 0:128] = high
            d_kv[here, 256:384] = low
            high, low = split(d_v[here, :])
            d_kv[here, 128:256] = high
            d_kv[here, 384:512] = low

            @pl.when(index < 4)
            def _():
                high, low = split(d_q[here, :])
                d_q2[here, 0:128] = high
                d_q2[here, 128:256] = low

            return carry

        lax.fori_loop(0, 8, body, 0)

    def to_prompt(pair):
        lanes = pl.ds(pair * 128, 128)
        high_w = jnp.concatenate([w_high[1, :, lanes], w_high[2, :, lanes]], axis=1)
        low_w = jnp.concatenate([w_low[1, :, lanes], w_low[2, :, lanes]], axis=1)

        def body(index, carry):
            here = pl.ds(pl.multiple_of(index * QB, QB), QB)
            high, low = d_kv[here, 0:256], d_kv[here, 256:512]
            result = dot_nt(high, high_w) + dot_nt(high, low_w) + dot_nt(low, high_w)
            on_prompt[here, :] = result if pair == 0 else on_prompt[here, :] + result
            return carry

        lax.fori_loop(0, 4, body, 0)

    def to_own(pair):
        lanes = pl.ds(pair * 128, 128)
        order = (1, 2, 0)
        high_w = jnp.concatenate([w_high[i, :, lanes] for i in order], axis=1)
        low_w = jnp.concatenate([w_low[i, :, lanes] for i in order], axis=1)

        def body(index, carry):
            here = pl.ds(pl.multiple_of(index * QB, QB), QB)
            there = pl.ds(pl.multiple_of(index * QB + rows, QB), QB)
            high = jnp.concatenate([d_kv[there, 0:256], d_q2[here, 0:128]], axis=1)
            low = jnp.concatenate([d_kv[there, 256:512], d_q2[here, 128:256]], axis=1)
            result = dot_nt(high, high_w) + dot_nt(high, low_w) + dot_nt(low, high_w)
            on_own[here, :] += result
            return carry

        lax.fori_loop(0, 4, body, 0)

    def weight_grads(pair):
        each = count // 2
        size = each * shard

        def body(index, carry):
            here = pl.ds(pl.multiple_of(index * size, size), size)
            high, low = xt_high[here, :], xt_low[here, :]
            first_kv = dot(high, d_kv[...])
            kv = first_kv[:, :256] + first_kv[:, 256:] + dot(low, d_kv[:, 0:256])
            high, low = high[:, rows:], low[:, rows:]
            first_q = dot(high, d_q2[...])
            query = first_q[:, :128] + first_q[:, 128:] + dot(low, d_q2[:, 0:128])
            for slot in range(each):
                part = slice(slot * shard, slot * shard + shard)
                qkv_g[pair, 0, index * each + slot] = query[part]
                qkv_g[pair, 1, index * each + slot] = kv[part, :128]
                qkv_g[pair, 2, index * each + slot] = kv[part, 128:]
            return carry

        lax.fori_loop(0, 2, body, 0)

    sums_q, sums_v = [], []
    for copy in reversed(down_loads):
        copy.start()
    send(0, 3)
    send(0, 2)
    for layer in reversed(range(layers)):
        down_begin(layer)
    on_own[pl.ds(own, own), :] = jnp.zeros((own, width), F32)
    for pair in range(pairs):
        for copy in stage(pair):
            copy.wait()
        prepare(pair)
        if pair + 1 < pairs:
            for copy in stage(pair + 1):
                copy.start()
        attend(pair)
        run(TRANSFERS.get((pair, 4), []))
        divide()
        sums_q.append(jnp.sum(d_q[...], axis=0, keepdims=True))
        sums_v.append(jnp.sum(d_v[...], axis=0, keepdims=True))
        if pair == 0:
            first_copy.wait()
        if pair + 1 < pairs:
            weight_grads(pair)
            qkv_begin(pair)
            to_prompt(pair)
            to_own(pair)

    def swap(src, dst, index):
        return remote(src, dst, t_send.at[index], t_recv.at[index], partner(0, 1))

    last = pairs - 1
    to_prompt(last)
    prompt_swap = swap(on_prompt.at[pl.ds(own, own)], prompt_in, 0)
    go(lambda: prompt_swap)
    qkv_on(0, 0)
    go(qkv_cross, 0)
    go(cross, 0)
    weight_grads(last)
    bias_q = jnp.concatenate(sums_q, axis=1)
    bias_v = jnp.concatenate(sums_v, axis=1)
    bias = jnp.concatenate([bias_q, bias_v, jnp.zeros((6, half), F32)], axis=0)
    nothing = jnp.zeros((8, half), F32)
    bias = jnp.where(
        role == 0,
        jnp.concatenate([bias, nothing], axis=1),
        jnp.concatenate([nothing, bias], axis=1),
    )
    inside = lane_ids((8, 128)) < shard
    for slot in range(count):
        turned = pltpu.roll(bias, (width - shard * slot) % width, 1) if slot else bias
        sm[slot] = small_ref[slot]
        sm[slot, pl.ds(0, 8), :] += jnp.where(inside, turned[:, :128], 0.0)

    qkv_begin(last)
    prompt_swap.wait_recv()
    on_prompt[pl.ds(0, own), :] += prompt_in[...]
    far = remote(on_prompt.at[pl.ds(0, own)], far_in, t_send.at[1], t_recv.at[1], partner(0, 2))

    @pl.when(group == 1)
    def _():
        far.start()

    for layer in reversed(range(layers)):
        qkv(1, layer)
    to_own(last)
    own_swap = swap(on_own.at[pl.ds(own, own)], grad_in, 2)
    go(lambda: own_swap)

    for layer in reversed(range(layers)):
        second(1, layer)
    qkv_on(1, 3)
    qkv(last, 3)
    onward(1, 3)
    qkv_on(1, 2)
    qkv(last, 2)
    onward(1, 2)
    qkv_on(1, 1)
    qkv(last, 1)
    onward(1, 1)
    qkv(last, 0)
    qkv_on(last, 3)
    qkv_on(1, 0)
    go(qkv_cross, 1)
    onward(1, 0)
    go(cross, 1)
    qkv_on(last, 2)
    qkv_finish(0)
    for kind in range(2):
        kinds[kind][9][group] = kinds[kind][7][0]
        cross_in(kind).wait_recv()
        go(hand, kind)
    qkv_finish(1)
    qkv_on(last, 1)
    qkv_on(last, 0)
    go(qkv_cross, last)
    small_x = remote(sm.at[me], sm_x, sx_send.at[0], sx_recv.at[0], partner(0, 2))
    go(lambda: small_x)
    own_swap.wait_recv()
    grad_in[...] += on_own[pl.ds(0, own), :]
    qkv_finish(last)
    small_x.wait_recv()
    small_out[...] = sm[me] + sm_x[...]
    small_pair = remote(small_out, sm_pair, sx_send.at[1], sx_recv.at[1], partner(0, 1))
    go(lambda: small_pair)

    @pl.when(group == 0)
    def _():
        far.wait_recv()
        grad_in[...] += on_prompt[pl.ds(0, own), :] + far_in[...]

    small_pair.wait_recv()
    for kind in range(2):
        hand(kind).wait_recv()
    down_hand().wait_recv()
    for pair in range(pairs):
        qkv_hand(pair).wait_recv()
    for make, which in started:
        make(*which).wait_send()
    for act in ended:
        act()
    small_out[...] += sm_pair[...]

    @pl.when(group == 1)
    def _():
        far.wait_send()


def run_backward(lens, lse, xt_high, xt_low, w_high, w_low, small, q, k, v, o, g, first_grad,
                 up_grads, out_grads, down_grads):
    bits = dp_bits()
    count = 1 << bits
    layers = count // 2
    anywhere = pl.BlockSpec(memory_space=pl.ANY)
    vmem = pl.BlockSpec(memory_space=pltpu.VMEM)
    width, both_rows = xt_high.shape
    rows, half = q.shape
    own = rows // 2
    pairs = half // 128
    shard = width // count
    shape = lambda *dims: jax.ShapeDtypeStruct(dims, F32)
    space = lambda *dims: pltpu.VMEM(dims, F32)
    short = lambda *dims: pltpu.VMEM(dims, BF)
    dma = lambda *dims: pltpu.SemaphoreType.DMA(dims)

    def buffers(unit):
        return [
            space(layers, 2, 1, *unit),
            space(layers, 2, 2, *unit),
            space(layers, 2, 1, *unit),
            space(layers, 1, *unit),
            space(layers, 2, 2, *unit),
            space(layers, 2, *unit),
            space(layers, 3, *unit),
            space(layers + 1, 3, *unit),
        ]

    up_unit, out_unit = up_grads.shape[3:], out_grads.shape[3:]
    tiny = small.shape[1:]
    return pl.pallas_call(
        functools.partial(backward_all_kernel, bits),
        in_specs=[pl.BlockSpec(memory_space=pltpu.SMEM)] + [vmem] * 6 + [anywhere] * 9,
        out_specs=[vmem] + [vmem, anywhere] * 4 + [vmem],
        out_shape=[
            shape(own, width),
            shape(2, 3, *up_unit),
            shape(2, 3, *up_unit),
            shape(2, 3, *out_unit),
            shape(2, 3, *out_unit),
            shape(2, *down_grads.shape[1:]),
            shape(2, *down_grads.shape[1:]),
            shape(pairs, 3, shard, 128),
            shape(pairs, 3, shard, 128),
            shape(*tiny),
        ],
        scratch_shapes=[
            space(layers + 1, *down_grads.shape[1:]),
            space(*down_grads.shape),
            space(rows, 128),
            space(both_rows, 128),
            space(both_rows, 128),
            space(rows, 128),
            space(rows, 128),
            short(2, rows, 256),
            short(2, rows, 256),
            short(2, rows, 128),
            short(2, rows, 128),
            short(2, rows, 128),
            short(2, rows, 128),
            short(2, rows, 128),
            short(2, rows, 128),
            short(2, 128, rows),
            short(2, 128, rows),
            space(2, 8, rows),
            space(rows, 128),
            space(both_rows, 128),
            space(both_rows, 128),
            short(both_rows, 512),
            short(rows, 256),
            space(rows, width),
            space(rows, width),
            space(own, width),
            space(own, width),
        ]
        + buffers(up_unit)
        + buffers(out_unit)
        + [
            space(pairs, 3, count, shard, 128),
            space(pairs, count + 1, 3, shard, 128),
            space(pairs, 3, shard, 128),
            space(count, *tiny),
            space(count + 1, *tiny),
            space(*tiny),
            space(*tiny),
            dma(6),
            dma(2, layers, 3),
            dma(2, layers, 5),
            dma(2, layers, 5),
            dma(2, layers),
            dma(2, layers + 1),
            dma(2, 2),
            dma(2, 2),
            dma(pairs, count),
            dma(pairs, count + 1),
            dma(pairs, 2),
            dma(pairs, 2),
            dma(count),
            dma(count + 1),
            dma(2),
            dma(2),
            dma(3),
            dma(3),
            dma(layers),
            dma(2),
            dma(2),
            dma(layers),
            dma(layers + 1),
        ],
        compiler_params=pltpu.CompilerParams(
            collective_id=3, has_side_effects=True, vmem_limit_bytes=67043328
        ),
        name="attention_backward_and_scatter",
    )(lens, lse, xt_high, xt_low, w_high, w_low, small, q, k, v, o, g, first_grad, up_grads, out_grads,
      down_grads)


def norm_forward(resid, gain, shift):
    center = resid - jnp.mean(resid, axis=-1, keepdims=True)
    inverse = lax.rsqrt(jnp.mean(center * center, axis=-1, keepdims=True) + EPSILON)
    normed = center * inverse
    return normed * gain + shift, normed, inverse


def norm_backward(grad_out, normed, inverse, gain):
    grad_normed = grad_out * gain
    first_term = jnp.mean(grad_normed, axis=-1, keepdims=True)
    second_term = jnp.mean(grad_normed * normed, axis=-1, keepdims=True)
    grad_resid = inverse * (grad_normed - first_term - normed * second_term)
    return grad_resid, jnp.sum(grad_out * normed, axis=0), jnp.sum(grad_out, axis=0)


def on_device(
    hidden_in,
    teacher,
    lengths,
    qkv_weight,
    qkv_bias,
    out_weight,
    out_bias,
    ln_gain,
    ln_shift,
    ffn_in,
    ffn_in_bias,
    ffn_out,
):
    _, rows, width = hidden_in.shape
    dp_count = lax.axis_size("dp")
    dp_index = lax.axis_index("dp")
    seq_index = lax.axis_index("seq")
    group, role = seq_index // 2, seq_index % 2
    total_tokens = dp_count * rows * SEQ
    shard = qkv_weight.shape[1]
    half = width // 2
    ffn = ffn_in.shape[1]
    ffn_shard = ffn // dp_count
    ffn_half = ffn_shard // 2

    x_own = hidden_in.reshape(rows, width)
    target = teacher.reshape(rows, width)
    lens = lengths.reshape(CONT)

    length_sum = jnp.sum(lens).astype(F32)
    lanes = lambda value: jnp.pad(value, ((0, 0), (0, 128 - value.shape[1])))
    up_rows = -(-ffn_shard // 128)
    up_bias = jnp.pad(ffn_in_bias, (0, up_rows * 128 - ffn_shard)).reshape(up_rows, 128)
    small_rows = -(-(9 + up_rows) // 8) * 8
    small = jnp.concatenate(
        [
            lanes(qkv_bias),
            lanes(out_bias),
            lanes(ln_gain),
            lanes(ln_shift),
            up_bias,
            jnp.full((small_rows - 8 - up_rows, 128), length_sum, F32),
        ]
    )
    local_lens = jnp.where(role == 0, lens, jnp.roll(lens, CONT // 2))
    local_lens = jnp.where(group == 0, 0, local_lens)
    out_half = shard // 2
    up_piece = pick(ffn_in.reshape(shard, dp_count, 2, ffn_half), role, 2)
    out_piece = pick(out_weight.reshape(2, out_half, width), role, 0)
    down_piece = pick(ffn_out.reshape(2, ffn_half, width), role, 0)
    (w_high, w_low, small, xt_high, xt_low, k_both, v_both, queries, attended, lse,
     out_blocks, w_up, w_down, out_other) = run_forward(
        local_lens,
        lax.dynamic_slice_in_dim(qkv_weight, role * half, half, 2),
        small,
        x_own,
        out_piece.reshape(2, 3, out_half // 6, width),
        up_piece.reshape(2, 3, shard // 6, ffn // 2),
        down_piece.reshape(2, 3, ffn_half // 6, width),
    )
    w_up = w_up.reshape(width, ffn // 2)
    w_down = w_down.reshape(ffn // 2, width)
    out_mine = pick(out_blocks.reshape(2, dp_count // 2, out_half, width), role, 0)
    out_other = out_other.reshape(dp_count // 2, out_half, width)
    w_out = ordered(role, out_mine[:, None], out_other[:, None], 1).reshape(half, width)
    vectors = small[:, :8, :shard].transpose(1, 0, 2).reshape(4, 2, width)
    b_out, gains, shifts = vectors[1], vectors[2], vectors[3]
    b_up = small[:, 8 : 8 + up_rows].reshape(dp_count, up_rows * 128)[:, :ffn_shard]
    b_up = pick(b_up.reshape(dp_count, 2, ffn_half), role, 1).reshape(ffn // 2)
    count = float(dp_count * PROMPT) + jnp.sum(small[:, small_rows - 1, 0])

    def reduce_pair(partial):
        return partial[:rows] + swap_pair(partial[rows:])

    def both_halves(own):
        return jnp.concatenate([own, swap_pair(own)], axis=0)

    first_resid = x_own + reduce_pair(mm(attended, w_out)) + b_out[0]
    first_norm, first_hat, first_inv = norm_forward(first_resid, gains[0], shifts[0])
    norm_group = both_halves(first_norm)
    pre_act = mm(norm_group, w_up) + b_up
    normal_cdf = 0.5 * (1.0 + lax.erf(pre_act * INV_ROOT_TWO))
    activated = pre_act * normal_cdf
    slope = normal_cdf + pre_act * jnp.exp(-0.5 * pre_act * pre_act) * INV_ROOT_TAU
    second_resid = first_norm + reduce_pair(mm(activated, w_down)) + b_out[1]
    final, second_hat, second_inv = norm_forward(second_resid, gains[1], shifts[1])

    slot = seq_index * rows + jnp.arange(rows, dtype=jnp.int32) - PROMPT
    own_len = jnp.sum(
        jnp.where((slot // CLEN)[None] == jnp.arange(CONT, dtype=jnp.int32)[:, None], lens[:, None], 0),
        axis=0,
    )
    valid = ((slot < 0) | (slot % CLEN < own_len)).astype(F32)
    difference = (final - target) * valid[:, None]
    squares = jnp.sum(difference * difference)
    grad_final = difference * (total_tokens / count)
    grad_second, grad_gain_two, grad_shift_two = norm_backward(
        grad_final, second_hat, second_inv, gains[1]
    )
    grad_bias_down = jnp.sum(grad_second, axis=0)
    second_group = both_halves(grad_second)
    grad_w_down = mm_tn(activated, second_group)
    ybit = dp_index & 1
    early = dp_count <= 8
    if early:
        down = grad_w_down.reshape(dp_count // 2, 2, 2, 2, ffn_half // 4, width)
        down_a, down_b = down[:, :, :, 0], down[:, :, :, 1]
        send_a, send_b = pick(down_a, ybit ^ 1, 1), pick(down_b, group ^ 1, 2)
        keep_a, keep_b = pick(down_a, ybit, 1), pick(down_b, group, 2)
        second_group, send_a, send_b = lax.optimization_barrier((second_group, send_a, send_b))
        come_a, come_b = swap_dp(send_a, 0), swap_group(send_b)
    grad_pre = mm_nt(second_group, w_down) * slope
    grad_b_up = jnp.sum(grad_pre, axis=0)
    grad_w_up = mm_tn(norm_group, grad_pre)
    if early:
        grad_w_up, come_a, come_b = lax.optimization_barrier((grad_w_up, come_a, come_b))
        down_a, down_b = keep_a + come_a, keep_b + come_b
        send_a, send_b = pick(down_a, group ^ 1, 1), pick(down_b, ybit ^ 1, 1)
        keep_a, keep_b = pick(down_a, group, 1), pick(down_b, ybit, 1)
        grad_pre, send_a, send_b = lax.optimization_barrier((grad_pre, send_a, send_b))
        come_a, come_b = swap_group(send_a), swap_dp(send_b, 0)
    if not early:
        share_down = scatter_rows(grad_w_down)
    grad_first_norm = grad_second + reduce_pair(mm_nt(grad_pre, w_up))
    grad_first, grad_gain_one, grad_shift_one = norm_backward(
        grad_first_norm, first_hat, first_inv, gains[0]
    )
    grad_bias_out = jnp.sum(grad_first, axis=0)
    first_group = both_halves(grad_first)
    grad_attended = mm_nt(first_group, w_out)
    if early:
        grad_attended, come_a, come_b = lax.optimization_barrier((grad_attended, come_a, come_b))
        half_down = jnp.stack([keep_a + come_a, keep_b + come_b], axis=1)
    grad_w_out = mm_tn(attended, first_group)
    mine = grad_w_out.reshape(dp_count // 2, 2, out_half, width)
    received = swap_pair(pick(mine, 1 - role, 1))
    mine = ordered(role, pick(mine, role, 1), received, 0)
    up = jnp.zeros((dp_count, 2, ffn_half), F32)
    up = lax.dynamic_update_slice(up, grad_b_up.reshape(dp_count, 1, ffn_half), (0, role, 0))
    up = jnp.pad(up.reshape(dp_count, ffn_shard), ((0, 0), (0, up_rows * 128 - ffn_shard)))

    def small_block(bias_q, bias_v):
        vectors = jnp.stack(
            [
                bias_q,
                bias_v,
                grad_bias_out,
                grad_bias_down,
                grad_gain_one,
                grad_gain_two,
                grad_shift_one,
                grad_shift_two,
            ]
        )
        vectors = vectors.reshape(8, dp_count, shard).transpose(1, 0, 2)
        return jnp.concatenate(
            [
                jnp.pad(vectors, ((0, 0), (0, 0), (0, 128 - shard))),
                up.reshape(dp_count, up_rows, 128),
                jnp.full((dp_count, small_rows - 8 - up_rows, 128), squares, F32),
            ],
            axis=1,
        )

    def join(share, axis):
        return ordered(role, share, swap_pair(share), axis)

    if early:
        (grad_input, up_mine, up_other, out_mine, out_other, down_mine, down_other,
         qkv_mine, qkv_other, small) = run_backward(
            local_lens, lse, xt_high, xt_low, w_high, w_low,
            small_block(jnp.zeros((width,), F32), jnp.zeros((width,), F32)),
            queries, k_both, v_both, attended, grad_attended, grad_first,
            grad_w_up.reshape(dp_count, 2, 3, shard // 6, ffn // 2),
            mine.reshape(dp_count, 2, 3, out_half // 6, width),
            half_down,
        )
        lay = lambda value: value.transpose(1, 2, 0, 3).reshape(3, shard, half)
        out_qkv = ordered(role, lay(qkv_mine), lay(qkv_other), 2)
        out_out = ordered(
            role, out_mine.reshape(out_half, width), out_other.reshape(out_half, width), 0
        )
        lay = lambda value: value.reshape(shard, dp_count, 1, ffn_half)
        out_up = ordered(role, lay(up_mine), lay(up_other), 2).reshape(shard, ffn)
        out_down = ordered(
            role, down_mine.reshape(ffn_half, width), down_other.reshape(ffn_half, width), 0
        )
    else:
        share_up = scatter_rows(grad_w_up)
        d_q, d_kp, d_vp, d_ks, d_vs = attend_backward(
            local_lens, queries, k_both, v_both, attended, grad_attended, lse
        )
        weights = w_high.astype(F32) + w_low.astype(F32)
        w_q, w_k, w_v = weights[0], weights[1], weights[2]
        x_t = xt_high.astype(F32) + xt_low.astype(F32)
        on_prompt = reduce_pair(mm_nt(d_kp, w_k) + mm_nt(d_vp, w_v))
        from_cont = lax.ppermute(on_prompt, "seq", [(2, 0), (3, 1)])
        grad_w_k = mm(x_t, jnp.concatenate([d_kp, d_ks], axis=0))
        grad_w_v = mm(x_t, jnp.concatenate([d_vp, d_vs], axis=0))
        grad_w_q = mm(x_t[:, 2 * rows :], d_q)
        on_own = reduce_pair(mm_nt(d_q, w_q) + mm_nt(d_ks, w_k) + mm_nt(d_vs, w_v))
        grad_input = grad_first + on_own + jnp.where(group == 0, on_prompt + from_cont, 0.0)

        def widen(value):
            return lax.dynamic_update_slice(jnp.zeros((width,), F32), value, (role * half,))

        share_qkv, share_out, small, other_qkv, other_out = scatter_all(
            jnp.stack([grad_w_q, grad_w_k, grad_w_v]).reshape(3, dp_count, shard, half),
            mine.reshape(dp_count, out_half, width),
            small_block(
                widen(jnp.sum(d_q, axis=0)),
                widen(jnp.sum(d_vp, axis=0) + jnp.sum(d_vs, axis=0)),
            ),
        )
        out_qkv = ordered(role, share_qkv, other_qkv, 2)
        out_out = ordered(role, share_out, other_out, 0)
        out_up = join(share_up.reshape(shard, dp_count, 1, ffn_half), 2).reshape(shard, ffn)
        out_down = join(share_down.reshape(ffn_half, width), 0)
    pairs = small[:8, :shard].reshape(4, 2, shard)
    out_b_up = small[8 : 8 + up_rows].reshape(up_rows * 128)[:ffn_shard]
    loss = small[small_rows - 1, 0] / (count * width)
    return (
        final[None],
        grad_input[None],
        out_qkv,
        pairs[0],
        out_out,
        pairs[1],
        pairs[2],
        pairs[3],
        out_up,
        out_b_up,
        out_down,
        loss,
    )


def solution(mesh):
    return jax.shard_map(
        on_device,
        mesh=mesh,
        in_specs=(
            P("dp", "seq", None),
            P("dp", "seq", None),
            P("dp", None),
            P(None, "dp", None),
            P(None, "dp"),
            P("dp", None),
            P(None, "dp"),
            P(None, "dp"),
            P(None, "dp"),
            P("dp", None),
            P("dp"),
            P("dp", None),
        ),
        out_specs=(
            P("dp", "seq", None),
            P("dp", "seq", None),
            P(None, "dp", None),
            P(None, "dp"),
            P("dp", None),
            P(None, "dp"),
            P(None, "dp"),
            P(None, "dp"),
            P("dp", None),
            P("dp"),
            P("dp", None),
            P(),
        ),
        check_vma=False,
    )
```
